512 devices in a mesh: wide: 32 (over y, z_hi, core), grp: 16 (over x, z_lo).
Axes of the slice: x: 4, y: 8, z: 8 (z_hi: 2, z_lo: 4; z = z_hi * 4 + z_lo), core: 2. Of those that a mesh axis runs over, the one named last changes fastest.
Arguments:
- obs_value: float32 [65536], P(('wide', 'grp')), may hold values from -6 to 6
- obs_tile: int32 [65536], P(('wide', 'grp')), may hold values from 0 to 31
- obs_cell: int32 [65536], P(('wide', 'grp')), may hold values from 0 to 32767
- obs_type: int32 [65536], P(('wide', 'grp')), may hold values from 0 to 2
- obs_weights: float32 [2, 8], replicated, may hold values from 0.2 to 1.5
- diffusivity: float32 [128, 8192], P('wide', 'grp'), may hold values from 0.03 to 0.24
- erodibility: float32 [128, 8192], P('wide', 'grp'), may hold values from 0.1 to 1
- class_mixing: float32 [8, 8], replicated, may hold values from -2.5 to 2.5
- fall_table: float32 [16], replicated, may hold values from 0.05 to 0.6
- fall_index: int32 [8], replicated, may hold values from 0 to 15
- bedload_rate: float32 [8], replicated, may hold values from 20 to 3000
Outputs:
- adjoint_tracer: float32 [8, 16, 128, 8192], P(None, None, 'wide', 'grp')
- adjoint_bed: float32 [8, 128, 8192], P(None, 'wide', 'grp')
The draws below stay inside these ranges and needn't reach their ends.
All inputs are finite; a program needn't handle non-finite values.
Results may differ from the reference program's by a relative error of at most 0.00019.
Values sent between devices are 32-bit elements; how exact they have to be, the bound alone decides.
No kernel may reach another device: no remote copies, remote signals or barrier semaphores. Data moves between devices by JAX's collectives and lax.ppermute only.
A program may use at most 64 MiB of HBM per device.

```python
import math
import jax
import jax.numpy as jnp
import numpy as np
from jax import lax

C = 8
K = 16
CX = 4
CY = 512
NOBS = 128
STEPS = 2
NTABLE = 16
NX = 128
NY = 8192
CELLS = 32768
OBS_TOTAL = 65536
N_WIDE = 32
N_GRP = 16


def touch_ends(drawn, key, least, top_value):
    place = [jax.random.randint(jax.random.fold_in(key, axis), (), 0, length) for axis, length in enumerate(drawn.shape)]
    widest = drawn.shape.index(max(drawn.shape))
    next_to = place[:widest] + [(place[widest] + 1) % drawn.shape[widest]] + place[widest + 1:]
    return drawn.at[tuple(place)].set(least).at[tuple(next_to)].set(top_value)


def block_levels(stream_key, dims, split, smallest, top_value):
    gain, own = 1.0, jax.random.fold_in(stream_key, 6)
    for dim, blocks in split:
        draws = jnp.exp(jax.random.uniform(jax.random.fold_in(own, dim), (blocks,), jnp.float32, smallest / len(split), top_value / len(split)))
        gain = gain * jnp.repeat(draws, dims[dim] // blocks).reshape([-1 if axis == dim else 1 for axis in range(len(dims))])
    return gain


def cumulative_ranks(amount, lean):
    portions = [(1 << 20) // math.isqrt(rank ** lean) + 1 for rank in range(1, amount + 1)]
    width = 1 + sum(portions) // (1 << 30)
    return np.cumsum(np.array([max(1, weight // width) for weight in portions]))


def skewed_ids(key, extent, number_of, lean):
    table = cumulative_ranks(number_of, lean)
    pick = jax.random.randint(jax.random.fold_in(key, 1), extent, 0, int(table[number_of - 1]))
    standing = jnp.searchsorted(jnp.asarray(table, jnp.int32), pick, side="right")
    return jax.random.permutation(jax.random.fold_in(key, 2), number_of)[standing].astype(jnp.int32)


def normal_values(stream_key, extent, spread, bound, shards=(), kind=jnp.bfloat16):
    level = block_levels(stream_key, extent, shards, -0.22, 0.18) if shards else 1.0
    array = jax.random.normal(stream_key, extent, jnp.float32) * spread * level
    return jnp.minimum(jnp.maximum(array, -bound), bound).astype(kind)


def setup_inputs(seed: int = 0) -> dict:
    key_list = jax.random.split(jax.random.key(seed), 12)
    return {
        "obs_value": normal_values(key_list[0], (OBS_TOTAL,), 1.0, 6.0, ((0, 512),), jnp.float32),
        "obs_tile": touch_ends(skewed_ids(key_list[1], (OBS_TOTAL,), N_WIDE, 2), jax.random.fold_in(key_list[1], 3), 0, N_WIDE - 1).astype(jnp.int32),
        "obs_cell": touch_ends(jax.random.randint(key_list[2], (OBS_TOTAL,), 0, CELLS), jax.random.fold_in(key_list[2], 1), 0, CELLS - 1).astype(jnp.int32),
        "obs_type": touch_ends(jax.random.randint(key_list[3], (OBS_TOTAL,), 0, 3), jax.random.fold_in(key_list[3], 1), 0, 2).astype(jnp.int32),
        "obs_weights": jnp.clip(jax.random.uniform(key_list[4], (2, C), jnp.float32, 0.2, 1.5), 0.2, 1.5),
        "diffusivity": jnp.clip(0.03 + 0.21 * jax.random.uniform(key_list[5], (NX, NY), jnp.float32) ** block_levels(key_list[5], (NX, NY), ((0, 32), (1, 16)), -0.2, 0.2), 0.03, 0.24),
        "erodibility": jnp.clip(jnp.exp(math.log(1.0) - 2.3025851 * jax.random.uniform(key_list[6], (NX, NY), jnp.float32) ** block_levels(key_list[6], (NX, NY), ((0, 32), (1, 16)), -0.2, 0.2)), 0.1, 1.0),
        "class_mixing": normal_values(key_list[7], (C, C), 0.35, 2.5, (), jnp.float32),
        "fall_table": jnp.clip(jax.random.uniform(key_list[8], (NTABLE,), jnp.float32, 0.05, 0.6), 0.05, 0.6),
        "fall_index": touch_ends(jax.random.randint(key_list[9], (C,), 0, NTABLE), jax.random.fold_in(key_list[9], 1), 0, NTABLE - 1).astype(jnp.int32),
        "bedload_rate": jnp.clip(jnp.exp(jax.random.uniform(key_list[10], (C,), jnp.float32, math.log(20.0), math.log(3000.0))), 20.0, 3000.0),
    }


def link(earlier, later):
    return (earlier[0] * later[0], later[0] * earlier[1] + later[1])


def solve_rows(rows, rate_rows):
    gain_f = 1.0 / (1.0 + rate_rows)
    gain_g = rate_rows / (1.0 + rate_rows)
    flipped = rows[:, ::-1]
    coeff = jnp.broadcast_to(gain_g[:, None], flipped.shape)
    result = lax.associative_scan(link, (coeff, gain_f[:, None] * flipped), axis=1)
    return result[1][:, ::-1]


def reference(obs_value, obs_tile, obs_cell, obs_type, obs_weights, diffusivity, erodibility, class_mixing, fall_table, fall_index, bedload_rate):
    slots = jnp.arange(OBS_TOTAL, dtype=jnp.int32)
    owner = (slots // NOBS) % N_GRP
    level = obs_cell // (CX * CY)
    xpos = obs_tile * CX + (obs_cell // CY) % CX
    ypos = owner * CY + obs_cell % CY
    live = (obs_type < 2).astype(jnp.float32)
    kind = jnp.where(obs_type < 2, obs_type, 0)
    forcing = jnp.zeros((2, K, NX, NY), jnp.float32).at[kind, level, xpos, ypos].add(obs_value * live)
    lq = jnp.einsum("tc,tkxy->ckxy", obs_weights, forcing, precision=lax.Precision.HIGHEST)
    lb = jnp.zeros((C, NX, NY), jnp.float32)
    table_hit = fall_index[:, None] == jnp.arange(NTABLE, dtype=jnp.int32)[None, :]
    settle = jnp.sum(jnp.where(table_hit, fall_table[None, :], 0.0), axis=1)
    rate_rows = jnp.repeat(bedload_rate, NX)
    for step in range(STEPS):
        lb = lb + erodibility * jnp.einsum("cd,cxy->dxy", class_mixing, lq[:, 0], precision=lax.Precision.HIGHEST)
        lb = solve_rows(lb.reshape(C * NX, NY), rate_rows).reshape(C, NX, NY)
        lq = lq.at[:, 0].add(settle[:, None, None] * lb)
        below = jnp.concatenate([jnp.zeros_like(lq[:, :1]), lq[:, :-1]], axis=1)
        lq = (1.0 - settle)[:, None, None, None] * lq + settle[:, None, None, None] * below
        moment = diffusivity * lq
        padded = jnp.pad(moment, ((0, 0), (0, 0), (1, 1), (1, 1)))
        beside = padded[:, :, 2:, 1:-1] + padded[:, :, :-2, 1:-1] + padded[:, :, 1:-1, 2:] + padded[:, :, 1:-1, :-2]
        lq = lq - 4.0 * moment + beside
    return lq, lb
```

```python
import functools
import jax
import jax.numpy as jnp
from jax import lax
from jax.experimental import pallas as pl
from jax.experimental.pallas import tpu as pltpu
from jax.sharding import PartitionSpec as P

F32 = jnp.float32
BF16 = jnp.bfloat16
C = 8
K = 16
LANES = 128
PACK = 24
W, MIX, SETTLE, RATE, SRC, MIXED, WIDE, GRP = 0, 16, 80, 88, 96, 112, 128, 129


def lane_of(shape=(8, LANES)):
    return lax.broadcasted_iota(jnp.int32, shape, len(shape) - 1)


def sub_of(shape=(8, LANES)):
    return lax.broadcasted_iota(jnp.int32, shape, len(shape) - 2)


def decay(rate):
    u = 1.0 / (2.0 * rate + 1.0)
    q = u * u
    return 2.0 * u * (1.0 + q * (1.0 / 3 + q * (1.0 / 5 + q * (1.0 / 7 + q / 9))))


def blocks(value):
    return [value[:, i * LANES : (i + 1) * LANES] for i in range(value.shape[1] // LANES)]


def stencil(field, diff, count):
    lane = lane_of()
    moment = [d * v for d, v in zip(diff, field)]
    after = [pltpu.roll(m, LANES - 1, 1) for m in moment]
    before = [pltpu.roll(m, 1, 1) for m in moment]
    out = []
    for b in range(count):
        sides = pltpu.roll(moment[b], 7, 0) + pltpu.roll(moment[b], 1, 0)
        sides = sides + jnp.where(lane == LANES - 1, after[(b + 1) % 5], after[b])
        sides = sides + jnp.where(lane == 0, before[(b - 1) % 5], before[b])
        out.append(field[b] - 4.0 * moment[b] + sides)
    return out


def sweep(rows, gain):
    lane = lane_of()
    zero = jnp.zeros((8, LANES), F32)
    power = gain
    for step in range(7):
        width = 1 << step
        turned = [pltpu.roll(v, LANES - width, 1) for v in rows] + [zero]
        near = lane < LANES - width
        rows = [
            rows[b] + power * jnp.where(near, turned[b], turned[b + 1]) for b in range(4)
        ]
        power = power * power
    rows = [rows[b] + power * rows[b + 1] if b < 3 else rows[b] for b in range(4)]
    power = power * power
    return [rows[b] + power * rows[b + 2] if b < 2 else rows[b] for b in range(4)]


def setup_kernel(par, dif, ero, low, high, de, link, table, gcol):
    de[0:4, :] = dif[...]
    de[4:6, :] = high[0:2, :]
    de[6:8, :] = low[0:2, :]
    de[8:12, :] = ero[...]
    de[12:14, :] = high[2:4, :]
    de[14:16, :] = low[2:4, :]
    length = dif.shape[1]
    lane, sub = lane_of(), sub_of()
    group = (lane // 8) % 8
    rate = jnp.zeros((8, LANES), F32)
    rate_sub = jnp.zeros((8, LANES), F32)
    for c in range(C):
        rate = jnp.where(group == c, par[RATE + c], rate)
        rate_sub = jnp.where(sub == c, par[RATE + c], rate_sub)
    log_gain = decay(rate)
    coef = jnp.zeros((8, LANES), F32)
    for c in range(C):
        part = (1.0 - par[SETTLE + c]) * par[SETTLE + c]
        for d in range(C):
            coef = jnp.where((group == c) & (sub == d), part * par[MIX + c * 8 + d], coef)
    table[0:8, :] = coef * jnp.exp(-log_gain)
    table[8:16, :] = coef * jnp.exp(-log_gain * length)
    table[16:24, :] = log_gain
    table[24:32, :] = 1.0 / (1.0 + rate)
    log_sub = decay(rate_sub)
    loss_sub = 1.0 / (1.0 + rate_sub)
    place = lax.broadcasted_iota(jnp.int32, (8, length), 1).astype(F32)
    wide_log = jnp.concatenate([log_sub] * (length // LANES), axis=1)
    down = jnp.exp(-wide_log * place) * jnp.concatenate([loss_sub] * (length // LANES), axis=1)
    d_rows, e_rows = (de[0:8, :], de[8:16, :])
    at = lax.broadcasted_iota(jnp.int32, (8, length), 1)
    d_after = jnp.where(at == length - 1, 0.0, pltpu.roll(d_rows, length - 1, 1))
    d_before = jnp.where(at == 0, 0.0, pltpu.roll(d_rows, 1, 1))
    own = e_rows * (1.0 - 4.0 * d_rows)
    own_after, own_before = (e_rows * d_after, e_rows * d_before)
    above = e_rows * pltpu.roll(d_rows, 7, 0)
    below = e_rows * pltpu.roll(d_rows, 1, 0)
    parts = [[], [], []]
    for c in range(C):
        rate_c = jnp.full((8, LANES), par[RATE + c], F32)
        gain_c = rate_c / (1.0 + rate_c)
        wide = lambda v: jnp.concatenate([v] * (length // LANES), axis=1)
        up = jnp.exp(-wide(decay(rate_c)) * (length - place))
        gcol[c * 8 : c * 8 + 8, :] = up
        mid = own + own_after * wide(1.0 / gain_c) + own_before * wide(gain_c)
        parts[0].append(mid * up)
        parts[1].append(above * up)
        parts[2].append(below * up)
    pad = jnp.zeros((64, length), F32)
    right = jnp.concatenate(parts[0] + parts[1] + parts[2] + [pad], axis=0)
    dims = (((1,), (1,)), ((), ()))
    both = lax.dot_general(
        down, right, dims, precision=lax.Precision.HIGHEST, preferred_element_type=F32
    )
    same = jnp.where(
        (group == sub) & (lane < 64),
        float(length) * loss_sub * jnp.exp(-log_sub * length),
        0.0,
    )
    link[:, 0:LANES] = both[:, 0:LANES] * coef + same
    link[:, LANES:] = both[:, LANES:] * coef


def first_kernel(par, obs, de, link, fields, solved, send, pick, spot, turn, edge):
    n_src = obs.shape[0]
    n_grp = send.shape[0]
    base = (par[WIDE] * 4.0)
    grp = par[GRP].astype(jnp.int32)
    ids = lax.broadcasted_iota(jnp.int32, (256, LANES), 0).astype(F32).astype(BF16)
    none = jnp.zeros((256, LANES), BF16)
    ones = jnp.ones((256, LANES), BF16)

    def spread(v):
        return jnp.broadcast_to(v.astype(BF16), (256, LANES))

    def put(n, carry):
        cols = pl.ds(pl.multiple_of(n * LANES, LANES), LANES)
        row = obs[n]
        value, xpos, layer, ypos = (
            row[:, 0:128], row[:, 128:256], row[:, 256:384], row[:, 384:512]
        )
        rel = xpos - base
        slot = jnp.where(rel < 0.0, rel + 8.0, rel)
        inside = (rel >= -2.0) & (rel <= 5.0)
        place = jnp.where(inside, layer * 8.0 + slot, -1.0)
        high = value.astype(BF16).astype(F32)
        hit = ids == spread(place)
        pick[0:256, cols] = jnp.where(hit, spread(high), none)
        pick[256:512, cols] = jnp.where(hit, spread(value - high), none)
        spot[0:256, cols] = jnp.where(
            ids == spread(jnp.where(ypos < 256.0, ypos, -1.0)), ones, none
        )
        spot[256:512, cols] = jnp.where(
            ids == spread(jnp.where(ypos < 256.0, -1.0, ypos - 256.0)), ones, none
        )
        return carry

    lax.fori_loop(0, n_src, put, 0, unroll=4)
    dims = (((1,), (1,)), ((), ()))
    for half in range(2):
        cols = slice(half * 256, half * 256 + 256)
        got = lax.dot_general(pick[...], spot[cols, :], dims, preferred_element_type=F32)
        fields[:, cols] = got[0:256] + got[256:512]

    lane, sub = lane_of(), sub_of()
    d_rows = blocks(de[0:8, :]) + [jnp.zeros((8, LANES), F32)]
    e_rows = blocks(de[8:16, :])
    f0, f1 = (blocks(fields[0:8, :]), blocks(fields[128:136, :]))
    bed = []
    for d in range(C):
        rate = jnp.full((8, LANES), par[RATE + d], F32)
        loss = 1.0 / (1.0 + rate)
        rows = [
            loss * e_rows[b] * (par[SRC + d] * f0[b] + par[SRC + 8 + d] * f1[b])
            for b in range(4)
        ]
        rows = sweep(rows, rate * loss)
        solved[d * 8 : d * 8 + 8, :] = jnp.concatenate(rows, axis=1)
        bed.append(rows)
    for d in range(C):
        rate = jnp.full((8, LANES), par[RATE + d], F32)
        loss = 1.0 / (1.0 + rate)
        log_gain = decay(rate)
        mixed = [par[MIXED + d] * f0[b] + par[MIXED + 8 + d] * f1[b] for b in range(4)]
        for c in range(C):
            part = (1.0 - par[SETTLE + c]) * par[SETTLE + c] * par[MIX + c * 8 + d]
            mixed = [mixed[b] + part * bed[c][b] for b in range(4)]
        mixed.append(jnp.zeros((8, LANES), F32))
        moved = stencil(mixed, d_rows, 4)
        total = jnp.zeros((8, LANES), F32)
        for b in range(4):
            fall = loss * jnp.exp(-log_gain * (lane + b * LANES).astype(F32))
            total = total + fall * (bed[d][b] + e_rows[b] * moved[b])
        tile = bed[d][0]
        tile = jnp.where(lane == 1, jnp.sum(total, axis=1, keepdims=True), tile)
        m_left, m_right = (d_rows[0] * mixed[0], d_rows[3] * mixed[3])
        for at, col in (
            (2, m_left[:, 0:1]),
            (3, m_right[:, 127:128]),
            (4, d_rows[0][:, 0:1]),
            (5, d_rows[3][:, 127:128]),
            (6, e_rows[0][:, 0:1]),
            (7, e_rows[3][:, 127:128]),
        ):
            tile = jnp.where(lane == at, col, tile)
        turn[d * 8 : d * 8 + 8, :] = tile
    turn[64:128, :] = jnp.zeros((64, LANES), F32)
    sums = turn[...].T[0:8, :]
    tile1 = jnp.where(lane < 64, link[:, LANES:], pltpu.roll(sums, 64, 1))
    for side, cols, rows in ((0, slice(0, 128), (0, 1)), (1, slice(384, 512), (126, 127))):
        turned = fields[:, cols].T
        turn[0:16, :] = de[:, cols]
        flux = turn[...].T
        for j in range(2):
            r = rows[j]
            edge[side, 2 * j : 2 * j + 1, :] = turned[r : r + 1, 0:128]
            edge[side, 2 * j + 1 : 2 * j + 2, :] = turned[r : r + 1, 128:256]
            edge[side, 4 + j : 5 + j, :] = flux[r : r + 1, :]
        edge[side, 6:8, :] = jnp.zeros((2, LANES), F32)
    for p in range(n_grp):
        send[p, 0:8, :] = link[:, 0:128]
        send[p, 8:16, :] = tile1
        send[p, 16:24, :] = jnp.where(grp + 1 == p, edge[1], edge[0])


def second_kernel(par, recv, fields, de, solved, table, gcol, tracer, bed_out, turn, twice):
    n_grp = recv.shape[0] // PACK
    grp = par[GRP].astype(jnp.int32)
    shape = (n_grp, LANES)
    lane16, sub16 = lane_of(shape), sub_of(shape)
    low16 = lane16 < 64
    group = (lane16 // 8) % 8
    within = lane16 % 8
    length = float(fields.shape[1])
    log_gain = jnp.broadcast_to(table[16:17, :], shape)
    loss = jnp.broadcast_to(table[24:25, :], shape)

    def twin(v):
        return jnp.where(low16, pltpu.roll(v, 64, 1), v)

    def later(v, k):
        return jnp.where(sub16 < n_grp - k, pltpu.roll(v, n_grp - k, 0), 0.0)

    def earlier(v, k):
        return jnp.where(sub16 >= k, pltpu.roll(v, k, 0), 0.0)

    def per_device(j):
        return twin(recv[pl.ds(8 + j, n_grp, stride=PACK), :])

    def over_classes(v):
        v = v + pltpu.roll(v, 32, 1)
        v = v + pltpu.roll(v, 16, 1)
        return v + pltpu.roll(v, 8, 1)

    head1, head2, m_left, m_right, d_left, d_right, e_left, e_right = (
        per_device(j) for j in range(8)
    )
    carry = later(head1, 1)
    k = 1
    while k < n_grp:
        carry = carry + jnp.exp(-log_gain * (length * k)) * later(carry, k)
        k *= 2
    plus = jnp.where(within < 7, pltpu.roll(carry, 127, 1), pltpu.roll(carry, 7, 1))
    minus = jnp.where(within > 0, pltpu.roll(carry, 1, 1), pltpu.roll(carry, 121, 1))
    pair = jnp.where(low16, carry, plus)
    right_add, left_add = (jnp.zeros(shape, F32), jnp.zeros(shape, F32))
    for d in range(C):
        v = recv[pl.ds(d, n_grp, stride=PACK), :] * pair
        v = v + pltpu.roll(v, 64, 1)
        u = recv[pl.ds(8 + d, n_grp, stride=PACK), :] * minus
        v = v + jnp.where(low16, u, pltpu.roll(u, 64, 1))
        mine = group == d
        head2 = head2 + jnp.where(mine, over_classes(v), 0.0)
        right_add = jnp.where(mine, over_classes(carry * table[d : d + 1, :]), right_add)
        left_add = jnp.where(mine, over_classes(carry * table[8 + d : 9 + d, :]), left_add)
    head2 = head2 + e_left * loss * earlier(m_right + d_right * right_add, 1)
    end = loss * jnp.exp(-log_gain * (length - 1.0))
    head2 = head2 + e_right * end * later(m_left + d_left * left_add, 1)
    ahead = (sub16 - grp - 1).astype(F32)
    fade = jnp.exp(-log_gain * length * jnp.maximum(ahead, 0.0))
    own1 = jnp.sum(jnp.where(sub16 == grp, carry, 0.0), axis=0, keepdims=True)
    own2 = jnp.sum(jnp.where(sub16 > grp, fade * head2, 0.0), axis=0, keepdims=True)

    lane, sub = lane_of(), sub_of()
    turn[...] = jnp.zeros(turn.shape, F32)
    before = recv[pl.ds(pl.multiple_of(jnp.maximum(grp - 1, 0) * PACK + 16, 8), 8), :]
    before = jnp.where(grp > 0, before, 0.0)
    after = recv[pl.ds(pl.multiple_of(jnp.minimum(grp + 1, n_grp - 1) * PACK + 16, 8), 8), :]
    after = jnp.where(grp < n_grp - 1, after, 0.0)
    for j in range(2):
        for source, row in ((before, 126 + j), (after, j)):
            turn[row : row + 1, 0:128] = source[2 * j : 2 * j + 1, :]
            turn[row : row + 1, 128:256] = source[2 * j + 1 : 2 * j + 2, :]
            turn[row : row + 1, 256:384] = source[4 + j : 5 + j, :]
    field_edge = turn[:, 0:256].T
    turn[:, 0:128] = field_edge[0:128]
    turn[:, 128:256] = field_edge[128:256]
    flux_edge = turn[:, 256:384].T
    d_rows = blocks(de[0:8, :]) + [flux_edge[0:8]]
    e_rows = blocks(de[8:16, :]) + [flux_edge[8:16]]

    def both(half):
        def step(k, carry):
            rows = pl.ds(pl.multiple_of(half * 128 + k * 8, 8), 8)
            here = pl.ds(pl.multiple_of(k * 8, 8), 8)
            field = blocks(fields[rows, :]) + [turn[here, half * 128 : half * 128 + 128]]
            field = stencil(stencil(field, d_rows, 5), d_rows, 4)
            twice[rows, :] = jnp.concatenate(field, axis=1)
            return carry

        return step

    lax.fori_loop(0, K, both(0), 0, unroll=2)
    lax.fori_loop(0, K, both(1), 0, unroll=2)

    f0 = blocks(fields[0:8, :]) + [turn[0:8, 0:128]]
    f1 = blocks(fields[128:136, :]) + [turn[0:8, 128:256]]
    bed = []
    for c in range(C):
        rate = jnp.full((8, LANES), par[RATE + c], F32)
        loss = 1.0 / (1.0 + rate)
        gain = rate * loss
        mine = lane == c * 8 + sub
        into = jnp.sum(jnp.where(mine, own1, 0.0), axis=1, keepdims=True)
        up = blocks(gcol[c * 8 : c * 8 + 8, :])
        rows = [v + u * into for v, u in zip(blocks(solved[c * 8 : c * 8 + 8, :]), up)]
        source = e_rows[4] * (par[SRC + c] * f0[4] + par[SRC + 8 + c] * f1[4])
        last = loss * source + gain * rows[0][:, 0:1]
        second = loss * source + gain * pltpu.roll(last, 127, 1)
        beyond = into + (into - pltpu.roll(source, 1, 1)) / rate
        rim = jnp.where(lane == 127, last, jnp.where(lane == 126, second, 0.0))
        rim = jnp.where(lane == 0, into, jnp.where(lane == 1, beyond, rim))
        bed.append(rows + [rim])
    for d in range(C):
        rate = jnp.full((8, LANES), par[RATE + d], F32)
        loss = 1.0 / (1.0 + rate)
        gain = rate * loss
        mixed = [par[MIXED + d] * f0[b] + par[MIXED + 8 + d] * f1[b] for b in range(5)]
        for c in range(C):
            part = (1.0 - par[SETTLE + c]) * par[SETTLE + c] * par[MIX + c * 8 + d]
            mixed = [mixed[b] + part * bed[c][b] for b in range(5)]
        moved = stencil(mixed, d_rows, 5)
        source = [loss * (bed[d][b] + e_rows[b] * moved[b]) for b in range(5)]
        rows = sweep(source[0:4], gain)
        mine = lane == d * 8 + sub
        into = jnp.sum(jnp.where(mine, own2, 0.0), axis=1, keepdims=True)
        up = blocks(gcol[d * 8 : d * 8 + 8, :])
        rows = [v + u * into for v, u in zip(rows, up)]
        last = source[4] + gain * rows[0][:, 0:1]
        rim = jnp.where(lane == 127, last, jnp.where(lane == 0, into, 0.0))
        bed_out[d] = jnp.concatenate(rows, axis=1)[0:4, :]
        s = par[SETTLE + d]
        stirred = stencil(rows + [rim], d_rows, 4)
        first = stencil(stencil(bed[d], d_rows, 5), d_rows, 4)
        stirred = jnp.concatenate(stirred, axis=1)[0:4, :]
        first = jnp.concatenate(first, axis=1)[0:4, :]
        keep, share, pass_on = ((1.0 - s) * (1.0 - s), 2.0 * s * (1.0 - s), s * s)
        w0, w1 = (par[W + d], par[W + 8 + d])
        old, older = (None, None)
        for k in range(K):
            now = w0 * twice[k * 8 : k * 8 + 4, :] + w1 * twice[128 + k * 8 : 132 + k * 8, :]
            if k == 0:
                now = now + s * first
            out = keep * now
            if k == 0:
                out = out + ((1.0 - s) * s) * stirred
            if k == 1:
                out = out + pass_on * stirred
            if old is not None:
                out = out + share * old
            if older is not None:
                out = out + pass_on * older
            tracer[d, k] = out
            old, older = (now, old)


VM = pl.BlockSpec(memory_space=pltpu.VMEM)
SM = pl.BlockSpec(memory_space=pltpu.SMEM)


def shape_of(*dims):
    return jax.ShapeDtypeStruct(dims, F32)


def local(
    obs_value, obs_tile, obs_cell, obs_type, obs_weights, diffusivity, erodibility,
    class_mixing, fall_table, fall_index, bedload_rate,
):
    n_wide, n_grp = (lax.axis_size("wide"), lax.axis_size("grp"))
    tile_x, tile_y = diffusivity.shape
    slots = obs_value.shape[0]
    up = [(i, i + 1) for i in range(n_wide - 1)]
    down = [(i + 1, i) for i in range(n_wide - 1)]
    head = jnp.concatenate([diffusivity[0:2], erodibility[0:2]], axis=0)
    tail = jnp.concatenate([diffusivity[2:4], erodibility[2:4]], axis=0)
    low = lax.ppermute(tail, "wide", up)
    high = lax.ppermute(head, "wide", down)

    live = jnp.where(obs_type < 2, obs_value, 0.0)
    layer = jnp.where(obs_type < 2, obs_type, 0) * K + obs_cell // (tile_x * tile_y)
    xpos = obs_tile * tile_x + (obs_cell // tile_y) % tile_x
    ypos = obs_cell % tile_y
    mine = jnp.concatenate([live, xpos.astype(F32), layer.astype(F32), ypos.astype(F32)])
    mine = jnp.broadcast_to(mine[None, None, :], (n_wide, 1, 4 * slots))
    obs = lax.all_to_all(mine, "wide", split_axis=0, concat_axis=0, tiled=True)

    hit = fall_index[:, None] == jnp.arange(fall_table.shape[0], dtype=jnp.int32)[None, :]
    settle = jnp.sum(jnp.where(hit, fall_table[None, :], 0.0), axis=1)
    source = jnp.sum(obs_weights[:, :, None] * class_mixing[None], axis=1)
    mixed = jnp.sum(
        (obs_weights * (1.0 - settle)[None])[:, :, None] * class_mixing[None], axis=1
    )
    place = jnp.stack([lax.axis_index("wide"), lax.axis_index("grp")]).astype(F32)
    par = jnp.concatenate(
        [obs_weights.reshape(-1), class_mixing.reshape(-1), settle, bedload_rate,
         source.reshape(-1), mixed.reshape(-1), place, jnp.zeros((126,), F32)]
    )

    de, link, table, gcol = pl.pallas_call(
        setup_kernel,
        out_shape=(shape_of(16, tile_y), shape_of(8, 256), shape_of(32, LANES), shape_of(64, tile_y)),
        in_specs=[SM, VM, VM, VM, VM],
        out_specs=(VM, VM, VM, VM),
        cost_estimate=pl.CostEstimate(flops=10_000_000, bytes_accessed=200_000, transcendentals=40_000),
    )(par, diffusivity, erodibility, low, high)

    fields, solved, send = pl.pallas_call(
        first_kernel,
        out_shape=(shape_of(256, tile_y), shape_of(64, tile_y), shape_of(n_grp, PACK, LANES)),
        in_specs=[SM, VM, VM, VM],
        out_specs=(VM, VM, VM),
        scratch_shapes=[
            pltpu.VMEM((512, n_wide * slots), BF16),
            pltpu.VMEM((512, n_wide * slots), BF16),
            pltpu.VMEM((128, 128), F32),
            pltpu.VMEM((2, 8, 128), F32),
        ],
    )(par, obs, de, link)

    recv = lax.all_to_all(send, "grp", split_axis=0, concat_axis=0, tiled=True)
    tracer, bed = pl.pallas_call(
        second_kernel,
        out_shape=(shape_of(C, K, tile_x, tile_y), shape_of(C, tile_x, tile_y)),
        in_specs=[SM, VM, VM, VM, VM, VM, VM],
        out_specs=(VM, VM),
        scratch_shapes=[pltpu.VMEM((128, 384), F32), pltpu.VMEM((256, tile_y), F32)],
    )(par, recv.reshape(n_grp * PACK, LANES), fields, de, solved, table, gcol)
    return (tracer, bed)


def solution(mesh):
    flat = P(("wide", "grp"))
    grid = P("wide", "grp")
    in_specs = (flat, flat, flat, flat, P(), grid, grid, P(), P(), P(), P())
    out_specs = (P(None, None, "wide", "grp"), P(None, "wide", "grp"))
    return jax.shard_map(local, mesh=mesh, in_specs=in_specs, out_specs=out_specs, check_vma=False)
```

```python
import jax
import jax.numpy as jnp
from jax import lax
from jax.experimental import pallas as pl
from jax.experimental.pallas import tpu as pltpu
from jax.sharding import PartitionSpec as P

F32 = jnp.float32
BF16 = jnp.bfloat16
C = 8
K = 16
LANES = 128
PACK = 24
W, MIX, SETTLE, RATE, SRC, MIXED, WIDE, GRP, PART = 0, 16, 80, 88, 96, 112, 128, 129, 136


def lane_of(shape=(8, LANES)):
    return lax.broadcasted_iota(jnp.int32, shape, len(shape) - 1)


def sub_of(shape=(8, LANES)):
    return lax.broadcasted_iota(jnp.int32, shape, len(shape) - 2)


def decay(rate):
    u = 1.0 / (2.0 * rate + 1.0)
    q = u * u
    return 2.0 * u * (1.0 + q * (1.0 / 3 + q * (1.0 / 5 + q * (1.0 / 7 + q / 9))))


def blocks(value):
    return [value[:, i * LANES : (i + 1) * LANES] for i in range(value.shape[1] // LANES)]


def stencil(field, diff, count):
    lane = lane_of()
    moment = [d * v for d, v in zip(diff, field)]
    after = [pltpu.roll(m, LANES - 1, 1) for m in moment]
    before = [pltpu.roll(m, 1, 1) for m in moment]
    out = []
    for b in range(count):
        sides = pltpu.roll(moment[b], 7, 0) + pltpu.roll(moment[b], 1, 0)
        sides = sides + jnp.where(lane == LANES - 1, after[(b + 1) % 5], after[b])
        sides = sides + jnp.where(lane == 0, before[(b - 1) % 5], before[b])
        out.append(field[b] - 4.0 * moment[b] + sides)
    return out


def sweep(rows, gain):
    lane = lane_of()
    zero = jnp.zeros((8, LANES), F32)
    power = gain
    for step in range(7):
        width = 1 << step
        turned = [pltpu.roll(v, LANES - width, 1) for v in rows] + [zero]
        near = lane < LANES - width
        rows = [
            rows[b] + power * jnp.where(near, turned[b], turned[b + 1]) for b in range(4)
        ]
        power = power * power
    rows = [rows[b] + power * rows[b + 1] if b < 3 else rows[b] for b in range(4)]
    power = power * power
    return [rows[b] + power * rows[b + 2] if b < 2 else rows[b] for b in range(4)]


def setup_kernel(
    weights, mixing, falls, index, rates, place, dif, ero, low, high, par, de, link, table, gcol
):
    par[WIDE] = place[0].astype(F32)
    par[GRP] = place[1].astype(F32)
    for c in range(C):
        settle = falls[index[c]]
        par[SETTLE + c] = settle
        par[RATE + c] = rates[c]
        part = (1.0 - settle) * settle
        for t in range(2):
            par[W + t * 8 + c] = weights[t, c]
        for d in range(C):
            par[MIX + c * 8 + d] = mixing[c, d]
            par[PART + c * 8 + d] = part * mixing[c, d]
    for t in range(2):
        for d in range(C):
            source, mixed = (0.0, 0.0)
            for c in range(C):
                term = par[W + t * 8 + c] * par[MIX + c * 8 + d]
                source = source + term
                mixed = mixed + term * (1.0 - par[SETTLE + c])
            par[SRC + t * 8 + d] = source
            par[MIXED + t * 8 + d] = mixed
    de[0:4, :] = dif[...]
    de[4:6, :] = high[0:2, :]
    de[6:8, :] = low[0:2, :]
    de[8:12, :] = ero[...]
    de[12:14, :] = high[2:4, :]
    de[14:16, :] = low[2:4, :]
    length = dif.shape[1]
    lane, sub = lane_of(), sub_of()
    group = (lane // 8) % 8
    rate = jnp.zeros((8, LANES), F32)
    rate_sub = jnp.zeros((8, LANES), F32)
    for c in range(C):
        rate = jnp.where(group == c, par[RATE + c], rate)
        rate_sub = jnp.where(sub == c, par[RATE + c], rate_sub)
    log_gain = decay(rate)
    coef = jnp.zeros((8, LANES), F32)
    for c in range(C):
        for d in range(C):
            coef = jnp.where((group == c) & (sub == d), par[PART + c * 8 + d], coef)
    table[0:8, :] = coef * jnp.exp(-log_gain)
    table[8:16, :] = coef * jnp.exp(-log_gain * length)
    table[16:24, :] = log_gain
    table[24:32, :] = 1.0 / (1.0 + rate)
    log_sub = decay(rate_sub)
    loss_sub = 1.0 / (1.0 + rate_sub)
    place = lax.broadcasted_iota(jnp.int32, (8, length), 1).astype(F32)
    wide_log = jnp.concatenate([log_sub] * (length // LANES), axis=1)
    down = jnp.exp(-wide_log * place) * jnp.concatenate([loss_sub] * (length // LANES), axis=1)
    d_rows, e_rows = (de[0:8, :], de[8:16, :])
    at = lax.broadcasted_iota(jnp.int32, (8, length), 1)
    d_after = jnp.where(at == length - 1, 0.0, pltpu.roll(d_rows, length - 1, 1))
    d_before = jnp.where(at == 0, 0.0, pltpu.roll(d_rows, 1, 1))
    own = e_rows * (1.0 - 4.0 * d_rows)
    own_after, own_before = (e_rows * d_after, e_rows * d_before)
    above = e_rows * pltpu.roll(d_rows, 7, 0)
    below = e_rows * pltpu.roll(d_rows, 1, 0)
    parts = [[], [], []]
    for c in range(C):
        rate_c = jnp.full((8, LANES), par[RATE + c], F32)
        gain_c = rate_c / (1.0 + rate_c)
        wide = lambda v: jnp.concatenate([v] * (length // LANES), axis=1)
        up = jnp.exp(-wide(decay(rate_c)) * (length - place))
        gcol[c * 8 : c * 8 + 8, :] = up
        mid = own + own_after * wide(1.0 / gain_c) + own_before * wide(gain_c)
        parts[0].append(mid * up)
        parts[1].append(above * up)
        parts[2].append(below * up)
    pad = jnp.zeros((64, length), F32)
    right = jnp.concatenate(parts[0] + parts[1] + parts[2] + [pad], axis=0)
    dims = (((1,), (1,)), ((), ()))
    both = lax.dot_general(
        down, right, dims, precision=lax.Precision.HIGHEST, preferred_element_type=F32
    )
    same = jnp.where(
        (group == sub) & (lane < 64),
        float(length) * loss_sub * jnp.exp(-log_sub * length),
        0.0,
    )
    link[:, 0:LANES] = both[:, 0:LANES] * coef + same
    link[:, LANES:] = both[:, LANES:] * coef


def first_kernel(par, obs, de, link, fields, solved, send, turn, edge):
    n_src = obs.shape[0]
    n_grp = send.shape[0]
    base = (par[WIDE] * 4.0)
    grp = par[GRP].astype(jnp.int32)
    ids = lax.broadcasted_iota(jnp.int32, (256, LANES), 0).astype(F32).astype(BF16)
    none = jnp.zeros((256, LANES), BF16)
    ones = jnp.ones((256, LANES), BF16)

    def spread(v):
        return jnp.broadcast_to(v.astype(BF16), (256, LANES))

    left_high, left_low, right = ([], [], [])
    for n in range(n_src):
        row = obs[n]
        value, xpos, layer, ypos = (
            row[:, 0:128], row[:, 128:256], row[:, 256:384], row[:, 384:512]
        )
        rel = xpos - base
        slot = jnp.where(rel < 0.0, rel + 8.0, rel)
        inside = (rel >= -2.0) & (rel <= 5.0)
        place = jnp.where(inside, layer * 8.0 + slot, -1.0)
        high = value.astype(BF16).astype(F32)
        hit = ids == spread(place)
        left_high.append(jnp.where(hit, spread(high), none))
        left_low.append(jnp.where(hit, spread(value - high), none))
        near = jnp.where(ids == spread(jnp.where(ypos < 256.0, ypos, -1.0)), ones, none)
        far = jnp.where(ids == spread(jnp.where(ypos < 256.0, -1.0, ypos - 256.0)), ones, none)
        right.append(jnp.concatenate([near, far], axis=0))
    dims = (((1,), (1,)), ((), ()))
    left = jnp.concatenate(
        [jnp.concatenate(left_high, axis=1), jnp.concatenate(left_low, axis=1)], axis=0
    )
    got = lax.dot_general(
        left, jnp.concatenate(right, axis=1), dims, preferred_element_type=F32
    )
    fields[...] = got[0:256] + got[256:512]

    lane, sub = lane_of(), sub_of()
    d_rows = blocks(de[0:8, :]) + [jnp.zeros((8, LANES), F32)]
    e_rows = blocks(de[8:16, :])
    f0, f1 = (blocks(fields[0:8, :]), blocks(fields[128:136, :]))
    bed = []
    for d in range(C):
        rate = jnp.full((8, LANES), par[RATE + d], F32)
        loss = 1.0 / (1.0 + rate)
        rows = [
            loss * e_rows[b] * (par[SRC + d] * f0[b] + par[SRC + 8 + d] * f1[b])
            for b in range(4)
        ]
        rows = sweep(rows, rate * loss)
        solved[d * 8 : d * 8 + 8, :] = jnp.concatenate(rows, axis=1)
        bed.append(rows)
    for d in range(C):
        rate = jnp.full((8, LANES), par[RATE + d], F32)
        loss = 1.0 / (1.0 + rate)
        log_gain = decay(rate)
        mixed = [par[MIXED + d] * f0[b] + par[MIXED + 8 + d] * f1[b] for b in range(4)]
        for c in range(C):
            part = par[PART + c * 8 + d]
            mixed = [mixed[b] + part * bed[c][b] for b in range(4)]
        mixed.append(jnp.zeros((8, LANES), F32))
        moved = stencil(mixed, d_rows, 4)
        total = jnp.zeros((8, LANES), F32)
        for b in range(4):
            fall = loss * jnp.exp(-log_gain * (lane + b * LANES).astype(F32))
            total = total + fall * (bed[d][b] + e_rows[b] * moved[b])
        tile = bed[d][0]
        tile = jnp.where(lane == 1, jnp.sum(total, axis=1, keepdims=True), tile)
        m_left, m_right = (d_rows[0] * mixed[0], d_rows[3] * mixed[3])
        for at, col in (
            (2, m_left[:, 0:1]),
            (3, m_right[:, 127:128]),
            (4, d_rows[0][:, 0:1]),
            (5, d_rows[3][:, 127:128]),
            (6, e_rows[0][:, 0:1]),
            (7, e_rows[3][:, 127:128]),
        ):
            tile = jnp.where(lane == at, col, tile)
        turn[d * 8 : d * 8 + 8, :] = tile
    turn[64:128, :] = jnp.zeros((64, LANES), F32)
    sums = turn[...].T[0:8, :]
    tile1 = jnp.where(lane < 64, link[:, LANES:], pltpu.roll(sums, 64, 1))
    for side, cols, rows in ((0, slice(0, 128), (0, 1)), (1, slice(384, 512), (126, 127))):
        turned = fields[:, cols].T
        turn[0:16, :] = de[:, cols]
        flux = turn[...].T
        for j in range(2):
            r = rows[j]
            edge[side, 2 * j : 2 * j + 1, :] = turned[r : r + 1, 0:128]
            edge[side, 2 * j + 1 : 2 * j + 2, :] = turned[r : r + 1, 128:256]
            edge[side, 4 + j : 5 + j, :] = flux[r : r + 1, :]
        edge[side, 6:8, :] = jnp.zeros((2, LANES), F32)
    for p in range(n_grp):
        send[p, 0:8, :] = link[:, 0:128]
        send[p, 8:16, :] = tile1
        send[p, 16:24, :] = jnp.where(grp + 1 == p, edge[1], edge[0])


def second_kernel(par, recv, fields, de, solved, table, gcol, tracer, bed_out, turn, twice):
    n_grp = recv.shape[0] // PACK
    grp = par[GRP].astype(jnp.int32)
    shape = (n_grp, LANES)
    lane16, sub16 = lane_of(shape), sub_of(shape)
    low16 = lane16 < 64
    group = (lane16 // 8) % 8
    within = lane16 % 8
    length = float(fields.shape[1])
    log_gain = jnp.broadcast_to(table[16:17, :], shape)
    loss = jnp.broadcast_to(table[24:25, :], shape)

    def twin(v):
        return jnp.where(low16, pltpu.roll(v, 64, 1), v)

    def later(v, k):
        return jnp.where(sub16 < n_grp - k, pltpu.roll(v, n_grp - k, 0), 0.0)

    def earlier(v, k):
        return jnp.where(sub16 >= k, pltpu.roll(v, k, 0), 0.0)

    def per_device(j):
        return twin(recv[pl.ds(8 + j, n_grp, stride=PACK), :])

    def over_classes(v):
        v = v + pltpu.roll(v, 32, 1)
        v = v + pltpu.roll(v, 16, 1)
        return v + pltpu.roll(v, 8, 1)

    head1, head2, m_left, m_right, d_left, d_right, e_left, e_right = (
        per_device(j) for j in range(8)
    )
    carry = later(head1, 1)
    k = 1
    while k < n_grp:
        carry = carry + jnp.exp(-log_gain * (length * k)) * later(carry, k)
        k *= 2
    plus = jnp.where(within < 7, pltpu.roll(carry, 127, 1), pltpu.roll(carry, 7, 1))
    minus = jnp.where(within > 0, pltpu.roll(carry, 1, 1), pltpu.roll(carry, 121, 1))
    pair = jnp.where(low16, carry, plus)
    right_add, left_add = (jnp.zeros(shape, F32), jnp.zeros(shape, F32))
    for d in range(C):
        v = recv[pl.ds(d, n_grp, stride=PACK), :] * pair
        v = v + pltpu.roll(v, 64, 1)
        u = recv[pl.ds(8 + d, n_grp, stride=PACK), :] * minus
        v = v + jnp.where(low16, u, pltpu.roll(u, 64, 1))
        mine = group == d
        head2 = head2 + jnp.where(mine, over_classes(v), 0.0)
        right_add = jnp.where(mine, over_classes(carry * table[d : d + 1, :]), right_add)
        left_add = jnp.where(mine, over_classes(carry * table[8 + d : 9 + d, :]), left_add)
    head2 = head2 + e_left * loss * earlier(m_right + d_right * right_add, 1)
    end = loss * jnp.exp(-log_gain * (length - 1.0))
    head2 = head2 + e_right * end * later(m_left + d_left * left_add, 1)
    ahead = (sub16 - grp - 1).astype(F32)
    fade = jnp.exp(-log_gain * length * jnp.maximum(ahead, 0.0))
    own1 = jnp.sum(jnp.where(sub16 == grp, carry, 0.0), axis=0, keepdims=True)
    own2 = jnp.sum(jnp.where(sub16 > grp, fade * head2, 0.0), axis=0, keepdims=True)

    lane, sub = lane_of(), sub_of()
    turn[...] = jnp.zeros(turn.shape, F32)
    before = recv[pl.ds(pl.multiple_of(jnp.maximum(grp - 1, 0) * PACK + 16, 8), 8), :]
    before = jnp.where(grp > 0, before, 0.0)
    after = recv[pl.ds(pl.multiple_of(jnp.minimum(grp + 1, n_grp - 1) * PACK + 16, 8), 8), :]
    after = jnp.where(grp < n_grp - 1, after, 0.0)
    for j in range(2):
        for source, row in ((before, 126 + j), (after, j)):
            turn[row : row + 1, 0:128] = source[2 * j : 2 * j + 1, :]
            turn[row : row + 1, 128:256] = source[2 * j + 1 : 2 * j + 2, :]
            turn[row : row + 1, 256:384] = source[4 + j : 5 + j, :]
    field_edge = turn[:, 0:256].T
    turn[:, 0:128] = field_edge[0:128]
    turn[:, 128:256] = field_edge[128:256]
    flux_edge = turn[:, 256:384].T
    d_rows = blocks(de[0:8, :]) + [flux_edge[0:8]]
    e_rows = blocks(de[8:16, :]) + [flux_edge[8:16]]

    def both(half):
        def step(k, carry):
            rows = pl.ds(pl.multiple_of(half * 128 + k * 8, 8), 8)
            here = pl.ds(pl.multiple_of(k * 8, 8), 8)
            field = blocks(fields[rows, :]) + [turn[here, half * 128 : half * 128 + 128]]
            field = stencil(stencil(field, d_rows, 5), d_rows, 4)
            twice[rows, :] = jnp.concatenate(field, axis=1)
            return carry

        return step

    lax.fori_loop(0, K, both(0), 0, unroll=2)
    lax.fori_loop(0, K, both(1), 0, unroll=2)

    f0 = blocks(fields[0:8, :]) + [turn[0:8, 0:128]]
    f1 = blocks(fields[128:136, :]) + [turn[0:8, 128:256]]
    bed = []
    for c in range(C):
        rate = jnp.full((8, LANES), par[RATE + c], F32)
        loss = 1.0 / (1.0 + rate)
        gain = rate * loss
        mine = lane == c * 8 + sub
        into = jnp.sum(jnp.where(mine, own1, 0.0), axis=1, keepdims=True)
        up = blocks(gcol[c * 8 : c * 8 + 8, :])
        rows = [v + u * into for v, u in zip(blocks(solved[c * 8 : c * 8 + 8, :]), up)]
        source = e_rows[4] * (par[SRC + c] * f0[4] + par[SRC + 8 + c] * f1[4])
        last = loss * source + gain * rows[0][:, 0:1]
        second = loss * source + gain * pltpu.roll(last, 127, 1)
        beyond = into + (into - pltpu.roll(source, 1, 1)) / rate
        rim = jnp.where(lane == 127, last, jnp.where(lane == 126, second, 0.0))
        rim = jnp.where(lane == 0, into, jnp.where(lane == 1, beyond, rim))
        bed.append(rows + [rim])
    for d in range(C):
        rate = jnp.full((8, LANES), par[RATE + d], F32)
        loss = 1.0 / (1.0 + rate)
        gain = rate * loss
        mixed = [par[MIXED + d] * f0[b] + par[MIXED + 8 + d] * f1[b] for b in range(5)]
        for c in range(C):
            part = par[PART + c * 8 + d]
            mixed = [mixed[b] + part * bed[c][b] for b in range(5)]
        moved = stencil(mixed, d_rows, 5)
        source = [loss * (bed[d][b] + e_rows[b] * moved[b]) for b in range(5)]
        rows = sweep(source[0:4], gain)
        mine = lane == d * 8 + sub
        into = jnp.sum(jnp.where(mine, own2, 0.0), axis=1, keepdims=True)
        up = blocks(gcol[d * 8 : d * 8 + 8, :])
        rows = [v + u * into for v, u in zip(rows, up)]
        last = source[4] + gain * rows[0][:, 0:1]
        rim = jnp.where(lane == 127, last, jnp.where(lane == 0, into, 0.0))
        bed_out[d] = jnp.concatenate(rows, axis=1)[0:4, :]
        s = par[SETTLE + d]
        stirred = stencil(rows + [rim], d_rows, 4)
        first = stencil(stencil(bed[d], d_rows, 5), d_rows, 4)
        stirred = jnp.concatenate(stirred, axis=1)[0:4, :]
        first = jnp.concatenate(first, axis=1)[0:4, :]
        keep, share, pass_on = ((1.0 - s) * (1.0 - s), 2.0 * s * (1.0 - s), s * s)
        w0, w1 = (par[W + d], par[W + 8 + d])
        old, older = (None, None)
        for k in range(K):
            now = w0 * twice[k * 8 : k * 8 + 4, :] + w1 * twice[128 + k * 8 : 132 + k * 8, :]
            if k == 0:
                now = now + s * first
            out = keep * now
            if k == 0:
                out = out + ((1.0 - s) * s) * stirred
            if k == 1:
                out = out + pass_on * stirred
            if old is not None:
                out = out + share * old
            if older is not None:
                out = out + pass_on * older
            tracer[d, k] = out
            old, older = (now, old)


VM = pl.BlockSpec(memory_space=pltpu.VMEM)
SM = pl.BlockSpec(memory_space=pltpu.SMEM)


def shape_of(*dims):
    return jax.ShapeDtypeStruct(dims, F32)


def local(
    obs_value, obs_tile, obs_cell, obs_type, obs_weights, diffusivity, erodibility,
    class_mixing, fall_table, fall_index, bedload_rate,
):
    n_wide, n_grp = (lax.axis_size("wide"), lax.axis_size("grp"))
    tile_x, tile_y = diffusivity.shape
    slots = obs_value.shape[0]
    up = [(i, i + 1) for i in range(n_wide - 1)]
    down = [(i + 1, i) for i in range(n_wide - 1)]
    head = jnp.concatenate([diffusivity[0:2], erodibility[0:2]], axis=0)
    tail = jnp.concatenate([diffusivity[2:4], erodibility[2:4]], axis=0)
    low = lax.ppermute(tail, "wide", up)
    high = lax.ppermute(head, "wide", down)

    live = jnp.where(obs_type < 2, obs_value, 0.0)
    layer = jnp.where(obs_type < 2, obs_type, 0) * K + obs_cell // (tile_x * tile_y)
    xpos = obs_tile * tile_x + (obs_cell // tile_y) % tile_x
    ypos = obs_cell % tile_y
    mine = jnp.concatenate([live, xpos.astype(F32), layer.astype(F32), ypos.astype(F32)])
    mine = jnp.broadcast_to(mine[None, None, :], (n_wide, 1, 4 * slots))
    obs = lax.all_to_all(mine, "wide", split_axis=0, concat_axis=0, tiled=True)

    place = jnp.stack([lax.axis_index("wide"), lax.axis_index("grp")]).astype(jnp.int32)

    par, de, link, table, gcol = pl.pallas_call(
        setup_kernel,
        out_shape=(shape_of(256), shape_of(16, tile_y), shape_of(8, 256), shape_of(32, LANES), shape_of(64, tile_y)),
        in_specs=[SM] * 6 + [VM] * 4,
        out_specs=(SM, VM, VM, VM, VM),
        cost_estimate=pl.CostEstimate(flops=10_000_000, bytes_accessed=200_000, transcendentals=40_000),
        compiler_params=pltpu.CompilerParams(vmem_limit_bytes=4 << 20),
    )(obs_weights, class_mixing, fall_table, fall_index, bedload_rate, place, diffusivity, erodibility, low, high)

    fields, solved, send = pl.pallas_call(
        first_kernel,
        out_shape=(shape_of(256, tile_y), shape_of(64, tile_y), shape_of(n_grp, PACK, LANES)),
        in_specs=[SM, VM, VM, VM],
        out_specs=(VM, VM, VM),
        scratch_shapes=[
            pltpu.VMEM((128, 128), F32),
            pltpu.VMEM((2, 8, 128), F32),
        ],
        compiler_params=pltpu.CompilerParams(vmem_limit_bytes=16 << 20),
    )(par, obs, de, link)

    recv = lax.all_to_all(send, "grp", split_axis=0, concat_axis=0, tiled=True)
    tracer, bed = pl.pallas_call(
        second_kernel,
        out_shape=(shape_of(C, K, tile_x, tile_y), shape_of(C, tile_x, tile_y)),
        in_specs=[SM, VM, VM, VM, VM, VM, VM],
        out_specs=(VM, VM),
        scratch_shapes=[pltpu.VMEM((128, 384), F32), pltpu.VMEM((256, tile_y), F32)],
        compiler_params=pltpu.CompilerParams(vmem_limit_bytes=8 << 20),
    )(par, recv.reshape(n_grp * PACK, LANES), fields, de, solved, table, gcol)
    return (tracer, bed)


def solution(mesh):
    flat = P(("wide", "grp"))
    grid = P("wide", "grp")
    in_specs = (flat, flat, flat, flat, P(), grid, grid, P(), P(), P(), P())
    out_specs = (P(None, None, "wide", "grp"), P(None, "wide", "grp"))
    return jax.shard_map(local, mesh=mesh, in_specs=in_specs, out_specs=out_specs, check_vma=False)
```

```python
import jax
import jax.numpy as jnp
from jax import lax
from jax.experimental import pallas as pl
from jax.experimental.pallas import tpu as pltpu
from jax.sharding import PartitionSpec as P

F32 = jnp.float32
BF16 = jnp.bfloat16
C = 8
K = 16
LANES = 128
PACK = 24
W, MIX, SETTLE, RATE, SRC, MIXED, WIDE, GRP, PART = 0, 16, 80, 88, 96, 112, 128, 129, 136


def lane_of(shape=(8, LANES)):
    return lax.broadcasted_iota(jnp.int32, shape, len(shape) - 1)


def sub_of(shape=(8, LANES)):
    return lax.broadcasted_iota(jnp.int32, shape, len(shape) - 2)


def decay(rate):
    u = 1.0 / (2.0 * rate + 1.0)
    q = u * u
    return 2.0 * u * (1.0 + q * (1.0 / 3 + q * (1.0 / 5 + q * (1.0 / 7 + q / 9))))


def blocks(value):
    return [value[:, i * LANES : (i + 1) * LANES] for i in range(value.shape[1] // LANES)]


def stencil(field, diff, count):
    lane = lane_of()
    ring = len(field)
    moment = [d * v for d, v in zip(diff, field)]
    after = [pltpu.roll(m, LANES - 1, 1) for m in moment]
    before = [pltpu.roll(m, 1, 1) for m in moment]
    out = []
    for b in range(count):
        sides = pltpu.roll(moment[b], 7, 0) + pltpu.roll(moment[b], 1, 0)
        right = 0.0 if ring == 4 and b == 3 else after[(b + 1) % ring]
        left = 0.0 if ring == 4 and b == 0 else before[(b - 1) % ring]
        sides = sides + jnp.where(lane == LANES - 1, right, after[b])
        sides = sides + jnp.where(lane == 0, left, before[b])
        out.append(field[b] - 4.0 * moment[b] + sides)
    return out


def sweep(rows, gain):
    lane = lane_of()
    zero = jnp.zeros((8, LANES), F32)
    power = gain
    for step in range(7):
        width = 1 << step
        turned = [pltpu.roll(v, LANES - width, 1) for v in rows] + [zero]
        near = lane < LANES - width
        rows = [
            rows[b] + power * jnp.where(near, turned[b], turned[b + 1]) for b in range(4)
        ]
        power = power * power
    rows = [rows[b] + power * rows[b + 1] if b < 3 else rows[b] for b in range(4)]
    power = power * power
    return [rows[b] + power * rows[b + 2] if b < 2 else rows[b] for b in range(4)]


def pack_kernel(place, value, tile, cell, kind, dif, ero, send):
    n_wide = send.shape[0]
    length = dif.shape[1]
    wide = place[0]
    sort = kind[...]
    live = sort < 2
    row = [
        jnp.where(live, value[...], 0.0),
        (tile[...] * 4 + (lax.shift_right_logical(cell[...], 9) & 3)).astype(F32),
        (jnp.where(live, sort, 0) * K + lax.shift_right_logical(cell[...], 11)).astype(F32),
        (cell[...] & 511).astype(F32),
    ]
    row = jnp.concatenate(row, axis=1)
    first = jnp.concatenate([dif[0:1], dif[1:2], ero[0:1], ero[1:2]], axis=1)
    last = jnp.concatenate([dif[2:3], dif[3:4], ero[2:3], ero[3:4]], axis=1)
    for p in range(n_wide):
        send[p] = jnp.concatenate([row, first], axis=1)

    @pl.when(wide + 1 < n_wide)
    def _():
        send[wide + 1] = jnp.concatenate([row, last], axis=1)


def fold(rows):
    low = sub_of() < 4
    return [jnp.where(low, rows[b], pltpu.roll(rows[b + 1], 4, 0)) for b in (0, 2)]


def setup_kernel(weights, mixing, falls, index, rates, place, par, coef_out, table, gcol, gdown):
    par[WIDE] = place[0].astype(F32)
    par[GRP] = place[1].astype(F32)
    for c in range(C):
        settle = falls[index[c]]
        par[SETTLE + c] = settle
        par[RATE + c] = rates[c]
        part = (1.0 - settle) * settle
        for t in range(2):
            par[W + t * 8 + c] = weights[t, c]
        for d in range(C):
            par[MIX + c * 8 + d] = mixing[c, d]
            par[PART + c * 8 + d] = part * mixing[c, d]
    for t in range(2):
        for d in range(C):
            source, mixed = (0.0, 0.0)
            for c in range(C):
                term = par[W + t * 8 + c] * par[MIX + c * 8 + d]
                source = source + term
                mixed = mixed + term * (1.0 - par[SETTLE + c])
            par[SRC + t * 8 + d] = source
            par[MIXED + t * 8 + d] = mixed
    length = gcol.shape[1]
    lane, sub = lane_of(), sub_of()
    group = (lane // 8) % 8
    rate = jnp.zeros((8, LANES), F32)
    rate_sub = jnp.zeros((8, LANES), F32)
    for c in range(C):
        rate = jnp.where(group == c, par[RATE + c], rate)
        rate_sub = jnp.where(sub == c, par[RATE + c], rate_sub)
    log_gain = decay(rate)
    coef = jnp.zeros((8, LANES), F32)
    for c in range(C):
        for d in range(C):
            coef = jnp.where((group == c) & (sub == d), par[PART + c * 8 + d], coef)
    table[0:8, :] = coef * jnp.exp(-log_gain)
    table[8:16, :] = coef * jnp.exp(-log_gain * length)
    table[16:24, :] = log_gain
    table[24:32, :] = 1.0 / (1.0 + rate)
    coef_out[0:8, :] = coef
    log_sub = decay(rate_sub)
    coef_out[8:16, :] = jnp.where(
        (group == sub) & (lane < 64),
        float(length) / (1.0 + rate_sub) * jnp.exp(-log_sub * length),
        0.0,
    )
    for c in range(C):
        rate_c = jnp.full((8, LANES), par[RATE + c], F32)
        log_c = decay(rate_c)
        for b in range(length // LANES):
            cols = slice(b * LANES, b * LANES + LANES)
            at = (lane + b * LANES).astype(F32)
            gcol[c * 8 : c * 8 + 8, cols] = jnp.exp(-log_c * (length - at))
            gdown[c * 8 : c * 8 + 8, cols] = jnp.exp(-log_c * at) / (1.0 + rate_c)


def links(par, coef, gcol, gdown, de):
    length = de.shape[1]
    d_rows, e_rows = (de[0:8, :], de[8:16, :])
    at = lax.broadcasted_iota(jnp.int32, (8, length), 1)
    d_after = jnp.where(at == length - 1, 0.0, pltpu.roll(d_rows, length - 1, 1))
    d_before = jnp.where(at == 0, 0.0, pltpu.roll(d_rows, 1, 1))
    own = e_rows * (1.0 - 4.0 * d_rows)
    own_after, own_before = (e_rows * d_after, e_rows * d_before)
    above = e_rows * pltpu.roll(d_rows, 7, 0)
    below = e_rows * pltpu.roll(d_rows, 1, 0)
    parts = [[], [], []]
    wide = lambda v: jnp.concatenate([v] * (length // LANES), axis=1)
    for c in range(C):
        rate_c = jnp.full((8, LANES), par[RATE + c], F32)
        gain_c = rate_c / (1.0 + rate_c)
        up = gcol[c * 8 : c * 8 + 8, :]
        mid = own + own_after * wide(1.0 + 1.0 / rate_c) + own_before * wide(gain_c)
        parts[0].append(mid * up)
        parts[1].append(above * up)
        parts[2].append(below * up)
    pad = jnp.zeros((64, length), F32)
    right = jnp.concatenate(parts[0] + parts[1] + parts[2] + [pad], axis=0)
    down = jnp.concatenate([gdown[d * 8 : d * 8 + 1, :] for d in range(C)], axis=0)
    dims = (((1,), (1,)), ((), ()))
    both = lax.dot_general(
        down, right, dims, precision=lax.Precision.HIGHEST, preferred_element_type=F32
    )
    return (both[:, 0:LANES] * coef[0:8, :] + coef[8:16, :], both[:, LANES:] * coef[0:8, :])


def first_kernel(
    par, obs, dif, ero, coef, gcol, gdown, de, fields, solved, send, edge, turn
):
    n_src = obs.shape[0]
    n_grp = send.shape[0]
    base = (par[WIDE] * 4.0)
    grp = par[GRP].astype(jnp.int32)
    ids = lax.broadcasted_iota(jnp.int32, (256, LANES), 0).astype(F32).astype(BF16)
    none = jnp.zeros((256, LANES), BF16)
    ones = jnp.ones((256, LANES), BF16)

    def spread(v):
        return jnp.broadcast_to(v.astype(BF16), (256, LANES))

    wide = par[WIDE].astype(jnp.int32)
    length = dif.shape[1]
    low_at, high_at = (jnp.maximum(wide - 1, 0), jnp.minimum(wide + 1, n_src - 1))
    has_low, has_high = (wide > 0, wide < n_src - 1)
    de[0:4, :] = dif[...]
    de[8:12, :] = ero[...]
    for j in range(4):
        cols = slice(512 + j * length, 512 + j * length + length)
        place = 8 * (j // 2) + j % 2
        de[place + 4 : place + 5, :] = jnp.where(has_high, obs[high_at, :, cols], 0.0)
        de[place + 6 : place + 7, :] = jnp.where(has_low, obs[low_at, :, cols], 0.0)
    left_high, left_low, right = ([], [], [])
    for n in range(n_src):
        row = obs[n, :, 0:512]
        value, xpos, layer, ypos = (
            row[:, 0:128], row[:, 128:256], row[:, 256:384], row[:, 384:512]
        )
        rel = xpos - base
        slot = jnp.where(rel < 0.0, rel + 8.0, rel)
        inside = (rel >= -2.0) & (rel <= 5.0)
        place = jnp.where(inside, layer * 8.0 + slot, -1.0)
        high = value.astype(BF16).astype(F32)
        hit = ids == spread(place)
        left_high.append(jnp.where(hit, spread(high), none))
        left_low.append(jnp.where(hit, spread(value - high), none))
        near = jnp.where(ids == spread(jnp.where(ypos < 256.0, ypos, -1.0)), ones, none)
        far = jnp.where(ids == spread(jnp.where(ypos < 256.0, -1.0, ypos - 256.0)), ones, none)
        right.append(jnp.concatenate([near, far], axis=0))
    dims = (((1,), (1,)), ((), ()))
    left = jnp.concatenate(
        [jnp.concatenate(left_high, axis=1), jnp.concatenate(left_low, axis=1)], axis=0
    )
    got = lax.dot_general(
        left, jnp.concatenate(right, axis=1), dims, preferred_element_type=F32
    )
    fields[...] = got[0:256] + got[256:512]

    lane, sub = lane_of(), sub_of()
    d_rows, e_rows = (blocks(de[0:8, :]), blocks(de[8:16, :]))
    f0, f1 = (blocks(fields[0:8, :]), blocks(fields[128:136, :]))
    bed = []
    for d in range(C):
        rate = jnp.full((8, LANES), par[RATE + d], F32)
        loss = 1.0 / (1.0 + rate)
        rows = [
            loss * e_rows[b] * (par[SRC + d] * f0[b] + par[SRC + 8 + d] * f1[b])
            for b in range(4)
        ]
        rows = sweep(rows, rate * loss)
        solved[d * 8 : d * 8 + 8, :] = jnp.concatenate(rows, axis=1)
        bed.append(rows)
    for d in range(C):
        mixed = [par[MIXED + d] * f0[b] + par[MIXED + 8 + d] * f1[b] for b in range(4)]
        for c in range(C):
            part = par[PART + c * 8 + d]
            mixed = [mixed[b] + part * bed[c][b] for b in range(4)]
        moved = stencil(mixed, d_rows, 4)
        total = jnp.zeros((8, LANES), F32)
        for b in range(4):
            fall = gdown[d * 8 : d * 8 + 8, b * LANES : b * LANES + LANES]
            total = total + fall * (bed[d][b] + e_rows[b] * moved[b])
        tile = bed[d][0]
        tile = jnp.where(lane == 1, jnp.sum(total, axis=1, keepdims=True), tile)
        m_left, m_right = (d_rows[0] * mixed[0], d_rows[3] * mixed[3])
        for at, col in (
            (2, m_left[:, 0:1]),
            (3, m_right[:, 127:128]),
            (4, d_rows[0][:, 0:1]),
            (5, d_rows[3][:, 127:128]),
            (6, e_rows[0][:, 0:1]),
            (7, e_rows[3][:, 127:128]),
        ):
            tile = jnp.where(lane == at, col, tile)
        turn[d * 8 : d * 8 + 8, :] = tile
    turn[64:128, :] = jnp.zeros((64, LANES), F32)
    sums = turn[...].T[0:8, :]
    tile0, tile1 = links(par, coef, gcol, gdown, de)
    tile1 = jnp.where(lane < 64, tile1, pltpu.roll(sums, 64, 1))
    for side, cols, rows in ((0, slice(0, 128), (0, 1)), (1, slice(384, 512), (126, 127))):
        turned = fields[:, cols].T
        turn[0:16, :] = de[:, cols]
        flux = turn[...].T
        for j in range(2):
            r = rows[j]
            edge[side, 2 * j : 2 * j + 1, :] = turned[r : r + 1, 0:128]
            edge[side, 2 * j + 1 : 2 * j + 2, :] = turned[r : r + 1, 128:256]
            edge[side, 4 + j : 5 + j, :] = flux[r : r + 1, :]
        edge[side, 6:8, :] = jnp.zeros((2, LANES), F32)
    for p in range(n_grp):
        send[p, 0:8, :] = tile0
        send[p, 8:16, :] = tile1
        send[p, 16:24, :] = jnp.where(grp + 1 == p, edge[1], edge[0])


def twice_kernel(fields, de, twice):
    d_rows = blocks(de[0:8, :])

    def step(f, carry):
        field = blocks(fields[pl.ds(pl.multiple_of(f * 8, 8), 8), :])
        field = stencil(stencil(field, d_rows, 4), d_rows, 4)
        there = pl.ds(pl.multiple_of(f * 16, 16), 16)
        twice[there, :] = jnp.concatenate(fold(field), axis=0)
        return carry

    lax.fori_loop(0, fields.shape[0] // 8, step, 0, unroll=4)


def second_kernel(
    par, recv, fields, de, solved, table, gcol, main, edge, tracer, bed_out, turn, rim, twice, store, sems
):
    n_grp = recv.shape[0] // PACK
    grp = par[GRP].astype(jnp.int32)
    shape = (n_grp, LANES)
    lane16, sub16 = lane_of(shape), sub_of(shape)
    low16 = lane16 < 64
    group = (lane16 // 8) % 8
    within = lane16 % 8
    length = float(fields.shape[1])
    log_gain = jnp.broadcast_to(table[16:17, :], shape)
    loss = jnp.broadcast_to(table[24:25, :], shape)

    def twin(v):
        return jnp.where(low16, pltpu.roll(v, 64, 1), v)

    def later(v, k):
        return jnp.where(sub16 < n_grp - k, pltpu.roll(v, n_grp - k, 0), 0.0)

    def earlier(v, k):
        return jnp.where(sub16 >= k, pltpu.roll(v, k, 0), 0.0)

    def per_device(j):
        return twin(recv[pl.ds(8 + j, n_grp, stride=PACK), :])

    def over_classes(v):
        v = v + pltpu.roll(v, 32, 1)
        v = v + pltpu.roll(v, 16, 1)
        return v + pltpu.roll(v, 8, 1)

    head1, head2, m_left, m_right, d_left, d_right, e_left, e_right = (
        per_device(j) for j in range(8)
    )
    carry = later(head1, 1)
    k = 1
    while k < n_grp:
        carry = carry + jnp.exp(-log_gain * (length * k)) * later(carry, k)
        k *= 2
    plus = jnp.where(within < 7, pltpu.roll(carry, 127, 1), pltpu.roll(carry, 7, 1))
    minus = jnp.where(within > 0, pltpu.roll(carry, 1, 1), pltpu.roll(carry, 121, 1))
    pair = jnp.where(low16, carry, plus)
    right_add, left_add = (jnp.zeros(shape, F32), jnp.zeros(shape, F32))
    for d in range(C):
        v = recv[pl.ds(d, n_grp, stride=PACK), :] * pair
        v = v + pltpu.roll(v, 64, 1)
        u = recv[pl.ds(8 + d, n_grp, stride=PACK), :] * minus
        v = v + jnp.where(low16, u, pltpu.roll(u, 64, 1))
        mine = group == d
        head2 = head2 + jnp.where(mine, over_classes(v), 0.0)
        right_add = jnp.where(mine, over_classes(carry * table[d : d + 1, :]), right_add)
        left_add = jnp.where(mine, over_classes(carry * table[8 + d : 9 + d, :]), left_add)
    head2 = head2 + e_left * loss * earlier(m_right + d_right * right_add, 1)
    end = loss * jnp.exp(-log_gain * (length - 1.0))
    head2 = head2 + e_right * end * later(m_left + d_left * left_add, 1)
    ahead = (sub16 - grp - 1).astype(F32)
    fade = jnp.exp(-log_gain * length * jnp.maximum(ahead, 0.0))
    own1 = jnp.sum(jnp.where(sub16 == grp, carry, 0.0), axis=0, keepdims=True)
    own2 = jnp.sum(jnp.where(sub16 > grp, fade * head2, 0.0), axis=0, keepdims=True)

    lane, sub = lane_of(), sub_of()
    turn[...] = jnp.zeros(turn.shape, F32)
    before = recv[pl.ds(pl.multiple_of(jnp.maximum(grp - 1, 0) * PACK + 16, 8), 8), :]
    before = jnp.where(grp > 0, before, 0.0)
    after = recv[pl.ds(pl.multiple_of(jnp.minimum(grp + 1, n_grp - 1) * PACK + 16, 8), 8), :]
    after = jnp.where(grp < n_grp - 1, after, 0.0)
    rim[...] = jnp.zeros(rim.shape, F32)
    for j in range(2):
        rim[j : j + 1, :] = before[2 + j : 3 + j, :]
        rim[2 + j : 3 + j, :] = after[j : j + 1, :]
        rim[8 + j : 9 + j, :] = before[j : j + 1, :]
        rim[10 + j : 11 + j, :] = after[2 + j : 3 + j, :]
        rim[16 + j : 17 + j, :] = edge[0, j : j + 1, :]
        rim[18 + j : 19 + j, :] = edge[1, 2 + j : 3 + j, :]
        rim[24 + j : 25 + j, :] = before[5:6, :]
        rim[26 + j : 27 + j, :] = after[4:5, :]
        rim[32 + j : 33 + j, :] = before[4:5, :]
        rim[34 + j : 35 + j, :] = after[5:6, :]
        rim[40 + j : 41 + j, :] = edge[0, 4:5, :]
        rim[42 + j : 43 + j, :] = edge[1, 5:6, :]

    def repeat(v):
        v = jnp.where(lane < 8, v, 0.0)
        for width in (8, 16, 32, 64):
            v = v + pltpu.roll(v, width, 1)
        return v

    def beside(v):
        inner = lane % 8
        up = jnp.where(inner < 7, pltpu.roll(v, 127, 1), pltpu.roll(v, 7, 1))
        return up + jnp.where(inner > 0, pltpu.roll(v, 1, 1), pltpu.roll(v, 121, 1))

    x1, x2, x0 = (rim[0:8, :], rim[8:16, :], rim[16:24, :])
    d1, d2, d0 = (repeat(rim[24:32, :]), repeat(rim[32:40, :]), repeat(rim[40:48, :]))
    m1 = d1 * x1
    inward = d0 * m1
    outer = x1 - 4.0 * m1 + beside(m1) + d2 * x2 + d0 * x0
    rim[0:8, :] = m1 - 4.0 * inward + beside(inward) + d1 * outer
    rim[8:16, :] = inward
    for j in range(2):
        cols = slice(j * 128, j * 128 + 128)
        turn[0:1, cols] = rim[j : j + 1, :]
        turn[1:2, cols] = rim[8 + j : 9 + j, :]
        turn[126:127, cols] = rim[10 + j : 11 + j, :]
        turn[127:128, cols] = rim[2 + j : 3 + j, :]
        for source, row in ((before, 126 + j), (after, j)):
            level = jnp.where(
                lane < 24, pltpu.roll(source, 16, 1), pltpu.roll(pltpu.roll(source, 7, 0), 24, 1)
            )[2 * j : 2 * j + 1, :]
            flux = source[4 + j : 5 + j, :]
            turn[row : row + 1, 256:384] = jnp.where(lane[0:1, :] < 16, flux, level)
    mend = turn[:, 0:256].T
    ends = turn[:, 256:384].T
    d_rows = blocks(de[0:8, :]) + [ends[0:8]]
    e_rows = blocks(de[8:16, :]) + [ends[8:16]]
    left_end, right_end = ((lane < 64) & (sub < 4), (lane >= 64) & (sub >= 4))
    for f in range(32):
        fix = mend[f * 8 : f * 8 + 8]
        at = f * 16
        twice[at : at + 8, :] = main[at : at + 8, :] + jnp.where(left_end, fix, 0.0)
        twice[at + 8 : at + 16, :] = main[at + 8 : at + 16, :] + jnp.where(
            right_end, pltpu.roll(fix, 4, 0), 0.0
        )

    f0 = blocks(fields[0:8, :]) + [ends[16:24]]
    f1 = blocks(fields[128:136, :]) + [ends[24:32]]
    bed = []
    for c in range(C):
        rate = jnp.full((8, LANES), par[RATE + c], F32)
        loss = 1.0 / (1.0 + rate)
        gain = rate * loss
        mine = lane == c * 8 + sub
        into = jnp.sum(jnp.where(mine, own1, 0.0), axis=1, keepdims=True)
        up = blocks(gcol[c * 8 : c * 8 + 8, :])
        rows = [v + u * into for v, u in zip(blocks(solved[c * 8 : c * 8 + 8, :]), up)]
        source = e_rows[4] * (par[SRC + c] * f0[4] + par[SRC + 8 + c] * f1[4])
        last = loss * source + gain * rows[0][:, 0:1]
        second = loss * source + gain * pltpu.roll(last, 127, 1)
        beyond = into + (into - pltpu.roll(source, 1, 1)) / rate
        rim_rows = jnp.where(lane == 127, last, jnp.where(lane == 126, second, 0.0))
        rim_rows = jnp.where(lane == 0, into, jnp.where(lane == 1, beyond, rim_rows))
        bed.append(rows + [rim_rows])
    once = [stencil(rows, d_rows, 5) for rows in bed]
    once0, once1 = (stencil(f0, d_rows, 5), stencil(f1, d_rows, 5))
    for d in range(C):
        rate = jnp.full((8, LANES), par[RATE + d], F32)
        loss = 1.0 / (1.0 + rate)
        gain = rate * loss
        moved = [par[MIXED + d] * once0[b] + par[MIXED + 8 + d] * once1[b] for b in range(5)]
        for c in range(C):
            part = par[PART + c * 8 + d]
            moved = [moved[b] + part * once[c][b] for b in range(5)]
        source = [loss * (bed[d][b] + e_rows[b] * moved[b]) for b in range(5)]
        rows = sweep(source[0:4], gain)
        mine = lane == d * 8 + sub
        into = jnp.sum(jnp.where(mine, own2, 0.0), axis=1, keepdims=True)
        up = blocks(gcol[d * 8 : d * 8 + 8, :])
        rows = [v + u * into for v, u in zip(rows, up)]
        last = source[4] + gain * rows[0][:, 0:1]
        rim_rows = jnp.where(lane == 127, last, jnp.where(lane == 0, into, 0.0))
        bed_out[d] = jnp.concatenate(rows, axis=1)[0:4, :]
        s = par[SETTLE + d]
        stirred = stencil(rows + [rim_rows], d_rows, 4)
        first = stencil(once[d], d_rows, 4)
        stirred, first = (fold(stirred), fold(first))
        keep, share, pass_on = ((1.0 - s) * (1.0 - s), 2.0 * s * (1.0 - s), s * s)
        w0, w1 = (par[W + d], par[W + 8 + d])
        for h in range(2):
            old, older = (None, None)
            for k in range(K):
                at = k * 16 + h * 8
                now = w0 * twice[at : at + 8, :] + w1 * twice[256 + at : 264 + at, :]
                if k == 0:
                    now = now + s * first[h]
                out = keep * now
                if k == 0:
                    out = out + ((1.0 - s) * s) * stirred[h]
                if k == 1:
                    out = out + pass_on * stirred[h]
                if old is not None:
                    out = out + share * old
                if older is not None:
                    out = out + pass_on * older
                store[d, k, h] = out
                old, older = (now, old)
        pltpu.make_async_copy(store.at[d], tracer.at[d], sems.at[d]).start()
    for d in range(C):
        pltpu.make_async_copy(store.at[d], tracer.at[d], sems.at[d]).wait()


VM = pl.BlockSpec(memory_space=pltpu.VMEM)
SM = pl.BlockSpec(memory_space=pltpu.SMEM)


def shape_of(*dims):
    return jax.ShapeDtypeStruct(dims, F32)


def local(
    obs_value, obs_tile, obs_cell, obs_type, obs_weights, diffusivity, erodibility,
    class_mixing, fall_table, fall_index, bedload_rate,
):
    n_wide, n_grp = (lax.axis_size("wide"), lax.axis_size("grp"))
    tile_x, tile_y = diffusivity.shape
    slots = obs_value.shape[0]
    grant = lambda size: pltpu.CompilerParams(vmem_limit_bytes=size << 20)
    place = jnp.stack([lax.axis_index("wide"), lax.axis_index("grp")]).astype(jnp.int32)
    line = lambda v: v.reshape(1, slots)
    mine = pl.pallas_call(
        pack_kernel,
        out_shape=shape_of(n_wide, 1, 4 * slots + 4 * tile_y),
        in_specs=[SM] + [VM] * 6,
        out_specs=VM,
        compiler_params=grant(2),
    )(place, line(obs_value), line(obs_tile), line(obs_cell), line(obs_type), diffusivity, erodibility)
    obs = lax.all_to_all(mine, "wide", split_axis=0, concat_axis=0, tiled=True)

    par, coef, table, gcol, gdown = pl.pallas_call(
        setup_kernel,
        out_shape=(shape_of(256), shape_of(16, LANES), shape_of(32, LANES), shape_of(64, tile_y), shape_of(64, tile_y)),
        in_specs=[SM] * 6,
        out_specs=(SM, VM, VM, VM, VM),
        cost_estimate=pl.CostEstimate(flops=10_000_000, bytes_accessed=200_000, transcendentals=40_000),
        compiler_params=grant(4),
    )(obs_weights, class_mixing, fall_table, fall_index, bedload_rate, place)

    de, fields, solved, send, edge = pl.pallas_call(
        first_kernel,
        out_shape=(shape_of(16, tile_y), shape_of(256, tile_y), shape_of(64, tile_y), shape_of(n_grp, PACK, LANES), shape_of(2, 8, LANES)),
        in_specs=[SM] + [VM] * 6,
        out_specs=(VM, VM, VM, VM, VM),
        scratch_shapes=[pltpu.VMEM((128, 128), F32)],
        compiler_params=grant(16),
    )(par, obs, diffusivity, erodibility, coef, gcol, gdown)

    recv = lax.all_to_all(send, "grp", split_axis=0, concat_axis=0, tiled=True)
    main = pl.pallas_call(
        twice_kernel,
        out_shape=shape_of(512, LANES),
        in_specs=[VM, VM],
        out_specs=VM,
        cost_estimate=pl.CostEstimate(flops=10_000_000, bytes_accessed=800_000, transcendentals=0),
        compiler_params=grant(4),
    )(fields, de)
    tracer, bed = pl.pallas_call(
        second_kernel,
        out_shape=(shape_of(C, K, 2, 8, LANES), shape_of(C, tile_x, tile_y)),
        in_specs=[SM] + [VM] * 8,
        out_specs=(pl.BlockSpec(memory_space=pl.ANY), VM),
        scratch_shapes=[
            pltpu.VMEM((128, 384), F32),
            pltpu.VMEM((48, LANES), F32),
            pltpu.VMEM((512, LANES), F32),
            pltpu.VMEM((C, K, 2, 8, LANES), F32),
            pltpu.SemaphoreType.DMA((C,)),
        ],
        compiler_params=grant(8),
    )(par, recv.reshape(n_grp * PACK, LANES), fields, de, solved, table, gcol, main, edge)
    tracer = tracer.reshape(C, K, 2, 2, tile_x, LANES).transpose(0, 1, 4, 2, 3, 5)
    return (tracer.reshape(C, K, tile_x, tile_y), bed)


def solution(mesh):
    flat = P(("wide", "grp"))
    grid = P("wide", "grp")
    in_specs = (flat, flat, flat, flat, P(), grid, grid, P(), P(), P(), P())
    out_specs = (P(None, None, "wide", "grp"), P(None, "wide", "grp"))
    return jax.shard_map(local, mesh=mesh, in_specs=in_specs, out_specs=out_specs, check_vma=False)
```

```python
import jax
import jax.numpy as jnp
from jax import lax
from jax.experimental import pallas as pl
from jax.experimental.pallas import tpu as pltpu
from jax.sharding import PartitionSpec as P

F32 = jnp.float32
BF16 = jnp.bfloat16
C = 8
K = 16
LANES = 128
PACK = 24
W, MIX, SETTLE, RATE, SRC, MIXED, PART, PLACES = 0, 16, 80, 88, 96, 112, 128, 192


def lane_of(shape=(8, LANES)):
    return lax.broadcasted_iota(jnp.int32, shape, len(shape) - 1)


def sub_of(shape=(8, LANES)):
    return lax.broadcasted_iota(jnp.int32, shape, len(shape) - 2)


def decay(rate):
    u = 1.0 / (2.0 * rate + 1.0)
    q = u * u
    return 2.0 * u * (1.0 + q * (1.0 / 3 + q * (1.0 / 5 + q * (1.0 / 7 + q / 9))))


def blocks(value):
    return [value[:, i * LANES : (i + 1) * LANES] for i in range(value.shape[1] // LANES)]


def stencil(field, diff, count):
    lane = lane_of()
    ring = len(field)
    moment = [d * v for d, v in zip(diff, field)]
    after = [pltpu.roll(m, LANES - 1, 1) for m in moment]
    before = [pltpu.roll(m, 1, 1) for m in moment]
    out = []
    for b in range(count):
        sides = pltpu.roll(moment[b], 7, 0) + pltpu.roll(moment[b], 1, 0)
        right = 0.0 if ring == 4 and b == 3 else after[(b + 1) % ring]
        left = 0.0 if ring == 4 and b == 0 else before[(b - 1) % ring]
        sides = sides + jnp.where(lane == LANES - 1, right, after[b])
        sides = sides + jnp.where(lane == 0, left, before[b])
        out.append(field[b] - 4.0 * moment[b] + sides)
    return out


def sweep(rows, gain):
    lane = lane_of()
    zero = jnp.zeros((8, LANES), F32)
    power = gain
    for step in range(7):
        width = 1 << step
        turned = [pltpu.roll(v, LANES - width, 1) for v in rows] + [zero]
        near = lane < LANES - width
        rows = [
            rows[b] + power * jnp.where(near, turned[b], turned[b + 1]) for b in range(4)
        ]
        power = power * power
    rows = [rows[b] + power * rows[b + 1] if b < 3 else rows[b] for b in range(4)]
    power = power * power
    return [rows[b] + power * rows[b + 2] if b < 2 else rows[b] for b in range(4)]


def pack_kernel(value, tile, cell, kind, dif, ero, send):
    n_wide = send.shape[0]
    length = dif.shape[1]
    wide = lax.axis_index("wide")
    sort = kind[...]
    live = sort < 2
    row = [
        jnp.where(live, value[...], 0.0),
        (tile[...] * 4 + (lax.shift_right_logical(cell[...], 9) & 3)).astype(F32),
        (jnp.where(live, sort, 0) * K + lax.shift_right_logical(cell[...], 11)).astype(F32),
        (cell[...] & 511).astype(F32),
    ]
    row = jnp.concatenate(row, axis=1)
    first = jnp.concatenate([dif[0:1], dif[1:2], ero[0:1], ero[1:2]], axis=1)
    last = jnp.concatenate([dif[2:3], dif[3:4], ero[2:3], ero[3:4]], axis=1)
    for p in range(n_wide):
        send[p] = jnp.concatenate([row, first], axis=1)

    @pl.when(wide + 1 < n_wide)
    def _():
        send[wide + 1] = jnp.concatenate([row, last], axis=1)


def fold(rows):
    low = sub_of() < 4
    return [jnp.where(low, rows[b], pltpu.roll(rows[b + 1], 4, 0)) for b in (0, 2)]


def setup_kernel(weights, mixing, falls, index, rates, tab, coef_out, table, gcol, gdown, par):
    for c in range(C):
        settle = falls[index[c]]
        par[SETTLE + c] = settle
        par[RATE + c] = rates[c]
        part = (1.0 - settle) * settle
        for t in range(2):
            par[W + t * 8 + c] = weights[t, c]
        for d in range(C):
            par[MIX + c * 8 + d] = mixing[c, d]
            par[PART + c * 8 + d] = part * mixing[c, d]
    for t in range(2):
        for d in range(C):
            source, mixed = (0.0, 0.0)
            for c in range(C):
                term = par[W + t * 8 + c] * par[MIX + c * 8 + d]
                source = source + term
                mixed = mixed + term * (1.0 - par[SETTLE + c])
            par[SRC + t * 8 + d] = source
            par[MIXED + t * 8 + d] = mixed
    for r in range(PLACES):
        tab[r : r + 1, :] = jnp.full((1, LANES), par[r], F32)
    length = gcol.shape[1]
    lane, sub = lane_of(), sub_of()
    group = (lane // 8) % 8
    rate = jnp.zeros((8, LANES), F32)
    rate_sub = jnp.zeros((8, LANES), F32)
    for c in range(C):
        rate = jnp.where(group == c, par[RATE + c], rate)
        rate_sub = jnp.where(sub == c, par[RATE + c], rate_sub)
    log_gain = decay(rate)
    coef = jnp.zeros((8, LANES), F32)
    for c in range(C):
        for d in range(C):
            coef = jnp.where((group == c) & (sub == d), par[PART + c * 8 + d], coef)
    table[0:8, :] = coef * jnp.exp(-log_gain)
    table[8:16, :] = coef * jnp.exp(-log_gain * length)
    table[16:24, :] = log_gain
    table[24:32, :] = 1.0 / (1.0 + rate)
    coef_out[0:8, :] = coef
    log_sub = decay(rate_sub)
    coef_out[8:16, :] = jnp.where(
        (group == sub) & (lane < 64),
        float(length) / (1.0 + rate_sub) * jnp.exp(-log_sub * length),
        0.0,
    )
    for c in range(C):
        rate_c = jnp.full((8, LANES), par[RATE + c], F32)
        log_c = decay(rate_c)
        for b in range(length // LANES):
            cols = slice(b * LANES, b * LANES + LANES)
            at = (lane + b * LANES).astype(F32)
            gcol[c * 8 : c * 8 + 8, cols] = jnp.exp(-log_c * (length - at))
            gdown[c * 8 : c * 8 + 8, cols] = jnp.exp(-log_c * at) / (1.0 + rate_c)


def links(par, coef, gcol, gdown, de):
    length = de.shape[1]
    d_rows, e_rows = (de[0:8, :], de[8:16, :])
    at = lax.broadcasted_iota(jnp.int32, (8, length), 1)
    d_after = jnp.where(at == length - 1, 0.0, pltpu.roll(d_rows, length - 1, 1))
    d_before = jnp.where(at == 0, 0.0, pltpu.roll(d_rows, 1, 1))
    own = e_rows * (1.0 - 4.0 * d_rows)
    own_after, own_before = (e_rows * d_after, e_rows * d_before)
    above = e_rows * pltpu.roll(d_rows, 7, 0)
    below = e_rows * pltpu.roll(d_rows, 1, 0)
    parts = [[], [], []]
    wide = lambda v: jnp.concatenate([v] * (length // LANES), axis=1)
    for c in range(C):
        rate_c = jnp.broadcast_to(par(RATE + c), (8, LANES))
        gain_c = rate_c / (1.0 + rate_c)
        up = gcol[c * 8 : c * 8 + 8, :]
        mid = own + own_after * wide(1.0 + 1.0 / rate_c) + own_before * wide(gain_c)
        parts[0].append(mid * up)
        parts[1].append(above * up)
        parts[2].append(below * up)
    pad = jnp.zeros((64, length), F32)
    right = jnp.concatenate(parts[0] + parts[1] + parts[2] + [pad], axis=0)
    down = jnp.concatenate([gdown[d * 8 : d * 8 + 1, :] for d in range(C)], axis=0)
    dims = (((1,), (1,)), ((), ()))
    down_high, right_high = (down.astype(BF16), right.astype(BF16))
    down_low = (down - down_high.astype(F32)).astype(BF16)
    right_low = (right - right_high.astype(F32)).astype(BF16)
    dot = lambda a, b: lax.dot_general(a, b, dims, preferred_element_type=F32)
    pair = dot(jnp.concatenate([down_high, down_low], axis=0), right_high)
    both = pair[0:8] + pair[8:16] + dot(down_high, right_low)
    return (both[:, 0:LANES] * coef[0:8, :] + coef[8:16, :], both[:, LANES:] * coef[0:8, :])


def first_kernel(
    tab, obs, dif, ero, coef, gcol, gdown, de, fields, solved, send, edge, turn
):
    length = dif.shape[1]
    pieces = 4 + 4 * length // LANES
    n_src = obs.shape[0] // pieces
    n_grp = send.shape[0]
    par = lambda r: tab[r : r + 1, :]
    wide, grp = (lax.axis_index("wide"), lax.axis_index("grp"))
    base = (wide * 4).astype(F32)
    ids = lax.broadcasted_iota(jnp.int32, (256, LANES), 0).astype(F32).astype(BF16)
    none = jnp.zeros((256, LANES), BF16)

    def spread(v):
        return jnp.broadcast_to(v.astype(BF16), (256, LANES))

    low_at, high_at = (jnp.maximum(wide - 1, 0), jnp.minimum(wide + 1, n_src - 1))
    has_low, has_high = (wide > 0, wide < n_src - 1)
    de[0:4, :] = dif[...]
    de[8:12, :] = ero[...]
    tiles = length // LANES
    for j in range(4):
        place = 8 * (j // 2) + j % 2
        for b in range(tiles):
            cols = slice(b * LANES, b * LANES + LANES)
            at = 4 + j * tiles + b
            above = obs[pl.ds(high_at * pieces + at, 1), :]
            below = obs[pl.ds(low_at * pieces + at, 1), :]
            de[place + 4 : place + 5, cols] = jnp.where(has_high, above, 0.0)
            de[place + 6 : place + 7, cols] = jnp.where(has_low, below, 0.0)
    value, xpos, layer, ypos = (obs[pl.ds(j, n_src, stride=pieces), :] for j in range(4))
    rel = xpos - base
    slot = jnp.where(rel < 0.0, rel + 8.0, rel)
    inside = (rel >= -2.0) & (rel <= 5.0)
    places = jnp.where(inside, layer * 8.0 + slot, -1.0)
    highs = value.astype(BF16).astype(F32)
    lows = value - highs
    front = jnp.where(ypos < 256.0, 1.0, 0.0)
    column = ypos - 256.0 * (1.0 - front)
    left_high, left_low, right = ([], [], [])
    for n in range(n_src):
        row = lambda v: spread(v[n : n + 1, :])
        hit = ids == row(places)
        left_high.append(jnp.where(hit, row(highs), none))
        left_low.append(jnp.where(hit, row(lows), none))
        meet = ids == row(column)
        near = jnp.where(meet, row(front), none)
        far = jnp.where(meet, row(1.0 - front), none)
        right.append(jnp.concatenate([near, far], axis=0))
    dims = (((1,), (1,)), ((), ()))
    left = jnp.concatenate(
        [jnp.concatenate(left_high, axis=1), jnp.concatenate(left_low, axis=1)], axis=0
    )
    got = lax.dot_general(
        left, jnp.concatenate(right, axis=1), dims, preferred_element_type=F32
    )
    fields[...] = got[0:256] + got[256:512]

    lane, sub = lane_of(), sub_of()
    d_rows, e_rows = (blocks(de[0:8, :]), blocks(de[8:16, :]))
    f0, f1 = (blocks(fields[0:8, :]), blocks(fields[128:136, :]))
    bed = []
    for d in range(C):
        rate = jnp.broadcast_to(par(RATE + d), (8, LANES))
        loss = 1.0 / (1.0 + rate)
        rows = [
            loss * e_rows[b] * (par(SRC + d) * f0[b] + par(SRC + 8 + d) * f1[b])
            for b in range(4)
        ]
        rows = sweep(rows, rate * loss)
        solved[d * 8 : d * 8 + 8, :] = jnp.concatenate(rows, axis=1)
        bed.append(rows)
    for d in range(C):
        mixed = [par(MIXED + d) * f0[b] + par(MIXED + 8 + d) * f1[b] for b in range(4)]
        for c in range(C):
            part = par(PART + c * 8 + d)
            mixed = [mixed[b] + part * bed[c][b] for b in range(4)]
        moved = stencil(mixed, d_rows, 4)
        total = jnp.zeros((8, LANES), F32)
        for b in range(4):
            fall = gdown[d * 8 : d * 8 + 8, b * LANES : b * LANES + LANES]
            total = total + fall * (bed[d][b] + e_rows[b] * moved[b])
        tile = bed[d][0]
        tile = jnp.where(lane == 1, jnp.sum(total, axis=1, keepdims=True), tile)
        m_left, m_right = (d_rows[0] * mixed[0], d_rows[3] * mixed[3])
        for at, col in (
            (2, m_left[:, 0:1]),
            (3, m_right[:, 127:128]),
            (4, d_rows[0][:, 0:1]),
            (5, d_rows[3][:, 127:128]),
            (6, e_rows[0][:, 0:1]),
            (7, e_rows[3][:, 127:128]),
        ):
            tile = jnp.where(lane == at, col, tile)
        turn[d * 8 : d * 8 + 8, :] = tile
    turn[64:128, :] = jnp.zeros((64, LANES), F32)
    sums = turn[...].T[0:8, :]
    tile0, tile1 = links(par, coef, gcol, gdown, de)
    tile1 = jnp.where(lane < 64, tile1, pltpu.roll(sums, 64, 1))
    for side, cols, rows in ((0, slice(0, 128), (0, 1)), (1, slice(384, 512), (126, 127))):
        turned = fields[:, cols].T
        turn[0:16, :] = de[:, cols]
        flux = turn[...].T
        for j in range(2):
            r = rows[j]
            edge[side, 2 * j : 2 * j + 1, :] = turned[r : r + 1, 0:128]
            edge[side, 2 * j + 1 : 2 * j + 2, :] = turned[r : r + 1, 128:256]
            edge[side, 4 + j : 5 + j, :] = flux[r : r + 1, :]
        edge[side, 6:8, :] = jnp.zeros((2, LANES), F32)
    for p in range(n_grp):
        send[p, 0:8, :] = tile0
        send[p, 8:16, :] = tile1
        send[p, 16:24, :] = jnp.where(grp + 1 == p, edge[1], edge[0])


def twice_kernel(fields, de, twice):
    d_rows = blocks(de[0:8, :])

    def step(f, carry):
        field = blocks(fields[pl.ds(pl.multiple_of(f * 8, 8), 8), :])
        field = stencil(stencil(field, d_rows, 4), d_rows, 4)
        there = pl.ds(pl.multiple_of(f * 16, 16), 16)
        twice[there, :] = jnp.concatenate(fold(field), axis=0)
        return carry

    lax.fori_loop(0, fields.shape[0] // 8, step, 0, unroll=4)


def second_kernel(
    tab, recv, fields, de, solved, table, gcol, main, edge, tracer, bed_out, turn, rim, twice, store, sems
):
    n_grp = recv.shape[0] // PACK
    par = lambda r: tab[r : r + 1, :]
    grp = lax.axis_index("grp")
    shape = (n_grp, LANES)
    lane16, sub16 = lane_of(shape), sub_of(shape)
    low16 = lane16 < 64
    group = (lane16 // 8) % 8
    within = lane16 % 8
    length = float(fields.shape[1])
    log_gain = jnp.broadcast_to(table[16:17, :], shape)
    loss = jnp.broadcast_to(table[24:25, :], shape)

    def twin(v):
        return jnp.where(low16, pltpu.roll(v, 64, 1), v)

    def later(v, k):
        return jnp.where(sub16 < n_grp - k, pltpu.roll(v, n_grp - k, 0), 0.0)

    def earlier(v, k):
        return jnp.where(sub16 >= k, pltpu.roll(v, k, 0), 0.0)

    def per_device(j):
        return twin(recv[pl.ds(8 + j, n_grp, stride=PACK), :])

    def over_classes(v):
        v = v + pltpu.roll(v, 32, 1)
        v = v + pltpu.roll(v, 16, 1)
        return v + pltpu.roll(v, 8, 1)

    head1, head2, m_left, m_right, d_left, d_right, e_left, e_right = (
        per_device(j) for j in range(8)
    )
    carry = later(head1, 1)
    k = 1
    while k < n_grp:
        carry = carry + jnp.exp(-log_gain * (length * k)) * later(carry, k)
        k *= 2
    plus = jnp.where(within < 7, pltpu.roll(carry, 127, 1), pltpu.roll(carry, 7, 1))
    minus = jnp.where(within > 0, pltpu.roll(carry, 1, 1), pltpu.roll(carry, 121, 1))
    pair = jnp.where(low16, carry, plus)
    right_add, left_add = (jnp.zeros(shape, F32), jnp.zeros(shape, F32))
    for d in range(C):
        v = recv[pl.ds(d, n_grp, stride=PACK), :] * pair
        v = v + pltpu.roll(v, 64, 1)
        u = recv[pl.ds(8 + d, n_grp, stride=PACK), :] * minus
        v = v + jnp.where(low16, u, pltpu.roll(u, 64, 1))
        mine = group == d
        head2 = head2 + jnp.where(mine, over_classes(v), 0.0)
        right_add = jnp.where(mine, over_classes(carry * table[d : d + 1, :]), right_add)
        left_add = jnp.where(mine, over_classes(carry * table[8 + d : 9 + d, :]), left_add)
    head2 = head2 + e_left * loss * earlier(m_right + d_right * right_add, 1)
    end = loss * jnp.exp(-log_gain * (length - 1.0))
    head2 = head2 + e_right * end * later(m_left + d_left * left_add, 1)
    ahead = (sub16 - grp - 1).astype(F32)
    fade = jnp.exp(-log_gain * length * jnp.maximum(ahead, 0.0))
    own1 = jnp.sum(jnp.where(sub16 == grp, carry, 0.0), axis=0, keepdims=True)
    own2 = jnp.sum(jnp.where(sub16 > grp, fade * head2, 0.0), axis=0, keepdims=True)

    lane, sub = lane_of(), sub_of()
    turn[...] = jnp.zeros(turn.shape, F32)
    before = recv[pl.ds(pl.multiple_of(jnp.maximum(grp - 1, 0) * PACK + 16, 8), 8), :]
    before = jnp.where(grp > 0, before, 0.0)
    after = recv[pl.ds(pl.multiple_of(jnp.minimum(grp + 1, n_grp - 1) * PACK + 16, 8), 8), :]
    after = jnp.where(grp < n_grp - 1, after, 0.0)
    rim[...] = jnp.zeros(rim.shape, F32)
    for j in range(2):
        rim[j : j + 1, :] = before[2 + j : 3 + j, :]
        rim[2 + j : 3 + j, :] = after[j : j + 1, :]
        rim[8 + j : 9 + j, :] = before[j : j + 1, :]
        rim[10 + j : 11 + j, :] = after[2 + j : 3 + j, :]
        rim[16 + j : 17 + j, :] = edge[0, j : j + 1, :]
        rim[18 + j : 19 + j, :] = edge[1, 2 + j : 3 + j, :]
        rim[24 + j : 25 + j, :] = before[5:6, :]
        rim[26 + j : 27 + j, :] = after[4:5, :]
        rim[32 + j : 33 + j, :] = before[4:5, :]
        rim[34 + j : 35 + j, :] = after[5:6, :]
        rim[40 + j : 41 + j, :] = edge[0, 4:5, :]
        rim[42 + j : 43 + j, :] = edge[1, 5:6, :]

    def repeat(v):
        v = jnp.where(lane < 8, v, 0.0)
        for width in (8, 16, 32, 64):
            v = v + pltpu.roll(v, width, 1)
        return v

    def beside(v):
        inner = lane % 8
        up = jnp.where(inner < 7, pltpu.roll(v, 127, 1), pltpu.roll(v, 7, 1))
        return up + jnp.where(inner > 0, pltpu.roll(v, 1, 1), pltpu.roll(v, 121, 1))

    x1, x2, x0 = (rim[0:8, :], rim[8:16, :], rim[16:24, :])
    d1, d2, d0 = (repeat(rim[24:32, :]), repeat(rim[32:40, :]), repeat(rim[40:48, :]))
    m1 = d1 * x1
    inward = d0 * m1
    outer = x1 - 4.0 * m1 + beside(m1) + d2 * x2 + d0 * x0
    rim[0:8, :] = m1 - 4.0 * inward + beside(inward) + d1 * outer
    rim[8:16, :] = inward
    for j in range(2):
        cols = slice(j * 128, j * 128 + 128)
        turn[0:1, cols] = rim[j : j + 1, :]
        turn[1:2, cols] = rim[8 + j : 9 + j, :]
        turn[126:127, cols] = rim[10 + j : 11 + j, :]
        turn[127:128, cols] = rim[2 + j : 3 + j, :]
        for source, row in ((before, 126 + j), (after, j)):
            level = jnp.where(
                lane < 24, pltpu.roll(source, 16, 1), pltpu.roll(pltpu.roll(source, 7, 0), 24, 1)
            )[2 * j : 2 * j + 1, :]
            flux = source[4 + j : 5 + j, :]
            turn[row : row + 1, 256:384] = jnp.where(lane[0:1, :] < 16, flux, level)
    mend = turn[:, 0:256].T
    ends = turn[:, 256:384].T
    d_rows = blocks(de[0:8, :]) + [ends[0:8]]
    e_rows = blocks(de[8:16, :]) + [ends[8:16]]
    left_end, right_end = ((lane < 64) & (sub < 4), (lane >= 64) & (sub >= 4))
    for f in range(32):
        fix = mend[f * 8 : f * 8 + 8]
        at = f * 16
        twice[at : at + 8, :] = main[at : at + 8, :] + jnp.where(left_end, fix, 0.0)
        twice[at + 8 : at + 16, :] = main[at + 8 : at + 16, :] + jnp.where(
            right_end, pltpu.roll(fix, 4, 0), 0.0
        )

    f0 = blocks(fields[0:8, :]) + [ends[16:24]]
    f1 = blocks(fields[128:136, :]) + [ends[24:32]]
    bed = []
    for c in range(C):
        rate = jnp.broadcast_to(par(RATE + c), (8, LANES))
        loss = 1.0 / (1.0 + rate)
        gain = rate * loss
        mine = lane == c * 8 + sub
        into = jnp.sum(jnp.where(mine, own1, 0.0), axis=1, keepdims=True)
        up = blocks(gcol[c * 8 : c * 8 + 8, :])
        rows = [v + u * into for v, u in zip(blocks(solved[c * 8 : c * 8 + 8, :]), up)]
        source = e_rows[4] * (par(SRC + c) * f0[4] + par(SRC + 8 + c) * f1[4])
        last = loss * source + gain * rows[0][:, 0:1]
        second = loss * source + gain * pltpu.roll(last, 127, 1)
        beyond = into + (into - pltpu.roll(source, 1, 1)) / rate
        rim_rows = jnp.where(lane == 127, last, jnp.where(lane == 126, second, 0.0))
        rim_rows = jnp.where(lane == 0, into, jnp.where(lane == 1, beyond, rim_rows))
        bed.append(rows + [rim_rows])
    once = [stencil(rows, d_rows, 5) for rows in bed]
    once0, once1 = (stencil(f0, d_rows, 5), stencil(f1, d_rows, 5))
    for d in range(C):
        rate = jnp.broadcast_to(par(RATE + d), (8, LANES))
        loss = 1.0 / (1.0 + rate)
        gain = rate * loss
        moved = [par(MIXED + d) * once0[b] + par(MIXED + 8 + d) * once1[b] for b in range(5)]
        for c in range(C):
            part = par(PART + c * 8 + d)
            moved = [moved[b] + part * once[c][b] for b in range(5)]
        source = [loss * (bed[d][b] + e_rows[b] * moved[b]) for b in range(5)]
        rows = sweep(source[0:4], gain)
        mine = lane == d * 8 + sub
        into = jnp.sum(jnp.where(mine, own2, 0.0), axis=1, keepdims=True)
        up = blocks(gcol[d * 8 : d * 8 + 8, :])
        rows = [v + u * into for v, u in zip(rows, up)]
        last = source[4] + gain * rows[0][:, 0:1]
        rim_rows = jnp.where(lane == 127, last, jnp.where(lane == 0, into, 0.0))
        bed_out[d] = jnp.concatenate(rows, axis=1)[0:4, :]
        s = par(SETTLE + d)
        stirred = stencil(rows + [rim_rows], d_rows, 4)
        first = stencil(once[d], d_rows, 4)
        stirred, first = (fold(stirred), fold(first))
        keep, share, pass_on = ((1.0 - s) * (1.0 - s), 2.0 * s * (1.0 - s), s * s)
        w0, w1 = (par(W + d), par(W + 8 + d))
        for h in range(2):
            old, older = (None, None)
            for k in range(K):
                at = k * 16 + h * 8
                now = w0 * twice[at : at + 8, :] + w1 * twice[256 + at : 264 + at, :]
                if k == 0:
                    now = now + s * first[h]
                out = keep * now
                if k == 0:
                    out = out + ((1.0 - s) * s) * stirred[h]
                if k == 1:
                    out = out + pass_on * stirred[h]
                if old is not None:
                    out = out + share * old
                if older is not None:
                    out = out + pass_on * older
                store[d, k, h] = out
                old, older = (now, old)
        pltpu.make_async_copy(store.at[d], tracer.at[d], sems.at[d]).start()
    for d in range(C):
        pltpu.make_async_copy(store.at[d], tracer.at[d], sems.at[d]).wait()


VM = pl.BlockSpec(memory_space=pltpu.VMEM)
SM = pl.BlockSpec(memory_space=pltpu.SMEM)


def shape_of(*dims):
    return jax.ShapeDtypeStruct(dims, F32)


def local(
    obs_value, obs_tile, obs_cell, obs_type, obs_weights, diffusivity, erodibility,
    class_mixing, fall_table, fall_index, bedload_rate,
):
    n_wide, n_grp = (lax.axis_size("wide"), lax.axis_size("grp"))
    tile_x, tile_y = diffusivity.shape
    slots = obs_value.shape[0]
    grant = lambda size: pltpu.CompilerParams(vmem_limit_bytes=size << 20)
    line = lambda v: v.reshape(1, slots)
    mine = pl.pallas_call(
        pack_kernel,
        out_shape=shape_of(n_wide, 1, 4 * slots + 4 * tile_y),
        in_specs=[VM] * 6,
        out_specs=VM,
        compiler_params=grant(62),
    )(line(obs_value), line(obs_tile), line(obs_cell), line(obs_type), diffusivity, erodibility)
    obs = lax.all_to_all(mine, "wide", split_axis=0, concat_axis=0, tiled=True)

    tab, coef, table, gcol, gdown = pl.pallas_call(
        setup_kernel,
        out_shape=(shape_of(PLACES, LANES), shape_of(16, LANES), shape_of(32, LANES), shape_of(64, tile_y), shape_of(64, tile_y)),
        in_specs=[SM] * 5,
        out_specs=(VM, VM, VM, VM, VM),
        scratch_shapes=[pltpu.SMEM((PLACES,), F32)],
        cost_estimate=pl.CostEstimate(flops=10_000_000, bytes_accessed=200_000, transcendentals=40_000),
        compiler_params=grant(4),
    )(obs_weights, class_mixing, fall_table, fall_index, bedload_rate)

    de, fields, solved, send, edge = pl.pallas_call(
        first_kernel,
        out_shape=(shape_of(16, tile_y), shape_of(256, tile_y), shape_of(64, tile_y), shape_of(n_grp, PACK, LANES), shape_of(2, 8, LANES)),
        in_specs=[VM] * 7,
        out_specs=(VM, VM, VM, VM, VM),
        scratch_shapes=[pltpu.VMEM((128, 128), F32)],
        compiler_params=grant(16),
    )(tab, obs.reshape(-1, LANES), diffusivity, erodibility, coef, gcol, gdown)

    recv = lax.all_to_all(send, "grp", split_axis=0, concat_axis=0, tiled=True)
    main = pl.pallas_call(
        twice_kernel,
        out_shape=shape_of(512, LANES),
        in_specs=[VM, VM],
        out_specs=VM,
        cost_estimate=pl.CostEstimate(flops=10_000_000, bytes_accessed=800_000, transcendentals=0),
        compiler_params=grant(4),
    )(fields, de)
    tracer, bed = pl.pallas_call(
        second_kernel,
        out_shape=(shape_of(C, K, 2, 8, LANES), shape_of(C, tile_x, tile_y)),
        in_specs=[VM] * 9,
        out_specs=(pl.BlockSpec(memory_space=pl.ANY), VM),
        scratch_shapes=[
            pltpu.VMEM((128, 384), F32),
            pltpu.VMEM((48, LANES), F32),
            pltpu.VMEM((512, LANES), F32),
            pltpu.VMEM((C, K, 2, 8, LANES), F32),
            pltpu.SemaphoreType.DMA((C,)),
        ],
        compiler_params=grant(8),
    )(tab, recv.reshape(n_grp * PACK, LANES), fields, de, solved, table, gcol, main, edge)
    tracer = tracer.reshape(C, K, 2, 2, tile_x, LANES).transpose(0, 1, 4, 2, 3, 5)
    return (tracer.reshape(C, K, tile_x, tile_y), bed)


def solution(mesh):
    flat = P(("wide", "grp"))
    grid = P("wide", "grp")
    in_specs = (flat, flat, flat, flat, P(), grid, grid, P(), P(), P(), P())
    out_specs = (P(None, None, "wide", "grp"), P(None, "wide", "grp"))
    return jax.shard_map(local, mesh=mesh, in_specs=in_specs, out_specs=out_specs, check_vma=False)
```

```python
import jax
import jax.numpy as jnp
from jax import lax
from jax.experimental import pallas as pl
from jax.experimental.pallas import tpu as pltpu
from jax.sharding import PartitionSpec as P

F32 = jnp.float32
BF16 = jnp.bfloat16
C = 8
K = 16
LANES = 128
PACK = 24
W, MIX, SETTLE, RATE, SRC, MIXED, PART, PLACES = 0, 16, 80, 88, 96, 112, 128, 192


def lane_of(shape=(8, LANES)):
    return lax.broadcasted_iota(jnp.int32, shape, len(shape) - 1)


def sub_of(shape=(8, LANES)):
    return lax.broadcasted_iota(jnp.int32, shape, len(shape) - 2)


def decay(rate):
    u = 1.0 / (2.0 * rate + 1.0)
    q = u * u
    return 2.0 * u * (1.0 + q * (1.0 / 3 + q * (1.0 / 5 + q * (1.0 / 7 + q / 9))))


def blocks(value):
    return [value[:, i * LANES : (i + 1) * LANES] for i in range(value.shape[1] // LANES)]


def stencil(field, diff, count):
    lane = lane_of()
    ring = len(field)
    moment = [d * v for d, v in zip(diff, field)]
    after = [pltpu.roll(m, LANES - 1, 1) for m in moment]
    before = [pltpu.roll(m, 1, 1) for m in moment]
    out = []
    for b in range(count):
        sides = pltpu.roll(moment[b], 7, 0) + pltpu.roll(moment[b], 1, 0)
        right = 0.0 if ring == 4 and b == 3 else after[(b + 1) % ring]
        left = 0.0 if ring == 4 and b == 0 else before[(b - 1) % ring]
        sides = sides + jnp.where(lane == LANES - 1, right, after[b])
        sides = sides + jnp.where(lane == 0, left, before[b])
        out.append(field[b] - 4.0 * moment[b] + sides)
    return out


def sweep(rows, gain):
    lane = lane_of()
    zero = jnp.zeros((8, LANES), F32)
    power = gain
    for step in range(7):
        width = 1 << step
        turned = [pltpu.roll(v, LANES - width, 1) for v in rows] + [zero]
        near = lane < LANES - width
        rows = [
            rows[b] + power * jnp.where(near, turned[b], turned[b + 1]) for b in range(4)
        ]
        power = power * power
    rows = [rows[b] + power * rows[b + 1] if b < 3 else rows[b] for b in range(4)]
    power = power * power
    return [rows[b] + power * rows[b + 2] if b < 2 else rows[b] for b in range(4)]


def pack_kernel(value, tile, cell, kind, dif, ero, send):
    n_wide = send.shape[0]
    length = dif.shape[1]
    wide = lax.axis_index("wide")
    sort = kind[...]
    live = sort < 2
    row = [
        jnp.where(live, value[...], 0.0),
        (tile[...] * 4 + (lax.shift_right_logical(cell[...], 9) & 3)).astype(F32),
        (jnp.where(live, sort, 0) * K + lax.shift_right_logical(cell[...], 11)).astype(F32),
        (cell[...] & 511).astype(F32),
    ]
    row = jnp.concatenate(row, axis=1)
    first = jnp.concatenate([dif[0:1], dif[1:2], ero[0:1], ero[1:2]], axis=1)
    last = jnp.concatenate([dif[2:3], dif[3:4], ero[2:3], ero[3:4]], axis=1)
    for p in range(n_wide):
        send[p] = jnp.concatenate([row, first], axis=1)

    @pl.when(wide + 1 < n_wide)
    def _():
        send[wide + 1] = jnp.concatenate([row, last], axis=1)


def fold(rows):
    low = sub_of() < 4
    return [jnp.where(low, rows[b], pltpu.roll(rows[b + 1], 4, 0)) for b in (0, 2)]


def setup_kernel(weights, mixing, falls, index, rates, tab, coef_out, table, chosen, blend, gcol, gdown, par):
    for c in range(C):
        settle = falls[index[c]]
        par[SETTLE + c] = settle
        par[RATE + c] = rates[c]
        part = (1.0 - settle) * settle
        for t in range(2):
            par[W + t * 8 + c] = weights[t, c]
        for d in range(C):
            par[MIX + c * 8 + d] = mixing[c, d]
            par[PART + c * 8 + d] = part * mixing[c, d]
    for t in range(2):
        for d in range(C):
            source, mixed = (0.0, 0.0)
            for c in range(C):
                term = par[W + t * 8 + c] * par[MIX + c * 8 + d]
                source = source + term
                mixed = mixed + term * (1.0 - par[SETTLE + c])
            par[SRC + t * 8 + d] = source
            par[MIXED + t * 8 + d] = mixed
    for r in range(PLACES):
        tab[r : r + 1, :] = jnp.full((1, LANES), par[r], F32)
    length = gcol.shape[1]
    lane, sub = lane_of(), sub_of()
    group = (lane // 8) % 8
    rate = jnp.zeros((8, LANES), F32)
    rate_sub = jnp.zeros((8, LANES), F32)
    for c in range(C):
        rate = jnp.where(group == c, par[RATE + c], rate)
        rate_sub = jnp.where(sub == c, par[RATE + c], rate_sub)
    log_gain = decay(rate)
    coef = jnp.zeros((8, LANES), F32)
    for c in range(C):
        for d in range(C):
            coef = jnp.where((group == c) & (sub == d), par[PART + c * 8 + d], coef)
    table[0:8, :] = log_gain
    table[8:16, :] = 1.0 / (1.0 + rate)
    at = lax.broadcasted_iota(jnp.int32, (256, LANES), 0)
    kind = at // 64
    shift = jnp.where(kind == 1, 7, jnp.where(kind == 2, 1, 0))
    meets = ((at + shift) % 8 == lane_of((256, LANES)) % 8) & (kind < 3)
    chosen[...] = jnp.where(meets, 1.0, 0.0).astype(BF16)
    coef_out[0:8, :] = coef
    log_sub = decay(rate_sub)
    coef_out[8:16, :] = jnp.where(
        (group == sub) & (lane < 64),
        float(length) / (1.0 + rate_sub) * jnp.exp(-log_sub * length),
        0.0,
    )
    for c in range(C):
        rate_c = jnp.full((8, LANES), par[RATE + c], F32)
        log_c = decay(rate_c)
        row = jnp.zeros((8, LANES), F32)
        for d in range(C):
            row = jnp.where(lane // 8 == d, par[PART + c * 8 + d], row)
        row = jnp.where(lane % 8 == sub, row, 0.0)
        blend[c * 8 : c * 8 + 8, 0:LANES] = row * jnp.exp(-log_c)
        blend[c * 8 : c * 8 + 8, LANES:] = row * jnp.exp(-log_c * length)
        for b in range(length // LANES):
            cols = slice(b * LANES, b * LANES + LANES)
            at = (lane + b * LANES).astype(F32)
            gcol[c * 8 : c * 8 + 8, cols] = jnp.exp(-log_c * (length - at))
            gdown[c * 8 : c * 8 + 8, cols] = jnp.exp(-log_c * at) / (1.0 + rate_c)


def links(par, coef, gcol, gdown, de):
    length = de.shape[1]
    d_rows, e_rows = (de[0:8, :], de[8:16, :])
    at = lax.broadcasted_iota(jnp.int32, (8, length), 1)
    d_after = jnp.where(at == length - 1, 0.0, pltpu.roll(d_rows, length - 1, 1))
    d_before = jnp.where(at == 0, 0.0, pltpu.roll(d_rows, 1, 1))
    own = e_rows * (1.0 - 4.0 * d_rows)
    own_after, own_before = (e_rows * d_after, e_rows * d_before)
    above = d_rows * pltpu.roll(e_rows, 1, 0)
    below = d_rows * pltpu.roll(e_rows, 7, 0)
    parts = [[], [], []]
    wide = lambda v: jnp.concatenate([v] * (length // LANES), axis=1)
    for c in range(C):
        rate_c = jnp.broadcast_to(par(RATE + c), (8, LANES))
        gain_c = rate_c / (1.0 + rate_c)
        up = gcol[c * 8 : c * 8 + 8, :]
        mid = own + own_after * wide(1.0 + 1.0 / rate_c) + own_before * wide(gain_c)
        parts[0].append(mid * up)
        parts[1].append(above * up)
        parts[2].append(below * up)
    pad = jnp.zeros((64, length), F32)
    right = jnp.concatenate(parts[0] + parts[1] + parts[2] + [pad], axis=0)
    down = jnp.concatenate([gdown[d * 8 : d * 8 + 1, :] for d in range(C)], axis=0)
    dims = (((1,), (1,)), ((), ()))
    down_high, right_high = (down.astype(BF16), right.astype(BF16))
    down_low = (down - down_high.astype(F32)).astype(BF16)
    right_low = (right - right_high.astype(F32)).astype(BF16)
    dot = lambda a, b: lax.dot_general(a, b, dims, preferred_element_type=F32)
    pair = dot(jnp.concatenate([down_high, down_low], axis=0), right_high)
    both = pair[0:8] + pair[8:16] + dot(down_high, right_low)
    return (both[:, 0:LANES] * coef[0:8, :] + coef[8:16, :], both[:, LANES:] * coef[0:8, :])


def first_kernel(
    tab, obs, dif, ero, coef, gcol, gdown, de, fields, solved, send, edge, turn
):
    length = dif.shape[1]
    pieces = 4 + 4 * length // LANES
    n_src = obs.shape[0] // pieces
    n_grp = send.shape[0]
    par = lambda r: tab[r : r + 1, :]
    wide, grp = (lax.axis_index("wide"), lax.axis_index("grp"))
    base = (wide * 4).astype(F32)
    ids = lax.broadcasted_iota(jnp.int32, (256, LANES), 0).astype(F32).astype(BF16)
    none = jnp.zeros((256, LANES), BF16)

    def spread(v):
        return jnp.broadcast_to(v.astype(BF16), (256, LANES))

    low_at, high_at = (jnp.maximum(wide - 1, 0), jnp.minimum(wide + 1, n_src - 1))
    has_low, has_high = (wide > 0, wide < n_src - 1)
    de[0:4, :] = dif[...]
    de[8:12, :] = ero[...]
    tiles = length // LANES
    for j in range(4):
        place = 8 * (j // 2) + j % 2
        for b in range(tiles):
            cols = slice(b * LANES, b * LANES + LANES)
            at = 4 + j * tiles + b
            above = obs[pl.ds(high_at * pieces + at, 1), :]
            below = obs[pl.ds(low_at * pieces + at, 1), :]
            de[place + 4 : place + 5, cols] = jnp.where(has_high, above, 0.0)
            de[place + 6 : place + 7, cols] = jnp.where(has_low, below, 0.0)
    value, xpos, layer, ypos = (obs[pl.ds(j, n_src, stride=pieces), :] for j in range(4))
    rel = xpos - base
    slot = jnp.where(rel < 0.0, rel + 8.0, rel)
    inside = (rel >= -2.0) & (rel <= 5.0)
    places = jnp.where(inside, layer * 8.0 + slot, -1.0)
    highs = value.astype(BF16).astype(F32)
    lows = value - highs
    front = jnp.where(ypos < 256.0, 1.0, 0.0)
    column = ypos - 256.0 * (1.0 - front)
    left_high, left_low, right = ([], [], [])
    for n in range(n_src):
        row = lambda v: spread(v[n : n + 1, :])
        hit = ids == row(places)
        left_high.append(jnp.where(hit, row(highs), none))
        left_low.append(jnp.where(hit, row(lows), none))
        meet = ids == row(column)
        near = jnp.where(meet, row(front), none)
        far = jnp.where(meet, row(1.0 - front), none)
        right.append(jnp.concatenate([near, far], axis=0))
    dims = (((1,), (1,)), ((), ()))
    left = jnp.concatenate(
        [jnp.concatenate(left_high, axis=1), jnp.concatenate(left_low, axis=1)], axis=0
    )
    got = lax.dot_general(
        left, jnp.concatenate(right, axis=1), dims, preferred_element_type=F32
    )
    fields[...] = got[0:256] + got[256:512]

    lane, sub = lane_of(), sub_of()
    d_rows, e_rows = (blocks(de[0:8, :]), blocks(de[8:16, :]))
    f0, f1 = (blocks(fields[0:8, :]), blocks(fields[128:136, :]))
    bed = []
    for d in range(C):
        rate = jnp.broadcast_to(par(RATE + d), (8, LANES))
        loss = 1.0 / (1.0 + rate)
        rows = [
            loss * e_rows[b] * (par(SRC + d) * f0[b] + par(SRC + 8 + d) * f1[b])
            for b in range(4)
        ]
        rows = sweep(rows, rate * loss)
        solved[d * 8 : d * 8 + 8, :] = jnp.concatenate(rows, axis=1)
        bed.append(rows)
    for d in range(C):
        mixed = [par(MIXED + d) * f0[b] + par(MIXED + 8 + d) * f1[b] for b in range(4)]
        for c in range(C):
            part = par(PART + c * 8 + d)
            mixed = [mixed[b] + part * bed[c][b] for b in range(4)]
        moved = stencil(mixed, d_rows, 4)
        total = jnp.zeros((8, LANES), F32)
        for b in range(4):
            fall = gdown[d * 8 : d * 8 + 8, b * LANES : b * LANES + LANES]
            total = total + fall * (bed[d][b] + e_rows[b] * moved[b])
        tile = bed[d][0]
        tile = jnp.where(lane == 1, jnp.sum(total, axis=1, keepdims=True), tile)
        m_left, m_right = (d_rows[0] * mixed[0], d_rows[3] * mixed[3])
        for at, col in (
            (2, m_left[:, 0:1]),
            (3, m_right[:, 127:128]),
            (4, d_rows[0][:, 0:1]),
            (5, d_rows[3][:, 127:128]),
            (6, e_rows[0][:, 0:1]),
            (7, e_rows[3][:, 127:128]),
        ):
            tile = jnp.where(lane == at, col, tile)
        turn[d * 8 : d * 8 + 8, :] = tile
    turn[64:128, :] = jnp.zeros((64, LANES), F32)
    sums = turn[...].T[0:8, :]
    tile0, tile1 = links(par, coef, gcol, gdown, de)
    tile1 = jnp.where(lane < 64, tile1, pltpu.roll(sums, 64, 1))
    for side, cols, rows in ((0, slice(0, 128), (0, 1)), (1, slice(384, 512), (126, 127))):
        turned = fields[:, cols].T
        turn[0:16, :] = de[:, cols]
        flux = turn[...].T
        for j in range(2):
            r = rows[j]
            edge[side, 2 * j : 2 * j + 1, :] = turned[r : r + 1, 0:128]
            edge[side, 2 * j + 1 : 2 * j + 2, :] = turned[r : r + 1, 128:256]
            edge[side, 4 + j : 5 + j, :] = flux[r : r + 1, :]
        edge[side, 6:8, :] = jnp.zeros((2, LANES), F32)
    for p in range(n_grp):
        send[p, 0:8, :] = tile0
        send[p, 8:16, :] = tile1
        send[p, 16:24, :] = jnp.where(grp + 1 == p, edge[1], edge[0])


def twice_kernel(fields, de, twice):
    d_rows = blocks(de[0:8, :])

    def step(f, carry):
        field = blocks(fields[pl.ds(pl.multiple_of(f * 8, 8), 8), :])
        field = stencil(stencil(field, d_rows, 4), d_rows, 4)
        there = pl.ds(pl.multiple_of(f * 16, 16), 16)
        twice[there, :] = jnp.concatenate(fold(field), axis=0)
        return carry

    lax.fori_loop(0, fields.shape[0] // 8, step, 0, unroll=4)


def second_kernel(
    tab, recv, fields, de, solved, table, chosen, blend, gcol, main, edge, tracer, bed_out, turn, rim, twice, store, carries, sems
):
    n_grp = recv.shape[0] // PACK
    par = lambda r: tab[r : r + 1, :]
    grp = lax.axis_index("grp")
    shape = (n_grp, LANES)
    lane16, sub16 = lane_of(shape), sub_of(shape)
    low16 = lane16 < 64
    group = lane16 // 8
    length = float(fields.shape[1])
    log_gain = jnp.broadcast_to(table[0:1, :], shape)
    loss = jnp.broadcast_to(table[8:9, :], shape)

    def later(v):
        return jnp.where(sub16 < n_grp - 1, pltpu.roll(v, n_grp - 1, 0), 0.0)

    def earlier(v):
        return jnp.where(sub16 >= 1, pltpu.roll(v, 1, 0), 0.0)

    def per_device(j):
        return pltpu.roll(recv[pl.ds(8 + j, n_grp, stride=PACK), :], 64, 1)

    def split(v):
        high = v.astype(BF16)
        return high, (v - high.astype(F32)).astype(BF16)

    dot = lambda a, b: jnp.dot(a, b, preferred_element_type=F32)
    fade_all = jnp.exp(-table[0:1, :] * length)
    into = jnp.zeros((1, LANES), F32)
    carries[n_grp - 1 : n_grp, :] = into
    for e in range(n_grp - 2, -1, -1):
        into = recv[(e + 1) * PACK + 8 : (e + 1) * PACK + 9, :] + fade_all * into
        carries[e : e + 1, :] = into
    carry = carries[...]
    turned = pltpu.roll(carry, 64, 1)
    carry = jnp.where(low16, turned, carry)
    wide_part, tall_part = ([], [])
    for d in range(C):
        wide_part.append(recv[pl.ds(d, n_grp, stride=PACK), :] * carry)
        tall = jnp.where(low16, recv[pl.ds(8 + d, n_grp, stride=PACK), :], 0.0)
        tall_part.append(tall * carry)
    terms = jnp.concatenate(
        [jnp.concatenate(wide_part, axis=0), jnp.concatenate(tall_part, axis=0)], axis=1
    )
    terms_high, terms_low = split(terms)
    linked = dot(terms_high, chosen[...]) + dot(terms_low, chosen[...])
    carry_high, carry_low = split(carry[:, 0:64])
    blend_high, blend_low = split(blend[...])
    added = dot(carry_high, blend_high) + dot(carry_low, blend_high) + dot(carry_high, blend_low)
    head2, m_left, m_right, d_left, d_right, e_left, e_right = (
        per_device(j) for j in range(1, 8)
    )
    picked = [
        jnp.where(group == d, linked[d * n_grp : (d + 1) * n_grp], 0.0) for d in range(C)
    ]
    while len(picked) > 1:
        picked = [a + b for a, b in zip(picked[0::2], picked[1::2])]
    head2 = head2 + picked[0]
    head2 = head2 + e_left * loss * earlier(m_right + d_right * added[:, 0:LANES])
    end = loss * jnp.exp(-log_gain * (length - 1.0))
    head2 = head2 + e_right * end * later(m_left + d_left * added[:, LANES:])
    ahead = (sub16 - grp - 1).astype(F32)
    fade = jnp.exp(-log_gain * length * jnp.maximum(ahead, 0.0))
    own1 = jnp.sum(jnp.where(sub16 == grp, carry, 0.0), axis=0, keepdims=True)
    own2 = jnp.sum(jnp.where(sub16 > grp, fade * head2, 0.0), axis=0, keepdims=True)

    lane, sub = lane_of(), sub_of()
    turn[...] = jnp.zeros(turn.shape, F32)
    before = recv[pl.ds(pl.multiple_of(jnp.maximum(grp - 1, 0) * PACK + 16, 8), 8), :]
    before = jnp.where(grp > 0, before, 0.0)
    after = recv[pl.ds(pl.multiple_of(jnp.minimum(grp + 1, n_grp - 1) * PACK + 16, 8), 8), :]
    after = jnp.where(grp < n_grp - 1, after, 0.0)
    rim[...] = jnp.zeros(rim.shape, F32)
    for j in range(2):
        rim[j : j + 1, :] = before[2 + j : 3 + j, :]
        rim[2 + j : 3 + j, :] = after[j : j + 1, :]
        rim[8 + j : 9 + j, :] = before[j : j + 1, :]
        rim[10 + j : 11 + j, :] = after[2 + j : 3 + j, :]
        rim[16 + j : 17 + j, :] = edge[0, j : j + 1, :]
        rim[18 + j : 19 + j, :] = edge[1, 2 + j : 3 + j, :]
        rim[24 + j : 25 + j, :] = before[5:6, :]
        rim[26 + j : 27 + j, :] = after[4:5, :]
        rim[32 + j : 33 + j, :] = before[4:5, :]
        rim[34 + j : 35 + j, :] = after[5:6, :]
        rim[40 + j : 41 + j, :] = edge[0, 4:5, :]
        rim[42 + j : 43 + j, :] = edge[1, 5:6, :]

    def repeat(v):
        v = jnp.where(lane < 8, v, 0.0)
        for width in (8, 16, 32, 64):
            v = v + pltpu.roll(v, width, 1)
        return v

    def beside(v):
        inner = lane % 8
        up = jnp.where(inner < 7, pltpu.roll(v, 127, 1), pltpu.roll(v, 7, 1))
        return up + jnp.where(inner > 0, pltpu.roll(v, 1, 1), pltpu.roll(v, 121, 1))

    x1, x2, x0 = (rim[0:8, :], rim[8:16, :], rim[16:24, :])
    d1, d2, d0 = (repeat(rim[24:32, :]), repeat(rim[32:40, :]), repeat(rim[40:48, :]))
    m1 = d1 * x1
    inward = d0 * m1
    outer = x1 - 4.0 * m1 + beside(m1) + d2 * x2 + d0 * x0
    rim[0:8, :] = m1 - 4.0 * inward + beside(inward) + d1 * outer
    rim[8:16, :] = inward
    for j in range(2):
        cols = slice(j * 128, j * 128 + 128)
        turn[0:1, cols] = rim[j : j + 1, :]
        turn[1:2, cols] = rim[8 + j : 9 + j, :]
        turn[126:127, cols] = rim[10 + j : 11 + j, :]
        turn[127:128, cols] = rim[2 + j : 3 + j, :]
        for source, row in ((before, 126 + j), (after, j)):
            level = jnp.where(
                lane < 24, pltpu.roll(source, 16, 1), pltpu.roll(pltpu.roll(source, 7, 0), 24, 1)
            )[2 * j : 2 * j + 1, :]
            flux = source[4 + j : 5 + j, :]
            turn[row : row + 1, 256:384] = jnp.where(lane[0:1, :] < 16, flux, level)
    mend = turn[:, 0:256].T
    ends = turn[:, 256:384].T
    d_rows = blocks(de[0:8, :]) + [ends[0:8]]
    e_rows = blocks(de[8:16, :]) + [ends[8:16]]
    left_end, right_end = ((lane < 64) & (sub < 4), (lane >= 64) & (sub >= 4))
    for f in range(32):
        fix = mend[f * 8 : f * 8 + 8]
        at = f * 16
        twice[at : at + 8, :] = main[at : at + 8, :] + jnp.where(left_end, fix, 0.0)
        twice[at + 8 : at + 16, :] = main[at + 8 : at + 16, :] + jnp.where(
            right_end, pltpu.roll(fix, 4, 0), 0.0
        )

    f0 = blocks(fields[0:8, :]) + [ends[16:24]]
    f1 = blocks(fields[128:136, :]) + [ends[24:32]]
    bed = []
    for c in range(C):
        rate = jnp.broadcast_to(par(RATE + c), (8, LANES))
        loss = 1.0 / (1.0 + rate)
        gain = rate * loss
        mine = lane == c * 8 + sub
        into = jnp.sum(jnp.where(mine, own1, 0.0), axis=1, keepdims=True)
        up = blocks(gcol[c * 8 : c * 8 + 8, :])
        rows = [v + u * into for v, u in zip(blocks(solved[c * 8 : c * 8 + 8, :]), up)]
        source = e_rows[4] * (par(SRC + c) * f0[4] + par(SRC + 8 + c) * f1[4])
        last = loss * source + gain * rows[0][:, 0:1]
        second = loss * source + gain * pltpu.roll(last, 127, 1)
        beyond = into + (into - pltpu.roll(source, 1, 1)) / rate
        rim_rows = jnp.where(lane == 127, last, jnp.where(lane == 126, second, 0.0))
        rim_rows = jnp.where(lane == 0, into, jnp.where(lane == 1, beyond, rim_rows))
        bed.append(rows + [rim_rows])
    once = [stencil(rows, d_rows, 5) for rows in bed]
    once0, once1 = (stencil(f0, d_rows, 5), stencil(f1, d_rows, 5))
    for d in range(C):
        rate = jnp.broadcast_to(par(RATE + d), (8, LANES))
        loss = 1.0 / (1.0 + rate)
        gain = rate * loss
        moved = [par(MIXED + d) * once0[b] + par(MIXED + 8 + d) * once1[b] for b in range(5)]
        for c in range(C):
            part = par(PART + c * 8 + d)
            moved = [moved[b] + part * once[c][b] for b in range(5)]
        source = [loss * (bed[d][b] + e_rows[b] * moved[b]) for b in range(5)]
        rows = sweep(source[0:4], gain)
        mine = lane == d * 8 + sub
        into = jnp.sum(jnp.where(mine, own2, 0.0), axis=1, keepdims=True)
        up = blocks(gcol[d * 8 : d * 8 + 8, :])
        rows = [v + u * into for v, u in zip(rows, up)]
        last = source[4] + gain * rows[0][:, 0:1]
        rim_rows = jnp.where(lane == 127, last, jnp.where(lane == 0, into, 0.0))
        bed_out[d] = jnp.concatenate(rows, axis=1)[0:4, :]
        s = par(SETTLE + d)
        stirred = stencil(rows + [rim_rows], d_rows, 4)
        first = stencil(once[d], d_rows, 4)
        stirred, first = (fold(stirred), fold(first))
        keep, share, pass_on = ((1.0 - s) * (1.0 - s), 2.0 * s * (1.0 - s), s * s)
        w0, w1 = (par(W + d), par(W + 8 + d))
        for h in range(2):
            old, older = (None, None)
            for k in range(K):
                at = k * 16 + h * 8
                now = w0 * twice[at : at + 8, :] + w1 * twice[256 + at : 264 + at, :]
                if k == 0:
                    now = now + s * first[h]
                out = keep * now
                if k == 0:
                    out = out + ((1.0 - s) * s) * stirred[h]
                if k == 1:
                    out = out + pass_on * stirred[h]
                if old is not None:
                    out = out + share * old
                if older is not None:
                    out = out + pass_on * older
                store[d, k, h] = out
                old, older = (now, old)
        pltpu.make_async_copy(store.at[d], tracer.at[d], sems.at[d]).start()
    for d in range(C):
        pltpu.make_async_copy(store.at[d], tracer.at[d], sems.at[d]).wait()


VM = pl.BlockSpec(memory_space=pltpu.VMEM)
SM = pl.BlockSpec(memory_space=pltpu.SMEM)


def shape_of(*dims):
    return jax.ShapeDtypeStruct(dims, F32)


def local(
    obs_value, obs_tile, obs_cell, obs_type, obs_weights, diffusivity, erodibility,
    class_mixing, fall_table, fall_index, bedload_rate,
):
    n_wide, n_grp = (lax.axis_size("wide"), lax.axis_size("grp"))
    tile_x, tile_y = diffusivity.shape
    slots = obs_value.shape[0]
    grant = lambda size: pltpu.CompilerParams(vmem_limit_bytes=size << 20)
    line = lambda v: v.reshape(1, slots)
    mine = pl.pallas_call(
        pack_kernel,
        out_shape=shape_of(n_wide, 1, 4 * slots + 4 * tile_y),
        in_specs=[VM] * 6,
        out_specs=VM,
        compiler_params=grant(62),
    )(line(obs_value), line(obs_tile), line(obs_cell), line(obs_type), diffusivity, erodibility)
    obs = lax.all_to_all(mine, "wide", split_axis=0, concat_axis=0, tiled=True)

    tab, coef, table, chosen, blend, gcol, gdown = pl.pallas_call(
        setup_kernel,
        out_shape=(shape_of(PLACES, LANES), shape_of(16, LANES), shape_of(16, LANES), jax.ShapeDtypeStruct((256, LANES), BF16), shape_of(64, 256), shape_of(64, tile_y), shape_of(64, tile_y)),
        in_specs=[SM] * 5,
        out_specs=(VM,) * 7,
        scratch_shapes=[pltpu.SMEM((PLACES,), F32)],
        cost_estimate=pl.CostEstimate(flops=10_000_000, bytes_accessed=200_000, transcendentals=40_000),
        compiler_params=grant(4),
    )(obs_weights, class_mixing, fall_table, fall_index, bedload_rate)

    de, fields, solved, send, edge = pl.pallas_call(
        first_kernel,
        out_shape=(shape_of(16, tile_y), shape_of(256, tile_y), shape_of(64, tile_y), shape_of(n_grp, PACK, LANES), shape_of(2, 8, LANES)),
        in_specs=[VM] * 7,
        out_specs=(VM, VM, VM, VM, VM),
        scratch_shapes=[pltpu.VMEM((128, 128), F32)],
        compiler_params=grant(16),
    )(tab, obs.reshape(-1, LANES), diffusivity, erodibility, coef, gcol, gdown)

    recv = lax.all_to_all(send, "grp", split_axis=0, concat_axis=0, tiled=True)
    main = pl.pallas_call(
        twice_kernel,
        out_shape=shape_of(512, LANES),
        in_specs=[VM, VM],
        out_specs=VM,
        cost_estimate=pl.CostEstimate(flops=10_000_000, bytes_accessed=800_000, transcendentals=0),
        compiler_params=grant(4),
    )(fields, de)
    tracer, bed = pl.pallas_call(
        second_kernel,
        out_shape=(shape_of(C, K, 2, 8, LANES), shape_of(C, tile_x, tile_y)),
        in_specs=[VM] * 11,
        out_specs=(pl.BlockSpec(memory_space=pl.ANY), VM),
        scratch_shapes=[
            pltpu.VMEM((128, 384), F32),
            pltpu.VMEM((48, LANES), F32),
            pltpu.VMEM((512, LANES), F32),
            pltpu.VMEM((C, K, 2, 8, LANES), F32),
            pltpu.VMEM((n_grp, LANES), F32),
            pltpu.SemaphoreType.DMA((C,)),
        ],
        compiler_params=grant(8),
    )(tab, recv.reshape(n_grp * PACK, LANES), fields, de, solved, table, chosen, blend, gcol, main, edge)
    tracer = tracer.reshape(C, K, 2, 2, tile_x, LANES).transpose(0, 1, 4, 2, 3, 5)
    return (tracer.reshape(C, K, tile_x, tile_y), bed)


def solution(mesh):
    flat = P(("wide", "grp"))
    grid = P("wide", "grp")
    in_specs = (flat, flat, flat, flat, P(), grid, grid, P(), P(), P(), P())
    out_specs = (P(None, None, "wide", "grp"), P(None, "wide", "grp"))
    return jax.shard_map(local, mesh=mesh, in_specs=in_specs, out_specs=out_specs, check_vma=False)
```

```python
import jax
import jax.numpy as jnp
from jax import lax
from jax.experimental import pallas as pl
from jax.experimental.pallas import tpu as pltpu
from jax.sharding import PartitionSpec as P

F32 = jnp.float32
BF16 = jnp.bfloat16
C = 8
K = 16
LANES = 128
PACK = 24
W, MIX, SETTLE, RATE, SRC, MIXED, PART, PLACES = 0, 16, 80, 88, 96, 112, 128, 192


def lane_of(shape=(8, LANES)):
    return lax.broadcasted_iota(jnp.int32, shape, len(shape) - 1)


def sub_of(shape=(8, LANES)):
    return lax.broadcasted_iota(jnp.int32, shape, len(shape) - 2)


def decay(rate):
    u = 1.0 / (2.0 * rate + 1.0)
    q = u * u
    return 2.0 * u * (1.0 + q * (1.0 / 3 + q * (1.0 / 5 + q * (1.0 / 7 + q / 9))))


def blocks(value):
    return [value[:, i * LANES : (i + 1) * LANES] for i in range(value.shape[1] // LANES)]


def stencil(field, diff, count):
    lane = lane_of()
    ring = len(field)
    moment = [d * v for d, v in zip(diff, field)]
    after = [pltpu.roll(m, LANES - 1, 1) for m in moment]
    before = [pltpu.roll(m, 1, 1) for m in moment]
    out = []
    for b in range(count):
        sides = pltpu.roll(moment[b], 7, 0) + pltpu.roll(moment[b], 1, 0)
        right = 0.0 if ring == 4 and b == 3 else after[(b + 1) % ring]
        left = 0.0 if ring == 4 and b == 0 else before[(b - 1) % ring]
        sides = sides + jnp.where(lane == LANES - 1, right, after[b])
        sides = sides + jnp.where(lane == 0, left, before[b])
        out.append(field[b] - 4.0 * moment[b] + sides)
    return out


def sweep(rows, gain):
    lane = lane_of()
    zero = jnp.zeros((8, LANES), F32)
    power = gain
    for step in range(7):
        width = 1 << step
        turned = [pltpu.roll(v, LANES - width, 1) for v in rows] + [zero]
        near = lane < LANES - width
        rows = [
            rows[b] + power * jnp.where(near, turned[b], turned[b + 1]) for b in range(4)
        ]
        power = power * power
    rows = [rows[b] + power * rows[b + 1] if b < 3 else rows[b] for b in range(4)]
    power = power * power
    return [rows[b] + power * rows[b + 2] if b < 2 else rows[b] for b in range(4)]


def pack_kernel(value, tile, cell, kind, dif, ero, send):
    n_wide = send.shape[0]
    length = dif.shape[1]
    wide = lax.axis_index("wide")
    sort = kind[...]
    live = sort < 2
    row = [
        jnp.where(live, value[...], 0.0),
        (tile[...] * 4 + (lax.shift_right_logical(cell[...], 9) & 3)).astype(F32),
        (jnp.where(live, sort, 0) * K + lax.shift_right_logical(cell[...], 11)).astype(F32),
        (cell[...] & 511).astype(F32),
    ]
    row = jnp.concatenate(row, axis=1)
    first = jnp.concatenate([dif[0:1], dif[1:2], ero[0:1], ero[1:2]], axis=1)
    last = jnp.concatenate([dif[2:3], dif[3:4], ero[2:3], ero[3:4]], axis=1)
    for p in range(n_wide):
        send[p] = jnp.concatenate([row, first], axis=1)

    @pl.when(wide + 1 < n_wide)
    def _():
        send[wide + 1] = jnp.concatenate([row, last], axis=1)


def fold(rows):
    low = sub_of() < 4
    return [jnp.where(low, rows[b], pltpu.roll(rows[b + 1], 4, 0)) for b in (0, 2)]


def setup_kernel(weights, mixing, falls, index, rates, tab, coef_out, table, chosen, blend, gcol, gdown, par):
    for c in range(C):
        settle = falls[index[c]]
        par[SETTLE + c] = settle
        par[RATE + c] = rates[c]
        part = (1.0 - settle) * settle
        for t in range(2):
            par[W + t * 8 + c] = weights[t, c]
        for d in range(C):
            par[MIX + c * 8 + d] = mixing[c, d]
            par[PART + c * 8 + d] = part * mixing[c, d]
    for t in range(2):
        for d in range(C):
            source, mixed = (0.0, 0.0)
            for c in range(C):
                term = par[W + t * 8 + c] * par[MIX + c * 8 + d]
                source = source + term
                mixed = mixed + term * (1.0 - par[SETTLE + c])
            par[SRC + t * 8 + d] = source
            par[MIXED + t * 8 + d] = mixed
    for r in range(PLACES):
        tab[r : r + 1, :] = jnp.full((1, LANES), par[r], F32)
    length = gcol.shape[1]
    lane, sub = lane_of(), sub_of()
    group = (lane // 8) % 8
    rate = jnp.zeros((8, LANES), F32)
    rate_sub = jnp.zeros((8, LANES), F32)
    for c in range(C):
        rate = jnp.where(group == c, par[RATE + c], rate)
        rate_sub = jnp.where(sub == c, par[RATE + c], rate_sub)
    log_gain = decay(rate)
    coef = jnp.zeros((8, LANES), F32)
    for c in range(C):
        for d in range(C):
            coef = jnp.where((group == c) & (sub == d), par[PART + c * 8 + d], coef)
    table[0:8, :] = log_gain
    table[8:16, :] = 1.0 / (1.0 + rate)
    at = lax.broadcasted_iota(jnp.int32, (256, LANES), 0)
    kind = at // 64
    shift = jnp.where(kind == 1, 7, jnp.where(kind == 2, 1, 0))
    meets = ((at + shift) % 8 == lane_of((256, LANES)) % 8) & (kind < 3)
    chosen[...] = jnp.where(meets, 1.0, 0.0).astype(BF16)
    coef_out[0:8, :] = coef
    log_sub = decay(rate_sub)
    coef_out[8:16, :] = jnp.where(
        (group == sub) & (lane < 64),
        float(length) / (1.0 + rate_sub) * jnp.exp(-log_sub * length),
        0.0,
    )
    for c in range(C):
        rate_c = jnp.full((8, LANES), par[RATE + c], F32)
        log_c = decay(rate_c)
        row = jnp.zeros((8, LANES), F32)
        for d in range(C):
            row = jnp.where(lane // 8 == d, par[PART + c * 8 + d], row)
        row = jnp.where(lane % 8 == sub, row, 0.0)
        blend[c * 8 : c * 8 + 8, 0:LANES] = row * jnp.exp(-log_c)
        blend[c * 8 : c * 8 + 8, LANES:] = row * jnp.exp(-log_c * length)
        for b in range(length // LANES):
            cols = slice(b * LANES, b * LANES + LANES)
            at = (lane + b * LANES).astype(F32)
            gcol[c * 8 : c * 8 + 8, cols] = jnp.exp(-log_c * (length - at))
            gdown[c * 8 : c * 8 + 8, cols] = jnp.exp(-log_c * at) / (1.0 + rate_c)


def links(par, coef, gcol, gdown, de):
    length = de.shape[1]
    d_rows, e_rows = (de[0:8, :], de[8:16, :])
    at = lax.broadcasted_iota(jnp.int32, (8, length), 1)
    d_after = jnp.where(at == length - 1, 0.0, pltpu.roll(d_rows, length - 1, 1))
    d_before = jnp.where(at == 0, 0.0, pltpu.roll(d_rows, 1, 1))
    own = e_rows * (1.0 - 4.0 * d_rows)
    own_after, own_before = (e_rows * d_after, e_rows * d_before)
    above = d_rows * pltpu.roll(e_rows, 1, 0)
    below = d_rows * pltpu.roll(e_rows, 7, 0)
    parts = [[], [], []]
    wide = lambda v: jnp.concatenate([v] * (length // LANES), axis=1)
    for c in range(C):
        rate_c = jnp.broadcast_to(par(RATE + c), (8, LANES))
        gain_c = rate_c / (1.0 + rate_c)
        up = gcol[c * 8 : c * 8 + 8, :]
        mid = own + own_after * wide(1.0 + 1.0 / rate_c) + own_before * wide(gain_c)
        parts[0].append(mid * up)
        parts[1].append(above * up)
        parts[2].append(below * up)
    pad = jnp.zeros((64, length), F32)
    right = jnp.concatenate(parts[0] + parts[1] + parts[2] + [pad], axis=0)
    down = jnp.concatenate([gdown[d * 8 : d * 8 + 1, :] for d in range(C)], axis=0)
    dims = (((1,), (1,)), ((), ()))
    down_high, right_high = (down.astype(BF16), right.astype(BF16))
    down_low = (down - down_high.astype(F32)).astype(BF16)
    right_low = (right - right_high.astype(F32)).astype(BF16)
    dot = lambda a, b: lax.dot_general(a, b, dims, preferred_element_type=F32)
    pair = dot(jnp.concatenate([down_high, down_low], axis=0), right_high)
    both = pair[0:8] + pair[8:16] + dot(down_high, right_low)
    return (both[:, 0:LANES] * coef[0:8, :] + coef[8:16, :], both[:, LANES:] * coef[0:8, :])


def arrange(obs, length, wide):
    pieces = 4 + 4 * length // LANES
    n_src = obs.shape[0] // pieces
    value, xpos, layer, ypos = (obs[pl.ds(j, n_src, stride=pieces), :] for j in range(4))
    rel = xpos - (wide * 4).astype(F32)
    slot = jnp.where(rel < 0.0, rel + 8.0, rel)
    inside = (rel >= -2.0) & (rel <= 5.0)
    places = jnp.where(inside, layer * 8.0 + slot, -1.0)
    ground = jnp.where(inside & (layer == 0.0), slot, -1.0)
    ground = jnp.where(inside & (layer == float(K)), slot + 8.0, ground)
    high = value.astype(BF16).astype(F32)
    return n_src, high, value - high, places, ground, ypos, jnp.where(inside, slot, -99.0), layer


def spread(rows, n, count=256):
    return jnp.broadcast_to(rows[n : n + 1, :].astype(BF16), (count, LANES))


def numbers(count):
    return lax.broadcasted_iota(jnp.int32, (count, LANES), 0).astype(F32).astype(BF16)


def columns_of(ypos, n_src):
    ids, none = (numbers(256), jnp.zeros((256, LANES), BF16))
    front = jnp.where(ypos < 256.0, 1.0, 0.0)
    back = 1.0 - front
    column = ypos - 256.0 * back
    right = []
    for n in range(n_src):
        meet = ids == spread(column, n)
        near = jnp.where(meet, spread(front, n), none)
        far = jnp.where(meet, spread(back, n), none)
        right.append(jnp.concatenate([near, far], axis=0))
    return jnp.concatenate(right, axis=1)


def contract(left, right):
    dims = (((1,), (1,)), ((), ()))
    return lax.dot_general(left, right, dims, preferred_element_type=F32)


def first_kernel(
    tab, obs, dif, ero, coef, gcol, gdown, de, ground_out, solved, send, edge, turn
):
    length = dif.shape[1]
    pieces = 4 + 4 * length // LANES
    n_src = obs.shape[0] // pieces
    n_grp = send.shape[0]
    par = lambda r: tab[r : r + 1, :]
    wide, grp = (lax.axis_index("wide"), lax.axis_index("grp"))
    low_at, high_at = (jnp.maximum(wide - 1, 0), jnp.minimum(wide + 1, n_src - 1))
    has_low, has_high = (wide > 0, wide < n_src - 1)
    de[0:4, :] = dif[...]
    de[8:12, :] = ero[...]
    tiles = length // LANES
    for j in range(4):
        place = 8 * (j // 2) + j % 2
        for b in range(tiles):
            cols = slice(b * LANES, b * LANES + LANES)
            at = 4 + j * tiles + b
            above = obs[pl.ds(high_at * pieces + at, 1), :]
            below = obs[pl.ds(low_at * pieces + at, 1), :]
            de[place + 4 : place + 5, cols] = jnp.where(has_high, above, 0.0)
            de[place + 6 : place + 7, cols] = jnp.where(has_low, below, 0.0)
    n_src, high, low, _, ground, ypos, slot, layer = arrange(obs, length, wide)
    block = jnp.zeros(ypos.shape, F32)
    for edge_at in (128.0, 256.0, 384.0):
        block = block + jnp.where(ypos >= edge_at, 1.0, 0.0)
    lane_code = jnp.where(ground >= 0.0, block * 16.0 + ground, -1.0)
    along = ypos - 128.0 * block
    code = jnp.where(ypos < 2.0, ypos, jnp.where(ypos >= length - 2.0, ypos - (length - 4.0), -99.0))
    end_code = code * 8.0 + slot
    end_code = jnp.where((code >= 0.0) & (slot >= 0.0), end_code, -1.0)
    parts = [[] for _ in range(6)]
    value_or_none = lambda hit, rows, n: jnp.where(
        hit, spread(rows, n, hit.shape[0]), jnp.zeros(hit.shape, BF16)
    )
    one_or_none = lambda hit: jnp.where(
        hit, jnp.ones(hit.shape, BF16), jnp.zeros(hit.shape, BF16)
    )
    ids32, ids64, ids128 = (numbers(32), numbers(64), numbers(128))
    for n in range(n_src):
        hit = ids64 == spread(lane_code, n, 64)
        parts[0].append(value_or_none(hit, high, n))
        parts[1].append(value_or_none(hit, low, n))
        parts[2].append(one_or_none(ids128 == spread(along, n, 128)))
        hit = ids32 == spread(end_code, n, 32)
        parts[3].append(value_or_none(hit, high, n))
        parts[4].append(value_or_none(hit, low, n))
        parts[5].append(one_or_none(ids32 == spread(layer, n, 32)))
    parts = [jnp.concatenate(part, axis=1) for part in parts]
    level = contract(jnp.concatenate(parts[0:2], axis=0), parts[2])
    level = level[0:64] + level[64:128]
    ground_out[...] = level
    ends = contract(jnp.concatenate(parts[3:5], axis=0), parts[5])
    ends = ends[0:32] + ends[32:64]
    grow = lax.broadcasted_iota(jnp.int32, (32, 256), 1)
    here = lax.broadcasted_iota(jnp.int32, (32, 256), 0)
    spot = jnp.where(grow // 8 == here, 1.0, 0.0).astype(BF16)
    ends_high = ends.astype(BF16)
    ends_low = (ends - ends_high.astype(F32)).astype(BF16)
    grown = jnp.dot(ends_high, spot, preferred_element_type=F32)
    grown = grown + jnp.dot(ends_low, spot, preferred_element_type=F32)
    grown = jnp.where(grow % 8 == here % 8, grown, 0.0)
    rims = [jnp.sum(grown[q * 8 : q * 8 + 8], axis=0, keepdims=True) for q in range(4)]
    lane, sub = lane_of(), sub_of()
    d_rows, e_rows = (blocks(de[0:8, :]), blocks(de[8:16, :]))
    f0, f1 = ([level[t + b * 16 : t + b * 16 + 8] for b in range(4)] for t in (0, 8))
    bed = []
    for d in range(C):
        rate = jnp.broadcast_to(par(RATE + d), (8, LANES))
        loss = 1.0 / (1.0 + rate)
        rows = [
            loss * e_rows[b] * (par(SRC + d) * f0[b] + par(SRC + 8 + d) * f1[b])
            for b in range(4)
        ]
        rows = sweep(rows, rate * loss)
        solved[d * 8 : d * 8 + 8, :] = jnp.concatenate(rows, axis=1)
        bed.append(rows)
    for d in range(C):
        mixed = [par(MIXED + d) * f0[b] + par(MIXED + 8 + d) * f1[b] for b in range(4)]
        for c in range(C):
            part = par(PART + c * 8 + d)
            mixed = [mixed[b] + part * bed[c][b] for b in range(4)]
        moved = stencil(mixed, d_rows, 4)
        total = jnp.zeros((8, LANES), F32)
        for b in range(4):
            fall = gdown[d * 8 : d * 8 + 8, b * LANES : b * LANES + LANES]
            total = total + fall * (bed[d][b] + e_rows[b] * moved[b])
        tile = bed[d][0]
        tile = jnp.where(lane == 1, jnp.sum(total, axis=1, keepdims=True), tile)
        m_left, m_right = (d_rows[0] * mixed[0], d_rows[3] * mixed[3])
        for at, col in (
            (2, m_left[:, 0:1]),
            (3, m_right[:, 127:128]),
            (4, d_rows[0][:, 0:1]),
            (5, d_rows[3][:, 127:128]),
            (6, e_rows[0][:, 0:1]),
            (7, e_rows[3][:, 127:128]),
        ):
            tile = jnp.where(lane == at, col, tile)
        turn[d * 8 : d * 8 + 8, :] = tile
    turn[64:128, :] = jnp.zeros((64, LANES), F32)
    sums = turn[...].T[0:8, :]
    tile0, tile1 = links(par, coef, gcol, gdown, de)
    tile1 = jnp.where(lane < 64, tile1, pltpu.roll(sums, 64, 1))
    for side, cols, rows in ((0, slice(0, 128), (0, 1)), (1, slice(384, 512), (126, 127))):
        turn[0:16, :] = de[:, cols]
        flux = turn[...].T
        for j in range(2):
            r = rows[j]
            q = 2 * side + j
            edge[side, 2 * j : 2 * j + 1, :] = rims[q][:, 0:128]
            edge[side, 2 * j + 1 : 2 * j + 2, :] = rims[q][:, 128:256]
            edge[side, 4 + j : 5 + j, :] = flux[r : r + 1, :]
        edge[side, 6:8, :] = jnp.zeros((2, LANES), F32)
    for p in range(n_grp):
        send[p, 0:8, :] = tile0
        send[p, 8:16, :] = tile1
        send[p, 16:24, :] = jnp.where(grp + 1 == p, edge[1], edge[0])


def twice_kernel(obs, de, twice, fields):
    d_rows = blocks(de[0:8, :])
    wide = lax.axis_index("wide")
    n_src, high, low, places, _, ypos, _, _ = arrange(obs, de.shape[1], wide)
    ids, none = (numbers(256), jnp.zeros((256, LANES), BF16))
    first, second = ([], [])
    for n in range(n_src):
        hit = ids == spread(places, n)
        first.append(jnp.where(hit, spread(high, n), none))
        second.append(jnp.where(hit, spread(low, n), none))
    left = [jnp.concatenate(parts, axis=1) for parts in (first, second)]
    got = contract(jnp.concatenate(left, axis=0), columns_of(ypos, n_src))
    fields[...] = got[0:256] + got[256:512]

    def step(f, carry):
        field = blocks(fields[pl.ds(pl.multiple_of(f * 8, 8), 8), :])
        field = stencil(stencil(field, d_rows, 4), d_rows, 4)
        there = pl.ds(pl.multiple_of(f * 16, 16), 16)
        twice[there, :] = jnp.concatenate(fold(field), axis=0)
        return carry

    lax.fori_loop(0, fields.shape[0] // 8, step, 0, unroll=4)


def second_kernel(
    tab, recv, fields, de, solved, table, chosen, blend, gcol, main, edge, tracer, bed_out, turn, rim, twice, store, carries, sems
):
    n_grp = recv.shape[0] // PACK
    par = lambda r: tab[r : r + 1, :]
    grp = lax.axis_index("grp")
    shape = (n_grp, LANES)
    lane16, sub16 = lane_of(shape), sub_of(shape)
    low16 = lane16 < 64
    group = lane16 // 8
    length = float(de.shape[1])
    log_gain = jnp.broadcast_to(table[0:1, :], shape)
    loss = jnp.broadcast_to(table[8:9, :], shape)

    def later(v):
        return jnp.where(sub16 < n_grp - 1, pltpu.roll(v, n_grp - 1, 0), 0.0)

    def earlier(v):
        return jnp.where(sub16 >= 1, pltpu.roll(v, 1, 0), 0.0)

    def per_device(j):
        return pltpu.roll(recv[pl.ds(8 + j, n_grp, stride=PACK), :], 64, 1)

    def split(v):
        high = v.astype(BF16)
        return high, (v - high.astype(F32)).astype(BF16)

    dot = lambda a, b: jnp.dot(a, b, preferred_element_type=F32)
    fade_all = jnp.exp(-table[0:1, :] * length)
    into = jnp.zeros((1, LANES), F32)
    carries[n_grp - 1 : n_grp, :] = into
    for e in range(n_grp - 2, -1, -1):
        into = recv[(e + 1) * PACK + 8 : (e + 1) * PACK + 9, :] + fade_all * into
        carries[e : e + 1, :] = into
    carry = carries[...]
    turned = pltpu.roll(carry, 64, 1)
    carry = jnp.where(low16, turned, carry)
    wide_part, tall_part = ([], [])
    for d in range(C):
        wide_part.append(recv[pl.ds(d, n_grp, stride=PACK), :] * carry)
        tall = jnp.where(low16, recv[pl.ds(8 + d, n_grp, stride=PACK), :], 0.0)
        tall_part.append(tall * carry)
    terms = jnp.concatenate(
        [jnp.concatenate(wide_part, axis=0), jnp.concatenate(tall_part, axis=0)], axis=1
    )
    terms_high, terms_low = split(terms)
    linked = dot(terms_high, chosen[...]) + dot(terms_low, chosen[...])
    carry_high, carry_low = split(carry[:, 0:64])
    blend_high, blend_low = split(blend[...])
    added = dot(carry_high, blend_high) + dot(carry_low, blend_high) + dot(carry_high, blend_low)
    head2, m_left, m_right, d_left, d_right, e_left, e_right = (
        per_device(j) for j in range(1, 8)
    )
    picked = [
        jnp.where(group == d, linked[d * n_grp : (d + 1) * n_grp], 0.0) for d in range(C)
    ]
    while len(picked) > 1:
        picked = [a + b for a, b in zip(picked[0::2], picked[1::2])]
    head2 = head2 + picked[0]
    head2 = head2 + e_left * loss * earlier(m_right + d_right * added[:, 0:LANES])
    end = loss * jnp.exp(-log_gain * (length - 1.0))
    head2 = head2 + e_right * end * later(m_left + d_left * added[:, LANES:])
    ahead = (sub16 - grp - 1).astype(F32)
    fade = jnp.exp(-log_gain * length * jnp.maximum(ahead, 0.0))
    own1 = jnp.sum(jnp.where(sub16 == grp, carry, 0.0), axis=0, keepdims=True)
    own2 = jnp.sum(jnp.where(sub16 > grp, fade * head2, 0.0), axis=0, keepdims=True)

    lane, sub = lane_of(), sub_of()
    turn[...] = jnp.zeros(turn.shape, F32)
    before = recv[pl.ds(pl.multiple_of(jnp.maximum(grp - 1, 0) * PACK + 16, 8), 8), :]
    before = jnp.where(grp > 0, before, 0.0)
    after = recv[pl.ds(pl.multiple_of(jnp.minimum(grp + 1, n_grp - 1) * PACK + 16, 8), 8), :]
    after = jnp.where(grp < n_grp - 1, after, 0.0)
    rim[...] = jnp.zeros(rim.shape, F32)
    for j in range(2):
        rim[j : j + 1, :] = before[2 + j : 3 + j, :]
        rim[2 + j : 3 + j, :] = after[j : j + 1, :]
        rim[8 + j : 9 + j, :] = before[j : j + 1, :]
        rim[10 + j : 11 + j, :] = after[2 + j : 3 + j, :]
        rim[16 + j : 17 + j, :] = edge[0, j : j + 1, :]
        rim[18 + j : 19 + j, :] = edge[1, 2 + j : 3 + j, :]
        rim[24 + j : 25 + j, :] = before[5:6, :]
        rim[26 + j : 27 + j, :] = after[4:5, :]
        rim[32 + j : 33 + j, :] = before[4:5, :]
        rim[34 + j : 35 + j, :] = after[5:6, :]
        rim[40 + j : 41 + j, :] = edge[0, 4:5, :]
        rim[42 + j : 43 + j, :] = edge[1, 5:6, :]

    def repeat(v):
        v = jnp.where(lane < 8, v, 0.0)
        for width in (8, 16, 32, 64):
            v = v + pltpu.roll(v, width, 1)
        return v

    def beside(v):
        inner = lane % 8
        up = jnp.where(inner < 7, pltpu.roll(v, 127, 1), pltpu.roll(v, 7, 1))
        return up + jnp.where(inner > 0, pltpu.roll(v, 1, 1), pltpu.roll(v, 121, 1))

    x1, x2, x0 = (rim[0:8, :], rim[8:16, :], rim[16:24, :])
    d1, d2, d0 = (repeat(rim[24:32, :]), repeat(rim[32:40, :]), repeat(rim[40:48, :]))
    m1 = d1 * x1
    inward = d0 * m1
    outer = x1 - 4.0 * m1 + beside(m1) + d2 * x2 + d0 * x0
    rim[0:8, :] = m1 - 4.0 * inward + beside(inward) + d1 * outer
    rim[8:16, :] = inward
    for j in range(2):
        cols = slice(j * 128, j * 128 + 128)
        turn[0:1, cols] = rim[j : j + 1, :]
        turn[1:2, cols] = rim[8 + j : 9 + j, :]
        turn[126:127, cols] = rim[10 + j : 11 + j, :]
        turn[127:128, cols] = rim[2 + j : 3 + j, :]
        for source, row in ((before, 126 + j), (after, j)):
            level = jnp.where(
                lane < 24, pltpu.roll(source, 16, 1), pltpu.roll(pltpu.roll(source, 7, 0), 24, 1)
            )[2 * j : 2 * j + 1, :]
            flux = source[4 + j : 5 + j, :]
            turn[row : row + 1, 256:384] = jnp.where(lane[0:1, :] < 16, flux, level)
    mend = turn[:, 0:256].T
    ends = turn[:, 256:384].T
    d_rows = blocks(de[0:8, :]) + [ends[0:8]]
    e_rows = blocks(de[8:16, :]) + [ends[8:16]]
    left_end, right_end = ((lane < 64) & (sub < 4), (lane >= 64) & (sub >= 4))
    for f in range(32):
        fix = mend[f * 8 : f * 8 + 8]
        at = f * 16
        twice[at : at + 8, :] = main[at : at + 8, :] + jnp.where(left_end, fix, 0.0)
        twice[at + 8 : at + 16, :] = main[at + 8 : at + 16, :] + jnp.where(
            right_end, pltpu.roll(fix, 4, 0), 0.0
        )

    f0 = [fields[b * 16 : b * 16 + 8, :] for b in range(4)] + [ends[16:24]]
    f1 = [fields[b * 16 + 8 : b * 16 + 16, :] for b in range(4)] + [ends[24:32]]
    bed = []
    for c in range(C):
        rate = jnp.broadcast_to(par(RATE + c), (8, LANES))
        loss = 1.0 / (1.0 + rate)
        gain = rate * loss
        mine = lane == c * 8 + sub
        into = jnp.sum(jnp.where(mine, own1, 0.0), axis=1, keepdims=True)
        up = blocks(gcol[c * 8 : c * 8 + 8, :])
        rows = [v + u * into for v, u in zip(blocks(solved[c * 8 : c * 8 + 8, :]), up)]
        source = e_rows[4] * (par(SRC + c) * f0[4] + par(SRC + 8 + c) * f1[4])
        last = loss * source + gain * rows[0][:, 0:1]
        second = loss * source + gain * pltpu.roll(last, 127, 1)
        beyond = into + (into - pltpu.roll(source, 1, 1)) / rate
        rim_rows = jnp.where(lane == 127, last, jnp.where(lane == 126, second, 0.0))
        rim_rows = jnp.where(lane == 0, into, jnp.where(lane == 1, beyond, rim_rows))
        bed.append(rows + [rim_rows])
    once = [stencil(rows, d_rows, 5) for rows in bed]
    once0, once1 = (stencil(f0, d_rows, 5), stencil(f1, d_rows, 5))
    for d in range(C):
        rate = jnp.broadcast_to(par(RATE + d), (8, LANES))
        loss = 1.0 / (1.0 + rate)
        gain = rate * loss
        moved = [par(MIXED + d) * once0[b] + par(MIXED + 8 + d) * once1[b] for b in range(5)]
        for c in range(C):
            part = par(PART + c * 8 + d)
            moved = [moved[b] + part * once[c][b] for b in range(5)]
        source = [loss * (bed[d][b] + e_rows[b] * moved[b]) for b in range(5)]
        rows = sweep(source[0:4], gain)
        mine = lane == d * 8 + sub
        into = jnp.sum(jnp.where(mine, own2, 0.0), axis=1, keepdims=True)
        up = blocks(gcol[d * 8 : d * 8 + 8, :])
        rows = [v + u * into for v, u in zip(rows, up)]
        last = source[4] + gain * rows[0][:, 0:1]
        rim_rows = jnp.where(lane == 127, last, jnp.where(lane == 0, into, 0.0))
        bed_out[d] = jnp.concatenate(rows, axis=1)[0:4, :]
        s = par(SETTLE + d)
        stirred = stencil(rows + [rim_rows], d_rows, 4)
        first = stencil(once[d], d_rows, 4)
        stirred, first = (fold(stirred), fold(first))
        keep, share, pass_on = ((1.0 - s) * (1.0 - s), 2.0 * s * (1.0 - s), s * s)
        w0, w1 = (par(W + d), par(W + 8 + d))
        for h in range(2):
            old, older = (None, None)
            for k in range(K):
                at = k * 16 + h * 8
                now = w0 * twice[at : at + 8, :] + w1 * twice[256 + at : 264 + at, :]
                if k == 0:
                    now = now + s * first[h]
                out = keep * now
                if k == 0:
                    out = out + ((1.0 - s) * s) * stirred[h]
                if k == 1:
                    out = out + pass_on * stirred[h]
                if old is not None:
                    out = out + share * old
                if older is not None:
                    out = out + pass_on * older
                store[d, k, h] = out
                old, older = (now, old)
        pltpu.make_async_copy(store.at[d], tracer.at[d], sems.at[d]).start()
    for d in range(C):
        pltpu.make_async_copy(store.at[d], tracer.at[d], sems.at[d]).wait()


VM = pl.BlockSpec(memory_space=pltpu.VMEM)
SM = pl.BlockSpec(memory_space=pltpu.SMEM)


def shape_of(*dims):
    return jax.ShapeDtypeStruct(dims, F32)


def local(
    obs_value, obs_tile, obs_cell, obs_type, obs_weights, diffusivity, erodibility,
    class_mixing, fall_table, fall_index, bedload_rate,
):
    n_wide, n_grp = (lax.axis_size("wide"), lax.axis_size("grp"))
    tile_x, tile_y = diffusivity.shape
    slots = obs_value.shape[0]
    grant = lambda size: pltpu.CompilerParams(vmem_limit_bytes=size << 20)
    line = lambda v: v.reshape(1, slots)
    mine = pl.pallas_call(
        pack_kernel,
        out_shape=shape_of(n_wide, 1, 4 * slots + 4 * tile_y),
        in_specs=[VM] * 6,
        out_specs=VM,
        compiler_params=grant(62),
    )(line(obs_value), line(obs_tile), line(obs_cell), line(obs_type), diffusivity, erodibility)
    obs = lax.all_to_all(mine, "wide", split_axis=0, concat_axis=0, tiled=True)

    tab, coef, table, chosen, blend, gcol, gdown = pl.pallas_call(
        setup_kernel,
        out_shape=(shape_of(PLACES, LANES), shape_of(16, LANES), shape_of(16, LANES), jax.ShapeDtypeStruct((256, LANES), BF16), shape_of(64, 256), shape_of(64, tile_y), shape_of(64, tile_y)),
        in_specs=[SM] * 5,
        out_specs=(VM,) * 7,
        scratch_shapes=[pltpu.SMEM((PLACES,), F32)],
        cost_estimate=pl.CostEstimate(flops=10_000_000, bytes_accessed=200_000, transcendentals=40_000),
        compiler_params=grant(4),
    )(obs_weights, class_mixing, fall_table, fall_index, bedload_rate)

    de, fields, solved, send, edge = pl.pallas_call(
        first_kernel,
        out_shape=(shape_of(16, tile_y), shape_of(64, LANES), shape_of(64, tile_y), shape_of(n_grp, PACK, LANES), shape_of(2, 8, LANES)),
        in_specs=[VM] * 7,
        out_specs=(VM, VM, VM, VM, VM),
        scratch_shapes=[pltpu.VMEM((128, 128), F32)],
        compiler_params=grant(16),
    )(tab, obs.reshape(-1, LANES), diffusivity, erodibility, coef, gcol, gdown)

    recv = lax.all_to_all(send, "grp", split_axis=0, concat_axis=0, tiled=True)
    main = pl.pallas_call(
        twice_kernel,
        out_shape=shape_of(512, LANES),
        in_specs=[VM, VM],
        out_specs=VM,
        scratch_shapes=[pltpu.VMEM((256, tile_y), F32)],
        cost_estimate=pl.CostEstimate(flops=10_000_000, bytes_accessed=800_000, transcendentals=0),
        compiler_params=grant(16),
    )(obs.reshape(-1, LANES), de)
    tracer, bed = pl.pallas_call(
        second_kernel,
        out_shape=(shape_of(C, K, 2, 8, LANES), shape_of(C, tile_x, tile_y)),
        in_specs=[VM] * 11,
        out_specs=(pl.BlockSpec(memory_space=pl.ANY), VM),
        scratch_shapes=[
            pltpu.VMEM((128, 384), F32),
            pltpu.VMEM((48, LANES), F32),
            pltpu.VMEM((512, LANES), F32),
            pltpu.VMEM((C, K, 2, 8, LANES), F32),
            pltpu.VMEM((n_grp, LANES), F32),
            pltpu.SemaphoreType.DMA((C,)),
        ],
        compiler_params=grant(8),
    )(tab, recv.reshape(n_grp * PACK, LANES), fields, de, solved, table, chosen, blend, gcol, main, edge)
    tracer = tracer.reshape(C, K, 2, 2, tile_x, LANES).transpose(0, 1, 4, 2, 3, 5)
    return (tracer.reshape(C, K, tile_x, tile_y), bed)


def solution(mesh):
    flat = P(("wide", "grp"))
    grid = P("wide", "grp")
    in_specs = (flat, flat, flat, flat, P(), grid, grid, P(), P(), P(), P())
    out_specs = (P(None, None, "wide", "grp"), P(None, "wide", "grp"))
    return jax.shard_map(local, mesh=mesh, in_specs=in_specs, out_specs=out_specs, check_vma=False)
```

```python
import jax
import jax.numpy as jnp
from jax import lax
from jax.experimental import pallas as pl
from jax.experimental.pallas import tpu as pltpu
from jax.sharding import PartitionSpec as P

F32 = jnp.float32
BF16 = jnp.bfloat16
C = 8
K = 16
LANES = 128
PACK = 24
W, MIX, SETTLE, RATE, SRC, MIXED, PART, PLACES = 0, 16, 80, 88, 96, 112, 128, 192


def lane_of(shape=(8, LANES)):
    return lax.broadcasted_iota(jnp.int32, shape, len(shape) - 1)


def sub_of(shape=(8, LANES)):
    return lax.broadcasted_iota(jnp.int32, shape, len(shape) - 2)


def decay(rate):
    u = 1.0 / (2.0 * rate + 1.0)
    q = u * u
    return 2.0 * u * (1.0 + q * (1.0 / 3 + q * (1.0 / 5 + q * (1.0 / 7 + q / 9))))


def blocks(value):
    return [value[:, i * LANES : (i + 1) * LANES] for i in range(value.shape[1] // LANES)]


def stencil(field, diff, count):
    lane = lane_of()
    ring = len(field)
    moment = [d * v for d, v in zip(diff, field)]
    after = [pltpu.roll(m, LANES - 1, 1) for m in moment]
    before = [pltpu.roll(m, 1, 1) for m in moment]
    out = []
    for b in range(count):
        sides = pltpu.roll(moment[b], 7, 0) + pltpu.roll(moment[b], 1, 0)
        right = 0.0 if ring == 4 and b == 3 else after[(b + 1) % ring]
        left = 0.0 if ring == 4 and b == 0 else before[(b - 1) % ring]
        sides = sides + jnp.where(lane == LANES - 1, right, after[b])
        sides = sides + jnp.where(lane == 0, left, before[b])
        out.append(field[b] - 4.0 * moment[b] + sides)
    return out


def sweep(rows, gain):
    lane = lane_of()
    zero = jnp.zeros((8, LANES), F32)
    power = gain
    for step in range(7):
        width = 1 << step
        turned = [pltpu.roll(v, LANES - width, 1) for v in rows] + [zero]
        near = lane < LANES - width
        rows = [
            rows[b] + power * jnp.where(near, turned[b], turned[b + 1]) for b in range(4)
        ]
        power = power * power
    rows = [rows[b] + power * rows[b + 1] if b < 3 else rows[b] for b in range(4)]
    power = power * power
    return [rows[b] + power * rows[b + 2] if b < 2 else rows[b] for b in range(4)]


def pack_kernel(value, tile, cell, kind, dif, ero, send):
    n_wide = send.shape[0]
    length = dif.shape[1]
    wide = lax.axis_index("wide")
    sort = kind[...]
    live = sort < 2
    row = [
        jnp.where(live, value[...], 0.0),
        (tile[...] * 4 + (lax.shift_right_logical(cell[...], 9) & 3)).astype(F32),
        (jnp.where(live, sort, 0) * K + lax.shift_right_logical(cell[...], 11)).astype(F32),
        (cell[...] & 511).astype(F32),
    ]
    row = jnp.concatenate(row, axis=1)
    first = jnp.concatenate([dif[0:1], dif[1:2], ero[0:1], ero[1:2]], axis=1)
    last = jnp.concatenate([dif[2:3], dif[3:4], ero[2:3], ero[3:4]], axis=1)
    for p in range(n_wide):
        send[p] = jnp.concatenate([row, first], axis=1)

    @pl.when(wide + 1 < n_wide)
    def _():
        send[wide + 1] = jnp.concatenate([row, last], axis=1)


def fold(rows):
    low = sub_of() < 4
    return [jnp.where(low, rows[b], pltpu.roll(rows[b + 1], 4, 0)) for b in (0, 2)]


def setup_kernel(weights, mixing, falls, index, rates, tab, coef_out, table, chosen, blend, gcol, gdown, par):
    for c in range(C):
        settle = falls[index[c]]
        par[SETTLE + c] = settle
        par[RATE + c] = rates[c]
        part = (1.0 - settle) * settle
        for t in range(2):
            par[W + t * 8 + c] = weights[t, c]
        for d in range(C):
            par[MIX + c * 8 + d] = mixing[c, d]
            par[PART + c * 8 + d] = part * mixing[c, d]
    for t in range(2):
        for d in range(C):
            source, mixed = (0.0, 0.0)
            for c in range(C):
                term = par[W + t * 8 + c] * par[MIX + c * 8 + d]
                source = source + term
                mixed = mixed + term * (1.0 - par[SETTLE + c])
            par[SRC + t * 8 + d] = source
            par[MIXED + t * 8 + d] = mixed
    for r in range(PLACES):
        tab[r : r + 1, :] = jnp.full((1, LANES), par[r], F32)
    length = gcol.shape[1]
    lane, sub = lane_of(), sub_of()
    group = (lane // 8) % 8
    rate = jnp.zeros((8, LANES), F32)
    rate_sub = jnp.zeros((8, LANES), F32)
    for c in range(C):
        rate = jnp.where(group == c, par[RATE + c], rate)
        rate_sub = jnp.where(sub == c, par[RATE + c], rate_sub)
    log_gain = decay(rate)
    coef = jnp.zeros((8, LANES), F32)
    for c in range(C):
        for d in range(C):
            coef = jnp.where((group == c) & (sub == d), par[PART + c * 8 + d], coef)
    table[0:8, :] = log_gain
    table[8:16, :] = 1.0 / (1.0 + rate)
    at = lax.broadcasted_iota(jnp.int32, (256, LANES), 0)
    kind = at // 64
    shift = jnp.where(kind == 1, 7, jnp.where(kind == 2, 1, 0))
    meets = ((at + shift) % 8 == lane_of((256, LANES)) % 8) & (kind < 3)
    chosen[...] = jnp.where(meets, 1.0, 0.0).astype(BF16)
    coef_out[0:8, :] = coef
    log_sub = decay(rate_sub)
    coef_out[8:16, :] = jnp.where(
        (group == sub) & (lane < 64),
        float(length) / (1.0 + rate_sub) * jnp.exp(-log_sub * length),
        0.0,
    )
    for c in range(C):
        rate_c = jnp.full((8, LANES), par[RATE + c], F32)
        log_c = decay(rate_c)
        row = jnp.zeros((8, LANES), F32)
        for d in range(C):
            row = jnp.where(lane // 8 == d, par[PART + c * 8 + d], row)
        row = jnp.where(lane % 8 == sub, row, 0.0)
        blend[c * 8 : c * 8 + 8, 0:LANES] = row * jnp.exp(-log_c)
        blend[c * 8 : c * 8 + 8, LANES:] = row * jnp.exp(-log_c * length)
        for b in range(length // LANES):
            cols = slice(b * LANES, b * LANES + LANES)
            at = (lane + b * LANES).astype(F32)
            gcol[c * 8 : c * 8 + 8, cols] = jnp.exp(-log_c * (length - at))
            gdown[c * 8 : c * 8 + 8, cols] = jnp.exp(-log_c * at) / (1.0 + rate_c)


def links(par, coef, gcol, gdown, de):
    length = de.shape[1]
    d_rows, e_rows = (de[0:8, :], de[8:16, :])
    at = lax.broadcasted_iota(jnp.int32, (8, length), 1)
    d_after = jnp.where(at == length - 1, 0.0, pltpu.roll(d_rows, length - 1, 1))
    d_before = jnp.where(at == 0, 0.0, pltpu.roll(d_rows, 1, 1))
    own = e_rows * (1.0 - 4.0 * d_rows)
    own_after, own_before = (e_rows * d_after, e_rows * d_before)
    above = d_rows * pltpu.roll(e_rows, 1, 0)
    below = d_rows * pltpu.roll(e_rows, 7, 0)
    parts = [[], [], []]
    wide = lambda v: jnp.concatenate([v] * (length // LANES), axis=1)
    for c in range(C):
        rate_c = jnp.broadcast_to(par(RATE + c), (8, LANES))
        gain_c = rate_c / (1.0 + rate_c)
        up = gcol[c * 8 : c * 8 + 8, :]
        mid = own + own_after * wide(1.0 + 1.0 / rate_c) + own_before * wide(gain_c)
        parts[0].append(mid * up)
        parts[1].append(above * up)
        parts[2].append(below * up)
    pad = jnp.zeros((64, length), F32)
    right = jnp.concatenate(parts[0] + parts[1] + parts[2] + [pad], axis=0)
    down = jnp.concatenate([gdown[d * 8 : d * 8 + 1, :] for d in range(C)], axis=0)
    dims = (((1,), (1,)), ((), ()))
    down_high, right_high = (down.astype(BF16), right.astype(BF16))
    down_low = (down - down_high.astype(F32)).astype(BF16)
    right_low = (right - right_high.astype(F32)).astype(BF16)
    dot = lambda a, b: lax.dot_general(a, b, dims, preferred_element_type=F32)
    pair = dot(jnp.concatenate([down_high, down_low], axis=0), right_high)
    both = pair[0:8] + pair[8:16] + dot(down_high, right_low)
    return (both[:, 0:LANES] * coef[0:8, :] + coef[8:16, :], both[:, LANES:] * coef[0:8, :])


def arrange(obs, length, wide):
    pieces = 4 + 4 * length // LANES
    n_src = obs.shape[0] // pieces
    value, xpos, layer, ypos = (obs[pl.ds(j, n_src, stride=pieces), :] for j in range(4))
    rel = xpos - (wide * 4).astype(F32)
    slot = jnp.where(rel < 0.0, rel + 8.0, rel)
    inside = (rel >= -2.0) & (rel <= 5.0)
    places = jnp.where(inside, layer * 8.0 + slot, -1.0)
    ground = jnp.where(inside & (layer == 0.0), slot, -1.0)
    ground = jnp.where(inside & (layer == float(K)), slot + 8.0, ground)
    high = value.astype(BF16).astype(F32)
    return n_src, high, value - high, places, ground, ypos, jnp.where(inside, slot, -99.0), layer


def spread(rows, n, count=256):
    return jnp.broadcast_to(rows[n : n + 1, :].astype(BF16), (count, LANES))


def numbers(count):
    return lax.broadcasted_iota(jnp.int32, (count, LANES), 0).astype(F32).astype(BF16)


def columns_of(ypos, n_src):
    ids, none = (numbers(256), jnp.zeros((256, LANES), BF16))
    front = jnp.where(ypos < 256.0, 1.0, 0.0)
    back = 1.0 - front
    column = ypos - 256.0 * back
    right = []
    for n in range(n_src):
        meet = ids == spread(column, n)
        near = jnp.where(meet, spread(front, n), none)
        far = jnp.where(meet, spread(back, n), none)
        right.append(jnp.concatenate([near, far], axis=0))
    return jnp.concatenate(right, axis=1)


def contract(left, right):
    dims = (((1,), (1,)), ((), ()))
    return lax.dot_general(left, right, dims, preferred_element_type=F32)


def first_kernel(
    tab, obs, dif, ero, coef, gcol, gdown, de, ground_out, solved, send, edge, turn
):
    length = dif.shape[1]
    pieces = 4 + 4 * length // LANES
    n_src = obs.shape[0] // pieces
    n_grp = send.shape[0]
    par = lambda r: tab[r : r + 1, :]
    wide, grp = (lax.axis_index("wide"), lax.axis_index("grp"))
    low_at, high_at = (jnp.maximum(wide - 1, 0), jnp.minimum(wide + 1, n_src - 1))
    has_low, has_high = (wide > 0, wide < n_src - 1)
    de[0:4, :] = dif[...]
    de[8:12, :] = ero[...]
    tiles = length // LANES
    for j in range(4):
        place = 8 * (j // 2) + j % 2
        for b in range(tiles):
            cols = slice(b * LANES, b * LANES + LANES)
            at = 4 + j * tiles + b
            above = obs[pl.ds(high_at * pieces + at, 1), :]
            below = obs[pl.ds(low_at * pieces + at, 1), :]
            de[place + 4 : place + 5, cols] = jnp.where(has_high, above, 0.0)
            de[place + 6 : place + 7, cols] = jnp.where(has_low, below, 0.0)
    n_src, high, low, _, ground, ypos, slot, layer = arrange(obs, length, wide)
    block = jnp.zeros(ypos.shape, F32)
    for edge_at in (128.0, 256.0, 384.0):
        block = block + jnp.where(ypos >= edge_at, 1.0, 0.0)
    lane_code = jnp.where(ground >= 0.0, block * 16.0 + ground, -1.0)
    along = ypos - 128.0 * block
    code = jnp.where(ypos < 2.0, ypos, jnp.where(ypos >= length - 2.0, ypos - (length - 4.0), -99.0))
    end_code = code * 8.0 + slot
    end_code = jnp.where((code >= 0.0) & (slot >= 0.0), end_code, -1.0)
    parts = [[] for _ in range(6)]
    value_or_none = lambda hit, rows, n: jnp.where(
        hit, spread(rows, n, hit.shape[0]), jnp.zeros(hit.shape, BF16)
    )
    one_or_none = lambda hit: jnp.where(
        hit, jnp.ones(hit.shape, BF16), jnp.zeros(hit.shape, BF16)
    )
    ids32, ids64, ids128 = (numbers(32), numbers(64), numbers(128))
    for n in range(n_src):
        hit = ids64 == spread(lane_code, n, 64)
        parts[0].append(value_or_none(hit, high, n))
        parts[1].append(value_or_none(hit, low, n))
        parts[2].append(one_or_none(ids128 == spread(along, n, 128)))
        hit = ids32 == spread(end_code, n, 32)
        parts[3].append(value_or_none(hit, high, n))
        parts[4].append(value_or_none(hit, low, n))
        parts[5].append(one_or_none(ids32 == spread(layer, n, 32)))
    parts = [jnp.concatenate(part, axis=1) for part in parts]
    level = contract(jnp.concatenate(parts[0:2], axis=0), parts[2])
    level = level[0:64] + level[64:128]
    ground_out[...] = level
    ends = contract(jnp.concatenate(parts[3:5], axis=0), parts[5])
    ends = ends[0:32] + ends[32:64]
    grow = lax.broadcasted_iota(jnp.int32, (32, 256), 1)
    here = lax.broadcasted_iota(jnp.int32, (32, 256), 0)
    spot = jnp.where(grow // 8 == here, 1.0, 0.0).astype(BF16)
    ends_high = ends.astype(BF16)
    ends_low = (ends - ends_high.astype(F32)).astype(BF16)
    grown = jnp.dot(ends_high, spot, preferred_element_type=F32)
    grown = grown + jnp.dot(ends_low, spot, preferred_element_type=F32)
    grown = jnp.where(grow % 8 == here % 8, grown, 0.0)
    rims = [jnp.sum(grown[q * 8 : q * 8 + 8], axis=0, keepdims=True) for q in range(4)]
    lane, sub = lane_of(), sub_of()
    d_rows, e_rows = (blocks(de[0:8, :]), blocks(de[8:16, :]))
    f0, f1 = ([level[t + b * 16 : t + b * 16 + 8] for b in range(4)] for t in (0, 8))
    bed = []
    for d in range(C):
        rate = jnp.broadcast_to(par(RATE + d), (8, LANES))
        loss = 1.0 / (1.0 + rate)
        rows = [
            loss * e_rows[b] * (par(SRC + d) * f0[b] + par(SRC + 8 + d) * f1[b])
            for b in range(4)
        ]
        rows = sweep(rows, rate * loss)
        solved[d * 8 : d * 8 + 8, :] = jnp.concatenate(rows, axis=1)
        bed.append(rows)
    for d in range(C):
        mixed = [par(MIXED + d) * f0[b] + par(MIXED + 8 + d) * f1[b] for b in range(4)]
        for c in range(C):
            part = par(PART + c * 8 + d)
            mixed = [mixed[b] + part * bed[c][b] for b in range(4)]
        moved = stencil(mixed, d_rows, 4)
        total = jnp.zeros((8, LANES), F32)
        for b in range(4):
            fall = gdown[d * 8 : d * 8 + 8, b * LANES : b * LANES + LANES]
            total = total + fall * (bed[d][b] + e_rows[b] * moved[b])
        tile = bed[d][0]
        tile = jnp.where(lane == 1, jnp.sum(total, axis=1, keepdims=True), tile)
        m_left, m_right = (d_rows[0] * mixed[0], d_rows[3] * mixed[3])
        for at, col in (
            (2, m_left[:, 0:1]),
            (3, m_right[:, 127:128]),
            (4, d_rows[0][:, 0:1]),
            (5, d_rows[3][:, 127:128]),
            (6, e_rows[0][:, 0:1]),
            (7, e_rows[3][:, 127:128]),
        ):
            tile = jnp.where(lane == at, col, tile)
        turn[d * 8 : d * 8 + 8, :] = tile
    turn[64:128, :] = jnp.zeros((64, LANES), F32)
    sums = turn[...].T[0:8, :]
    tile0, tile1 = links(par, coef, gcol, gdown, de)
    tile1 = jnp.where(lane < 64, tile1, pltpu.roll(sums, 64, 1))
    for side, cols, rows in ((0, slice(0, 128), (0, 1)), (1, slice(384, 512), (126, 127))):
        turn[0:16, :] = de[:, cols]
        flux = turn[...].T
        for j in range(2):
            r = rows[j]
            q = 2 * side + j
            edge[side, 2 * j : 2 * j + 1, :] = rims[q][:, 0:128]
            edge[side, 2 * j + 1 : 2 * j + 2, :] = rims[q][:, 128:256]
            edge[side, 4 + j : 5 + j, :] = flux[r : r + 1, :]
        edge[side, 6:8, :] = jnp.zeros((2, LANES), F32)
    for p in range(n_grp):
        send[p, 0:8, :] = tile0
        send[p, 8:16, :] = tile1
        send[p, 16:24, :] = jnp.where(grp + 1 == p, edge[1], edge[0])


def twice_kernel(obs, de, twice, fields):
    d_rows = blocks(de[0:8, :])
    wide = lax.axis_index("wide")
    n_src, high, low, places, _, ypos, _, _ = arrange(obs, de.shape[1], wide)
    ids, none = (numbers(256), jnp.zeros((256, LANES), BF16))
    first, second = ([], [])
    for n in range(n_src):
        hit = ids == spread(places, n)
        first.append(jnp.where(hit, spread(high, n), none))
        second.append(jnp.where(hit, spread(low, n), none))
    left = [jnp.concatenate(parts, axis=1) for parts in (first, second)]
    got = contract(jnp.concatenate(left, axis=0), columns_of(ypos, n_src))
    fields[...] = got[0:256] + got[256:512]

    def step(f, carry):
        field = blocks(fields[pl.ds(pl.multiple_of(f * 8, 8), 8), :])
        field = stencil(stencil(field, d_rows, 4), d_rows, 4)
        there = pl.ds(pl.multiple_of(f * 16, 16), 16)
        twice[there, :] = jnp.concatenate(fold(field), axis=0)
        return carry

    lax.fori_loop(0, fields.shape[0] // 8, step, 0, unroll=4)


def second_kernel(
    tab, recv, fields, de, solved, table, chosen, blend, gcol, main, edge, tracer, bed_out, turn, rim, twice, store, bed_store, carries, sems, bed_sems
):
    n_grp = recv.shape[0] // PACK
    par = lambda r: tab[r : r + 1, :]
    grp = lax.axis_index("grp")
    shape = (n_grp, LANES)
    lane16, sub16 = lane_of(shape), sub_of(shape)
    low16 = lane16 < 64
    group = lane16 // 8
    length = float(de.shape[1])
    log_gain = jnp.broadcast_to(table[0:1, :], shape)
    loss = jnp.broadcast_to(table[8:9, :], shape)

    def later(v):
        return jnp.where(sub16 < n_grp - 1, pltpu.roll(v, n_grp - 1, 0), 0.0)

    def earlier(v):
        return jnp.where(sub16 >= 1, pltpu.roll(v, 1, 0), 0.0)

    def per_device(j):
        return pltpu.roll(recv[pl.ds(8 + j, n_grp, stride=PACK), :], 64, 1)

    def split(v):
        high = v.astype(BF16)
        return high, (v - high.astype(F32)).astype(BF16)

    dot = lambda a, b: jnp.dot(a, b, preferred_element_type=F32)
    fade_all = jnp.exp(-table[0:1, :] * length)
    into = jnp.zeros((1, LANES), F32)
    carries[n_grp - 1 : n_grp, :] = into
    for e in range(n_grp - 2, -1, -1):
        into = recv[(e + 1) * PACK + 8 : (e + 1) * PACK + 9, :] + fade_all * into
        carries[e : e + 1, :] = into
    carry = carries[...]
    turned = pltpu.roll(carry, 64, 1)
    carry = jnp.where(low16, turned, carry)
    wide_part, tall_part = ([], [])
    for d in range(C):
        wide_part.append(recv[pl.ds(d, n_grp, stride=PACK), :] * carry)
        tall = jnp.where(low16, recv[pl.ds(8 + d, n_grp, stride=PACK), :], 0.0)
        tall_part.append(tall * carry)
    terms = jnp.concatenate(
        [jnp.concatenate(wide_part, axis=0), jnp.concatenate(tall_part, axis=0)], axis=1
    )
    terms_high, terms_low = split(terms)
    linked = dot(terms_high, chosen[...]) + dot(terms_low, chosen[...])
    carry_high, carry_low = split(carry[:, 0:64])
    blend_high, blend_low = split(blend[...])
    added = dot(carry_high, blend_high) + dot(carry_low, blend_high) + dot(carry_high, blend_low)
    head2, m_left, m_right, d_left, d_right, e_left, e_right = (
        per_device(j) for j in range(1, 8)
    )
    picked = [
        jnp.where(group == d, linked[d * n_grp : (d + 1) * n_grp], 0.0) for d in range(C)
    ]
    while len(picked) > 1:
        picked = [a + b for a, b in zip(picked[0::2], picked[1::2])]
    head2 = head2 + picked[0]
    head2 = head2 + e_left * loss * earlier(m_right + d_right * added[:, 0:LANES])
    end = loss * jnp.exp(-log_gain * (length - 1.0))
    head2 = head2 + e_right * end * later(m_left + d_left * added[:, LANES:])
    ahead = (sub16 - grp - 1).astype(F32)
    fade = jnp.exp(-log_gain * length * jnp.maximum(ahead, 0.0))
    own1 = jnp.sum(jnp.where(sub16 == grp, carry, 0.0), axis=0, keepdims=True)
    own2 = jnp.sum(jnp.where(sub16 > grp, fade * head2, 0.0), axis=0, keepdims=True)

    lane, sub = lane_of(), sub_of()
    turn[...] = jnp.zeros(turn.shape, F32)
    before = recv[pl.ds(pl.multiple_of(jnp.maximum(grp - 1, 0) * PACK + 16, 8), 8), :]
    before = jnp.where(grp > 0, before, 0.0)
    after = recv[pl.ds(pl.multiple_of(jnp.minimum(grp + 1, n_grp - 1) * PACK + 16, 8), 8), :]
    after = jnp.where(grp < n_grp - 1, after, 0.0)
    rim[...] = jnp.zeros(rim.shape, F32)
    for j in range(2):
        rim[j : j + 1, :] = before[2 + j : 3 + j, :]
        rim[2 + j : 3 + j, :] = after[j : j + 1, :]
        rim[8 + j : 9 + j, :] = before[j : j + 1, :]
        rim[10 + j : 11 + j, :] = after[2 + j : 3 + j, :]
        rim[16 + j : 17 + j, :] = edge[0, j : j + 1, :]
        rim[18 + j : 19 + j, :] = edge[1, 2 + j : 3 + j, :]
        rim[24 + j : 25 + j, :] = before[5:6, :]
        rim[26 + j : 27 + j, :] = after[4:5, :]
        rim[32 + j : 33 + j, :] = before[4:5, :]
        rim[34 + j : 35 + j, :] = after[5:6, :]
        rim[40 + j : 41 + j, :] = edge[0, 4:5, :]
        rim[42 + j : 43 + j, :] = edge[1, 5:6, :]

    def repeat(v):
        v = jnp.where(lane < 8, v, 0.0)
        for width in (8, 16, 32, 64):
            v = v + pltpu.roll(v, width, 1)
        return v

    def beside(v):
        inner = lane % 8
        up = jnp.where(inner < 7, pltpu.roll(v, 127, 1), pltpu.roll(v, 7, 1))
        return up + jnp.where(inner > 0, pltpu.roll(v, 1, 1), pltpu.roll(v, 121, 1))

    x1, x2, x0 = (rim[0:8, :], rim[8:16, :], rim[16:24, :])
    d1, d2, d0 = (repeat(rim[24:32, :]), repeat(rim[32:40, :]), repeat(rim[40:48, :]))
    m1 = d1 * x1
    inward = d0 * m1
    outer = x1 - 4.0 * m1 + beside(m1) + d2 * x2 + d0 * x0
    rim[0:8, :] = m1 - 4.0 * inward + beside(inward) + d1 * outer
    rim[8:16, :] = inward
    for j in range(2):
        cols = slice(j * 128, j * 128 + 128)
        turn[0:1, cols] = rim[j : j + 1, :]
        turn[1:2, cols] = rim[8 + j : 9 + j, :]
        turn[126:127, cols] = rim[10 + j : 11 + j, :]
        turn[127:128, cols] = rim[2 + j : 3 + j, :]
        for source, row in ((before, 126 + j), (after, j)):
            level = jnp.where(
                lane < 24, pltpu.roll(source, 16, 1), pltpu.roll(pltpu.roll(source, 7, 0), 24, 1)
            )[2 * j : 2 * j + 1, :]
            flux = source[4 + j : 5 + j, :]
            turn[row : row + 1, 256:384] = jnp.where(lane[0:1, :] < 16, flux, level)
    mend = turn[:, 0:256].T
    ends = turn[:, 256:384].T
    d_rows = blocks(de[0:8, :]) + [ends[0:8]]
    e_rows = blocks(de[8:16, :]) + [ends[8:16]]
    left_end, right_end = ((lane < 64) & (sub < 4), (lane >= 64) & (sub >= 4))
    for f in range(32):
        fix = mend[f * 8 : f * 8 + 8]
        at = f * 16
        twice[at : at + 8, :] = main[at : at + 8, :] + jnp.where(left_end, fix, 0.0)
        twice[at + 8 : at + 16, :] = main[at + 8 : at + 16, :] + jnp.where(
            right_end, pltpu.roll(fix, 4, 0), 0.0
        )

    f0 = [fields[b * 16 : b * 16 + 8, :] for b in range(4)] + [ends[16:24]]
    f1 = [fields[b * 16 + 8 : b * 16 + 16, :] for b in range(4)] + [ends[24:32]]
    bed = []
    for c in range(C):
        rate = jnp.broadcast_to(par(RATE + c), (8, LANES))
        loss = 1.0 / (1.0 + rate)
        gain = rate * loss
        mine = lane == c * 8 + sub
        into = jnp.sum(jnp.where(mine, own1, 0.0), axis=1, keepdims=True)
        up = blocks(gcol[c * 8 : c * 8 + 8, :])
        rows = [v + u * into for v, u in zip(blocks(solved[c * 8 : c * 8 + 8, :]), up)]
        source = e_rows[4] * (par(SRC + c) * f0[4] + par(SRC + 8 + c) * f1[4])
        last = loss * source + gain * rows[0][:, 0:1]
        second = loss * source + gain * pltpu.roll(last, 127, 1)
        beyond = into + (into - pltpu.roll(source, 1, 1)) / rate
        rim_rows = jnp.where(lane == 127, last, jnp.where(lane == 126, second, 0.0))
        rim_rows = jnp.where(lane == 0, into, jnp.where(lane == 1, beyond, rim_rows))
        bed.append(rows + [rim_rows])
    once = [stencil(rows, d_rows, 5) for rows in bed]
    once0, once1 = (stencil(f0, d_rows, 5), stencil(f1, d_rows, 5))
    for d in range(C):
        rate = jnp.broadcast_to(par(RATE + d), (8, LANES))
        loss = 1.0 / (1.0 + rate)
        gain = rate * loss
        moved = [par(MIXED + d) * once0[b] + par(MIXED + 8 + d) * once1[b] for b in range(5)]
        for c in range(C):
            part = par(PART + c * 8 + d)
            moved = [moved[b] + part * once[c][b] for b in range(5)]
        source = [loss * (bed[d][b] + e_rows[b] * moved[b]) for b in range(5)]
        rows = sweep(source[0:4], gain)
        mine = lane == d * 8 + sub
        into = jnp.sum(jnp.where(mine, own2, 0.0), axis=1, keepdims=True)
        up = blocks(gcol[d * 8 : d * 8 + 8, :])
        rows = [v + u * into for v, u in zip(rows, up)]
        last = source[4] + gain * rows[0][:, 0:1]
        rim_rows = jnp.where(lane == 127, last, jnp.where(lane == 0, into, 0.0))
        bed_store[d] = jnp.concatenate(rows, axis=1)[0:4, :]
        pltpu.make_async_copy(bed_store.at[d], bed_out.at[d], bed_sems.at[d]).start()
        s = par(SETTLE + d)
        stirred = stencil(rows + [rim_rows], d_rows, 4)
        first = stencil(once[d], d_rows, 4)
        stirred, first = (fold(stirred), fold(first))
        keep, share, pass_on = ((1.0 - s) * (1.0 - s), 2.0 * s * (1.0 - s), s * s)
        w0, w1 = (par(W + d), par(W + 8 + d))
        for h in range(2):
            old, older = (None, None)
            for k in range(K):
                at = k * 16 + h * 8
                now = w0 * twice[at : at + 8, :] + w1 * twice[256 + at : 264 + at, :]
                if k == 0:
                    now = now + s * first[h]
                out = keep * now
                if k == 0:
                    out = out + ((1.0 - s) * s) * stirred[h]
                if k == 1:
                    out = out + pass_on * stirred[h]
                if old is not None:
                    out = out + share * old
                if older is not None:
                    out = out + pass_on * older
                store[d, k, h] = out
                old, older = (now, old)
        pltpu.make_async_copy(store.at[d], tracer.at[d], sems.at[d]).start()
    for d in range(C):
        pltpu.make_async_copy(store.at[d], tracer.at[d], sems.at[d]).wait()
        pltpu.make_async_copy(bed_store.at[d], bed_out.at[d], bed_sems.at[d]).wait()


VM = pl.BlockSpec(memory_space=pltpu.VMEM)
SM = pl.BlockSpec(memory_space=pltpu.SMEM)


def shape_of(*dims):
    return jax.ShapeDtypeStruct(dims, F32)


def local(
    obs_value, obs_tile, obs_cell, obs_type, obs_weights, diffusivity, erodibility,
    class_mixing, fall_table, fall_index, bedload_rate,
):
    n_wide, n_grp = (lax.axis_size("wide"), lax.axis_size("grp"))
    tile_x, tile_y = diffusivity.shape
    slots = obs_value.shape[0]
    grant = lambda size: pltpu.CompilerParams(vmem_limit_bytes=size << 20)
    line = lambda v: v.reshape(1, slots)
    mine = pl.pallas_call(
        pack_kernel,
        out_shape=shape_of(n_wide, 1, 4 * slots + 4 * tile_y),
        in_specs=[VM] * 6,
        out_specs=VM,
        compiler_params=grant(62),
    )(line(obs_value), line(obs_tile), line(obs_cell), line(obs_type), diffusivity, erodibility)
    obs = lax.all_to_all(mine, "wide", split_axis=0, concat_axis=0, tiled=True)

    tab, coef, table, chosen, blend, gcol, gdown = pl.pallas_call(
        setup_kernel,
        out_shape=(shape_of(PLACES, LANES), shape_of(16, LANES), shape_of(16, LANES), jax.ShapeDtypeStruct((256, LANES), BF16), shape_of(64, 256), shape_of(64, tile_y), shape_of(64, tile_y)),
        in_specs=[SM] * 5,
        out_specs=(VM,) * 7,
        scratch_shapes=[pltpu.SMEM((PLACES,), F32)],
        cost_estimate=pl.CostEstimate(flops=10_000_000, bytes_accessed=200_000, transcendentals=40_000),
        compiler_params=grant(4),
    )(obs_weights, class_mixing, fall_table, fall_index, bedload_rate)

    de, fields, solved, send, edge = pl.pallas_call(
        first_kernel,
        out_shape=(shape_of(16, tile_y), shape_of(64, LANES), shape_of(64, tile_y), shape_of(n_grp, PACK, LANES), shape_of(2, 8, LANES)),
        in_specs=[VM] * 7,
        out_specs=(VM, VM, VM, VM, VM),
        scratch_shapes=[pltpu.VMEM((128, 128), F32)],
        compiler_params=grant(16),
    )(tab, obs.reshape(-1, LANES), diffusivity, erodibility, coef, gcol, gdown)

    recv = lax.all_to_all(send, "grp", split_axis=0, concat_axis=0, tiled=True)
    main = pl.pallas_call(
        twice_kernel,
        out_shape=shape_of(512, LANES),
        in_specs=[VM, VM],
        out_specs=VM,
        scratch_shapes=[pltpu.VMEM((256, tile_y), F32)],
        cost_estimate=pl.CostEstimate(flops=10_000_000, bytes_accessed=800_000, transcendentals=0),
        compiler_params=grant(16),
    )(obs.reshape(-1, LANES), de)
    tracer, bed = pl.pallas_call(
        second_kernel,
        out_shape=(shape_of(C, K, 2, 8, LANES), shape_of(C, tile_x, tile_y)),
        in_specs=[VM] * 11,
        out_specs=(pl.BlockSpec(memory_space=pl.ANY),) * 2,
        scratch_shapes=[
            pltpu.VMEM((128, 384), F32),
            pltpu.VMEM((48, LANES), F32),
            pltpu.VMEM((512, LANES), F32),
            pltpu.VMEM((C, K, 2, 8, LANES), F32),
            pltpu.VMEM((C, tile_x, tile_y), F32),
            pltpu.VMEM((n_grp, LANES), F32),
            pltpu.SemaphoreType.DMA((C,)),
            pltpu.SemaphoreType.DMA((C,)),
        ],
        compiler_params=grant(8),
    )(tab, recv.reshape(n_grp * PACK, LANES), fields, de, solved, table, chosen, blend, gcol, main, edge)
    tracer = tracer.reshape(C, K, 2, 2, tile_x, LANES).transpose(0, 1, 4, 2, 3, 5)
    return (tracer.reshape(C, K, tile_x, tile_y), bed)


def solution(mesh):
    flat = P(("wide", "grp"))
    grid = P("wide", "grp")
    in_specs = (flat, flat, flat, flat, P(), grid, grid, P(), P(), P(), P())
    out_specs = (P(None, None, "wide", "grp"), P(None, "wide", "grp"))
    return jax.shard_map(local, mesh=mesh, in_specs=in_specs, out_specs=out_specs, check_vma=False)
```
